256 devices in a mesh: gx: 4 (over x), gy: 8 (over z), gz: 8 (over y, core).
Axes of the slice: x: 4, y: 4, z: 8, core: 2. Of those that a mesh axis runs over, the one named last changes fastest.
Arguments:
- conduct: float32 [3, 128, 128, 512], P(None, 'gz', 'gy', 'gx'), may hold values from 0.5 to 2
- cross: float32 [3, 128, 128, 512], P(None, 'gz', 'gy', 'gx'), may hold values from -0.25 to 0.25
- tissue: int32 [128, 128, 512], P('gz', 'gy', 'gx'), may hold values 0 or 1
- src_z: int32 [2048], replicated, may hold values from 0 to 127
- src_y: int32 [2048], replicated, may hold values from 0 to 127
- src_x: int32 [2048], replicated, may hold values from 0 to 511
Outputs:
- solution: float32 [128, 128, 512], P('gz', 'gy', 'gx')
The draws below stay inside these ranges and needn't reach their ends.
All inputs are finite; a program needn't handle non-finite values. No bound on the sum of `tissue` on one device may be relied on, other than what follows from the above.
Results may differ from the reference program's by a relative error of at most 0.0001.
Values sent between devices are 32-bit elements; how exact they have to be, the bound alone decides.
A program may use at most 128 MiB of HBM per device.

```python
import math
import jax
import jax.numpy as jnp
from jax import lax

LEVELS = 4
NU = 2
COARSE = 12
NX = 512
NY = 128
NZ = 128
SOURCES = 2048


def touch_ends(result, stream_key, smallest, top_value):
    shape = result.shape
    place = [jax.random.randint(jax.random.fold_in(stream_key, axis), (), 0, shape[axis]) for axis in range(len(shape))]
    result = result.at[tuple(place)].set(smallest)
    longest = shape.index(max(shape))
    place[longest] = (place[longest] + 1) % shape[longest]
    return result.at[tuple(place)].set(top_value)


def shard_levels(rng, shape, cuts, smallest, high):
    loudness = 1.0
    for axis_at, blocks in cuts:
        draws = jax.random.uniform(jax.random.fold_in(jax.random.fold_in(rng, 6), axis_at), (blocks,), jnp.float32, smallest / len(cuts), high / len(cuts))
        loudness = loudness * jnp.repeat(jnp.exp(draws), shape[axis_at] // blocks).reshape((-1,) + (1,) * (len(shape) - 1 - axis_at))
    return loudness


def setup_inputs(seed: int = 0) -> dict:
    key_list = jax.random.split(jax.random.key(seed), 7)
    conduct = jnp.clip(jnp.exp(math.log(2.0) - 1.3862944 * jax.random.uniform(key_list[0], (3, NZ, NY, NX), jnp.float32) ** shard_levels(key_list[0], (3, NZ, NY, NX), ((1, 8), (2, 8), (3, 4)), -0.2, 0.2)), 0.5, 2.0)
    cross = jnp.clip(jax.random.uniform(key_list[1], (3, NZ, NY, NX), jnp.float32, -0.25, 0.25) * shard_levels(key_list[1], (3, NZ, NY, NX), ((1, 8), (2, 8), (3, 4)), -0.4, 0.0), -0.25, 0.25)
    tissue = touch_ends((jax.random.randint(key_list[2], (NZ, NY, NX), 0, 5) < 4).astype(jnp.int32), jax.random.fold_in(key_list[2], 1), 0, 1)
    src_z = touch_ends(jax.random.randint(key_list[3], (SOURCES,), 0, NZ), jax.random.fold_in(key_list[3], 1), 0, NZ - 1).astype(jnp.int32)
    src_y = touch_ends(jax.random.randint(key_list[4], (SOURCES,), 0, NY), jax.random.fold_in(key_list[4], 1), 0, NY - 1).astype(jnp.int32)
    src_x = touch_ends(jax.random.randint(key_list[5], (SOURCES,), 0, NX), jax.random.fold_in(key_list[5], 1), 0, NX - 1).astype(jnp.int32)
    return dict(conduct=conduct, cross=cross, tissue=tissue, src_z=src_z, src_y=src_y, src_x=src_x)


tau_step = 4000.0
relax_weight = 0.55
stim_height = 64000.0
pair_list = ((0, 1), (0, 2), (1, 2))


def offset_for(dimension, sign):
    return tuple(sign if number == dimension else 0 for number in range(3))


def joined(lead_off, other_off):
    return tuple(lead_off[number] + other_off[number] for number in range(3))


def window(padded, offset, extent):
    begin = tuple(1 + offset[number] for number in range(3))
    finish = tuple(begin[number] + extent[number] for number in range(3))
    return lax.slice(padded, begin, finish)


def laplace_part(tensor_pad, field_pad, extent):
    middle = (0, 0, 0)
    center = window(field_pad, middle, extent)
    accumulated = jnp.zeros(extent, jnp.float32)
    for dimension in range(3):
        step_up = offset_for(dimension, 1)
        step_down = offset_for(dimension, -1)
        conduct_mid = window(tensor_pad[dimension], middle, extent)
        w_plus = 0.5 * (conduct_mid + window(tensor_pad[dimension], step_up, extent))
        w_minus = 0.5 * (conduct_mid + window(tensor_pad[dimension], step_down, extent))
        accumulated = accumulated + w_plus * (window(field_pad, step_up, extent) - center) - w_minus * (center - window(field_pad, step_down, extent))
    for number, dims_pair in enumerate(pair_list):
        lead_dim, other_dim = dims_pair
        mixed = tensor_pad[3 + number]
        lead_up = offset_for(lead_dim, 1)
        lead_down = offset_for(lead_dim, -1)
        other_up = offset_for(other_dim, 1)
        other_down = offset_for(other_dim, -1)
        up_up = window(field_pad, joined(lead_up, other_up), extent)
        up_down = window(field_pad, joined(lead_up, other_down), extent)
        down_up = window(field_pad, joined(lead_down, other_up), extent)
        down_down = window(field_pad, joined(lead_down, other_down), extent)
        cross_term = window(mixed, lead_up, extent) * (up_up - up_down) - window(mixed, lead_down, extent) * (down_up - down_down)
        cross_term = cross_term + window(mixed, other_up, extent) * (up_up - down_up) - window(mixed, other_down, extent) * (up_down - down_down)
        accumulated = accumulated + 0.25 * cross_term
    return accumulated


def diagonal_of(tensor_pad, tau_level, extent):
    middle = (0, 0, 0)
    accumulated = jnp.zeros(extent, jnp.float32)
    for dimension in range(3):
        conduct_mid = window(tensor_pad[dimension], middle, extent)
        w_plus = 0.5 * (conduct_mid + window(tensor_pad[dimension], offset_for(dimension, 1), extent))
        w_minus = 0.5 * (conduct_mid + window(tensor_pad[dimension], offset_for(dimension, -1), extent))
        accumulated = accumulated + (w_plus + w_minus)
    return 1.0 + tau_level * accumulated


def apply_operator(tensor_pad, field_pad, tau_level, extent):
    return window(field_pad, (0, 0, 0), extent) - tau_level * laplace_part(tensor_pad, field_pad, extent)


def pad_grid(values):
    return jnp.pad(values, 1)


def pad_tensor(tensor):
    return jnp.pad(tensor, ((0, 0), (1, 1), (1, 1), (1, 1)))


def relax_once(tensor_pad, diagonal, tau_level, forcing, values, padder):
    applied = apply_operator(tensor_pad, padder(values), tau_level, values.shape)
    return values + relax_weight * (forcing - applied) / diagonal


def coarsen(tensor):
    comps, size_z, size_y, size_x = tensor.shape
    return tensor.reshape(comps, size_z // 2, 2, size_y // 2, 2, size_x // 2, 2).mean(axis=(2, 4, 6))


def restrict(values):
    size_z, size_y, size_x = values.shape
    return values.reshape(size_z // 2, 2, size_y // 2, 2, size_x // 2, 2).mean(axis=(1, 3, 5))


def prolong(values):
    size_z, size_y, size_x = values.shape
    spread = jnp.broadcast_to(values[:, None, :, None, :, None], (size_z, 2, size_y, 2, size_x, 2))
    return spread.reshape(2 * size_z, 2 * size_y, 2 * size_x)


def reference(conduct, cross, tissue, src_z, src_y, src_x):
    weight = tissue.astype(jnp.float32)[None]
    tensor = jnp.concatenate([conduct * weight, cross * weight], axis=0)
    flat_index = ((src_z * NY + src_y) * NX + src_x).astype(jnp.int32)
    forcing = jnp.zeros((NZ * NY * NX,), jnp.float32).at[flat_index].add(stim_height).reshape(NZ, NY, NX)
    tensor_pads = []
    diagonals = []
    for grid_level in range(LEVELS + 1):
        if grid_level > 0:
            tensor = coarsen(tensor)
        tensor_pad = pad_tensor(tensor)
        tensor_pads.append(tensor_pad)
        diagonals.append(diagonal_of(tensor_pad, tau_step / 4.0 ** grid_level, tensor.shape[1:]))
    fields = []
    forcings = []
    for grid_level in range(LEVELS):
        tau_level = tau_step / 4.0 ** grid_level
        values = relax_weight * forcing / diagonals[grid_level]
        for repeat in range(NU - 1):
            values = relax_once(tensor_pads[grid_level], diagonals[grid_level], tau_level, forcing, values, pad_grid)
        residual = forcing - apply_operator(tensor_pads[grid_level], pad_grid(values), tau_level, values.shape)
        fields.append(values)
        forcings.append(forcing)
        forcing = restrict(residual)
    tau_level = tau_step / 4.0 ** LEVELS
    values = relax_weight * forcing / diagonals[LEVELS]
    for repeat in range(COARSE - 1):
        values = relax_once(tensor_pads[LEVELS], diagonals[LEVELS], tau_level, forcing, values, pad_grid)
    for grid_level in reversed(range(LEVELS)):
        tau_level = tau_step / 4.0 ** grid_level
        values = fields[grid_level] + prolong(values)
        for repeat in range(NU):
            values = relax_once(tensor_pads[grid_level], diagonals[grid_level], tau_level, forcings[grid_level], values, pad_grid)
    return values
```

```python
import functools

import jax
import jax.numpy as jnp
from jax import lax
from jax.experimental import pallas as pl
from jax.experimental.pallas import tpu as pltpu
from jax.sharding import PartitionSpec as P

tau_step = 4000.0
relax = 0.55
stim_height = 64000.0
COARSE = 12
RO = 8
LANES = 128
MESH = pl.DeviceIdType.MESH
F32 = jnp.float32
PAIRS = ((0, 1, 3), (0, 2, 4), (1, 2, 5))


class Level:
    def __init__(self, index, nz, ny, nx, split):
        self.index, self.nz, self.ny, self.nx, self.split = index, nz, ny, nx, split
        self.rows = max(8, -(-ny // 8) * 8)
        self.zrows = max(8, -(-nz // 8) * 8)
        self.stride = RO + self.rows + 8
        self.tau = tau_step / 4.0**index
        self.right = nx % LANES


def lanes_of(shape):
    return lax.broadcasted_iota(jnp.int32, shape, len(shape) - 1)


def rows_of(shape):
    return lax.broadcasted_iota(jnp.int32, shape, len(shape) - 2)


def roll(value, shift, axis=None):
    axis = value.ndim - 1 if axis is None else axis
    if isinstance(shift, int):
        shift = shift % value.shape[axis]
        if shift == 0:
            return value
    return pltpu.roll(value, shift, axis)


def dot(a, b):
    return lax.dot_general(
        a, b, (((1,), (0,)), ((), ())), precision=lax.Precision.HIGHEST, preferred_element_type=F32
    )


MESSAGES = [("z", 1, (0, 0, -1)), ("z", 0, (0, 0, 1))]
for _face, _oy in ((0, -1), (1, 1)):
    for _part, _oz in ((0, 0), (1, -1), (2, 1)):
        MESSAGES.append(("y", 3 * _face + _part, (0, _oy, _oz)))
for _side, _ox in ((0, -1), (1, 1)):
    for _part, (_oy, _oz) in enumerate(((0, 0), (-1, 0), (1, 0), (0, -1), (0, 1))):
        MESSAGES.append(("p", 5 * _side + _part, (_ox, _oy, _oz)))
FACES = [("z", 1, (0, 0, -1)), ("z", 0, (0, 0, 1)), ("y", 0, (0, -1, 0)), ("y", 1, (0, 1, 0)), ("p", 0, (-1, 0, 0)), ("p", 1, (1, 0, 0))]


def kernel(names, levels, sizes, sources, *refs):
    R = dict(zip(names, refs))
    GX, GY, GZ = sizes
    gx, gy, gz = lax.axis_index("gx"), lax.axis_index("gy"), lax.axis_index("gz")

    def device(ox, oy, oz):
        return (lax.rem(gx + (ox + GX), GX), lax.rem(gy + (oy + GY), GY), lax.rem(gz + (oz + GZ), GZ))

    peers = [offset for _, _, offset in MESSAGES]
    peers += [(k, 0, 0) for k in range(1, GX)] + [(0, k, 0) for k in range(1, GY)] + [(0, 0, k) for k in range(1, GZ)]
    seen, unique = set(), []
    for ox, oy, oz in peers:
        key = (ox % GX, oy % GY, oz % GZ)
        if key not in seen:
            seen.add(key)
            unique.append(key)
    barrier = pltpu.get_barrier_semaphore()
    for ox, oy, oz in unique:
        pl.semaphore_signal(barrier, inc=1, device_id=device(ox, oy, oz), device_id_type=MESH)

    def flag(condition):
        return jnp.where(condition, 0.0, 1.0).astype(F32)

    in_xp, in_xm = flag(gx == GX - 1), flag(gx == 0)
    in_yp, in_ym = flag(gy == GY - 1), flag(gy == 0)
    in_zp, in_zm = flag(gz == GZ - 1), flag(gz == 0)

    def clean(level, value):
        return value if level.ny == level.rows else jnp.where(rows_of(value.shape) < level.ny, value, 0.0)

    def bounds(level):
        if level.split:
            return in_zp, in_zm, in_yp, in_ym, in_xp, in_xm
        return (jnp.zeros((), F32),) * 6

    def pack_x(level, get):
        shape = (level.rows, LANES)
        lane = lanes_of(shape)
        out = jnp.zeros(shape, F32)
        for z in range(level.nz):
            value = get(z)
            first = (level.right + 2 * (z + 1)) % LANES
            last = (2 * (z + 1) + LANES - 1) % LANES
            a = roll(value, first)
            b = roll(value, last - (level.nx - 1))
            out = jnp.where(lane == first, a, jnp.where(lane == last, b, out))
        return out

    def coarsen_rows(level, lower, get, count):
        stage = R["stage"]
        half = level.ny // 2
        for i in range(count):
            for z in range(level.nz // 2):
                total = None
                for dz in range(2):
                    for dy in range(2):
                        piece = get(i, 2 * z + dz, pl.ds(RO + dy, half, stride=2))
                        total = piece if total is None else total + piece
                stage[pl.ds((i * (level.nz // 2) + z) * lower.rows, half), :] = total

    def coarsen_lanes(level, rows):
        a, b = rows_of((LANES, LANES)), lanes_of((LANES, LANES))
        matrix = jnp.where((b == a // 2) & (b < level.nx // 2), 0.125, 0.0).astype(F32)
        return dot(R["stage"][pl.ds(0, rows), :], matrix)

    def coefficients(level):
        l = level.index
        K, C, D = R[f"K{l}"], R[f"C{l}"], R[f"D{l}"]
        n, rows = level.nz, level.rows
        shape = (rows, LANES)
        lane, row = lanes_of(shape), rows_of(shape)
        zp, zm, yp, ym, xp, xm = bounds(level)
        keep_yp = jnp.where(row == level.ny - 1, yp, 1.0)
        keep_ym = jnp.where(row == 0, ym, 1.0)
        keep_xp = jnp.where(lane == level.nx - 1, xp, 1.0)
        keep_xm = jnp.where(lane == 0, xm, 1.0)

        def step(z, carry):
            ze = z + 1

            def at(comp, dz=0, dy=0):
                return K[comp, ze + dz, pl.ds(RO + dy, rows), :]

            def along(comp, which, sign):
                value = at(comp)
                if level.split:
                    halo = R[f"KH{l}"][which, z]
                    value = jnp.where(lane == (level.right if sign > 0 else LANES - 1), halo, value)
                return roll(value, LANES - 1 if sign > 0 else 1)

            keep_zp = jnp.where(z == n - 1, zp, 1.0)
            keep_zm = jnp.where(z == 0, zm, 1.0)
            keep = ((keep_zp, keep_zm), (keep_yp, keep_ym), (keep_xp, keep_xm))
            weights = (
                (0.5 * (at(0) + at(0, 1)), 0.5 * (at(0) + at(0, -1))),
                (0.5 * (at(1) + at(1, 0, 1)), 0.5 * (at(1) + at(1, 0, -1))),
                (0.5 * (at(2) + along(2, 0, 1)), 0.5 * (at(2) + along(2, 0, -1))),
            )
            total = weights[0][0] + weights[0][1] + weights[1][0] + weights[1][1] + weights[2][0] + weights[2][1]
            diagonal = 1.0 + level.tau * total
            inverse = relax / diagonal
            scale = level.tau * inverse
            D[0, z] = inverse
            D[1, z] = diagonal * (1.0 / relax)
            for a in range(3):
                for s in range(2):
                    C[2 * a + s, z] = scale * weights[a][s] * keep[a][s]
            quarter = 0.25 * scale

            def shifted(comp, axis, sign):
                if axis == 0:
                    return at(comp, sign)
                if axis == 1:
                    return at(comp, 0, sign)
                return along(comp, 1 if comp == 4 else 2, sign)

            for number, (a, b, comp) in enumerate(PAIRS):
                ka = [shifted(comp, a, 1), shifted(comp, a, -1)]
                kb = [shifted(comp, b, 1), shifted(comp, b, -1)]
                for sa in range(2):
                    for sb in range(2):
                        value = quarter * (ka[sa] + kb[sb]) * keep[a][sa] * keep[b][sb]
                        C[6 + 4 * number + 2 * sa + sb, z] = value if sa == sb else -value
            return carry

        lax.fori_loop(0, n, step, 0)

    def sweep(level, source, emit, halo=True):
        l = level.index
        V, C, G, XP, XM = R[f"V{l}"], R[f"C{l}"], R[f"G{l}"], R[f"XP{l}"], R[f"XM{l}"]
        rows = level.rows

        def shift(ze, carry):
            value = V[source, ze]
            up = down = value
            if halo:
                lane = lanes_of(value.shape)
                edge = R[f"H{l}"][source, ze]
                up = jnp.where(lane == level.right, edge, value)
                down = jnp.where(lane == LANES - 1, edge, value)
            XP[ze] = roll(up, LANES - 1)
            XM[ze] = roll(down, 1)
            return carry

        lax.fori_loop(0, level.nz + 2, shift, 0)

        def step(z, carry):
            ze = z + 1

            def at(dz, dy, dx):
                where_rows = pl.ds(RO + dy, rows)
                if dx == 0:
                    return V[source, ze + dz, where_rows, :]
                return (XP if dx > 0 else XM)[ze + dz, where_rows, :]

            center = at(0, 0, 0)
            parts = [G[z] - relax * center, None, None]
            offsets = [(1, 0, 0), (-1, 0, 0), (0, 1, 0), (0, -1, 0), (0, 0, 1), (0, 0, -1)]
            for a, b, _ in PAIRS:
                for sa in (1, -1):
                    for sb in (1, -1):
                        offset = [0, 0, 0]
                        offset[a], offset[b] = sa, sb
                        offsets.append(tuple(offset))
            for number, offset in enumerate(offsets):
                term = C[number, z] * at(*offset)
                slot = number % 3
                parts[slot] = term if parts[slot] is None else parts[slot] + term
            emit(z, center, (parts[0] + parts[1]) + parts[2])
            return carry

        lax.fori_loop(0, level.nz, step, 0)

    def into(level, slot):
        V = R[f"V{level.index}"]

        def emit(z, value, delta):
            V[slot, z + 1, pl.ds(RO, level.rows), :] = value + delta

        return emit

    pending = []
    count = [0]

    def drain():
        for copy in pending:
            copy.wait_send()
        pending.clear()

    def exchange(level, slot, step, during=None):
        l = level.index
        V, H, YB, PB, X = R[f"V{l}"], R[f"H{l}"], R[f"YB{l}"], R[f"PB{l}"], R["PX"]
        ZB = R[f"ZB{l}"]
        RZ, RY, RP = R[f"RZ{l}"], R[f"RY{l}"], R[f"RP{l}"]
        nz, ny, rows, zrows = level.nz, level.ny, level.rows, level.zrows
        drain()
        for z in range(nz):
            YB[0, pl.ds(z, 1), :] = V[slot, z + 1, pl.ds(RO, 1), :]
            YB[1, pl.ds(z, 1), :] = V[slot, z + 1, pl.ds(RO + ny - 1, 1), :]
        ZB[0] = V[slot, 1, pl.ds(RO, rows), :]
        ZB[1] = V[slot, nz, pl.ds(RO, rows), :]
        PB[...] = pack_x(level, lambda z: V[slot, z + 1, pl.ds(RO, rows), :])
        parity = count[0] % 2
        count[0] += 1
        copies = []
        ylow, zlow = rows - 8, zrows - 8
        for number, (kind, where, (ox, oy, oz)) in enumerate(MESSAGES):
            if kind == "z":
                src, dst = ZB.at[0 if where else 1], RZ.at[step, where]
            elif kind == "y":
                face = where // 3
                if where % 3 == 0:
                    src, dst = YB.at[face], RY.at[step, where]
                else:
                    low = 0 if where % 3 == 1 else zlow
                    src, dst = YB.at[face, pl.ds(low, 8)], RY.at[step, where, pl.ds(0, 8)]
            else:
                part = where % 5
                if part in (1, 2):
                    low = 0 if part == 1 else ylow
                    src, dst = PB.at[pl.ds(low, 8)], RP.at[step, where, pl.ds(0, 8)]
                else:
                    src, dst = PB, RP.at[step, where]
            copy = pltpu.make_async_remote_copy(
                src_ref=src, dst_ref=dst, send_sem=R["send"].at[number], recv_sem=R["recv"].at[parity, number],
                device_id=device(ox, oy, oz), device_id_type=MESH,
            )
            copy.start()
            copies.append(copy)
        pending.extend(copies)
        if during is not None:
            during()
        for copy in copies:
            copy.wait_recv()
        V[slot, nz + 1, pl.ds(RO, rows), :] = RZ[step, 1]
        V[slot, 0, pl.ds(RO, rows), :] = RZ[step, 0]
        for face in range(2):
            place = RO + ny if face == 0 else RO - 1
            for z in range(nz):
                V[slot, z + 1, pl.ds(place, 1), :] = RY[step, 3 * face, pl.ds(z, 1), :]
            V[slot, nz + 1, pl.ds(place, 1), :] = RY[step, 3 * face + 1, pl.ds(0, 1), :]
            V[slot, 0, pl.ds(place, 1), :] = RY[step, 3 * face + 2, pl.ds(nz - 1 - zlow, 1), :]

        def merged(part, size):
            even = lanes_of((size, LANES)) % 2 == 0
            return jnp.where(even, RP[step, part, pl.ds(0, size), :], RP[step, 5 + part, pl.ds(0, size), :])

        lane = lanes_of((rows, LANES))
        middle = merged(0, rows)
        above = roll(merged(3, rows), 2 * nz)
        below = roll(merged(4, rows), -2 * nz)

        def slab_lanes(ze):
            return (lane == (level.right + 2 * ze) % LANES) | (lane == (2 * ze + LANES - 1) % LANES)

        middle = jnp.where(slab_lanes(nz + 1), above, jnp.where(slab_lanes(0), below, middle))
        size = level.stride
        X[pl.ds(RO, rows), :] = middle
        X[pl.ds(RO + ny, 1), :] = merged(1, 8)[0:1]
        X[pl.ds(RO - 1, 1), :] = merged(2, 8)[ny - 1 - ylow : ny - ylow]
        whole = X[pl.ds(0, size), :]
        for ze in range(nz + 2):
            H[slot, ze] = roll(whole, -2 * ze)

    def start_faces(level):
        l = level.index
        K, KY, KP, KZ = R[f"K{l}"], R[f"KY{l}"], R[f"KP{l}"], R[f"KZ{l}"]
        nz, ny, rows = level.nz, level.ny, level.rows
        for i, comp in enumerate((0, 3, 4)):
            KZ[0, i] = K[comp, 1, pl.ds(RO, rows), :]
            KZ[1, i] = K[comp, nz, pl.ds(RO, rows), :]
        for i, comp in enumerate((1, 3, 5)):
            for z in range(nz):
                KY[0, i, pl.ds(z, 1), :] = K[comp, z + 1, pl.ds(RO, 1), :]
                KY[1, i, pl.ds(z, 1), :] = K[comp, z + 1, pl.ds(RO + ny - 1, 1), :]
        for i, comp in enumerate((2, 4, 5)):
            KP[i] = pack_x(level, lambda z: K[comp, z + 1, pl.ds(RO, rows), :])
        copies = []
        for number, (kind, where, (ox, oy, oz)) in enumerate(FACES):
            if kind == "z":
                src, dst = KZ.at[0 if where else 1], R[f"RKZ{l}"].at[where]
            elif kind == "y":
                src, dst = KY.at[where], R[f"RKY{l}"].at[where]
            else:
                src, dst = KP, R[f"RKP{l}"].at[where]
            copy = pltpu.make_async_remote_copy(
                src_ref=src, dst_ref=dst, send_sem=R["ksend"].at[l, number], recv_sem=R["krecv"].at[l, number],
                device_id=device(ox, oy, oz), device_id_type=MESH,
            )
            copy.start()
            copies.append(copy)
        return copies

    def finish_faces(level, copies):
        l = level.index
        K, KH = R[f"K{l}"], R[f"KH{l}"]
        nz, ny, rows = level.nz, level.ny, level.rows
        for copy in copies:
            copy.wait()
        for i, comp in enumerate((0, 3, 4)):
            K[comp, nz + 1, pl.ds(RO, rows), :] = R[f"RKZ{l}"][1, i] * in_zp
            K[comp, 0, pl.ds(RO, rows), :] = R[f"RKZ{l}"][0, i] * in_zm
        for i, comp in enumerate((1, 3, 5)):
            for z in range(nz):
                K[comp, z + 1, pl.ds(RO + ny, 1), :] = R[f"RKY{l}"][0, i, pl.ds(z, 1), :] * in_yp
                K[comp, z + 1, pl.ds(RO - 1, 1), :] = R[f"RKY{l}"][1, i, pl.ds(z, 1), :] * in_ym
        even = lanes_of((rows, LANES)) % 2 == 0
        for i in range(3):
            both = jnp.where(even, R[f"RKP{l}"][0, i] * in_xp, R[f"RKP{l}"][1, i] * in_xm)
            for z in range(nz):
                KH[i, z] = roll(both, -2 * (z + 1))

    class Gather:
        def __init__(self, tag, comps):
            self.tag, self.comps = tag, comps
            self.copies = []

        def send(self, phase, src, dst_of, targets):
            self.copies = []
            for number, offset in enumerate(targets):
                copy = pltpu.make_async_remote_copy(
                    src_ref=src, dst_ref=dst_of(number), send_sem=R[f"gs{self.tag}"].at[phase, number],
                    recv_sem=R[f"gr{self.tag}"].at[phase, number], device_id=device(*offset), device_id_type=MESH,
                )
                copy.start()
                self.copies.append(copy)

        def wait(self):
            for copy in self.copies:
                copy.wait()

        def phase_x(self, tiles):
            own, received = R[f"GX{self.tag}"], R[f"RX{self.tag}"]
            own[...] = tiles
            self.send(0, own, lambda number: received.at[number], [(k, 0, 0) for k in range(1, GX)])

        def phase_y(self):
            self.wait()
            slots = R[f"RY{self.tag}"]
            total = R[f"GX{self.tag}"][...]
            for k in range(GX - 1):
                total = total + R[f"RX{self.tag}"][k]
            slots[gy] = total
            self.send(1, slots.at[gy], lambda number: slots.at[gy], [(0, k, 0) for k in range(1, GY)])

        def phase_z(self):
            self.wait()
            slots, out = R[f"RY{self.tag}"], R[f"RZ{self.tag}"]
            for i in range(self.comps):
                for y in range(GY):
                    out[gz, i, pl.ds(2 * y, 2), :] = slots[y, pl.ds(2 * i, 2), :]
            self.send(2, out.at[gz], lambda number: out.at[gz], [(0, 0, k) for k in range(1, GZ)])

        def finish(self, store):
            self.wait()
            out = R[f"RZ{self.tag}"]
            for i in range(self.comps):
                for z in range(GZ):
                    value = out[z, i]
                    left = lanes_of(value.shape) < 64
                    store(i, 2 * z, jnp.where(left, value, 0.0))
                    store(i, 2 * z + 1, jnp.where(left, roll(value, 64), 0.0))

    def own_tile(values, comps, total_rows):
        T = R["tile"]
        T[...] = jnp.zeros(T.shape, F32)
        for i in range(comps):
            low = values[(2 * i) * 8 : (2 * i) * 8 + 8]
            high = values[(2 * i + 1) * 8 : (2 * i + 1) * 8 + 8]
            T[pl.ds(2 * i, 2), :] = (low + roll(high, 64))[0:2]
        return roll(T[pl.ds(0, total_rows), :], 16 * gx)

    L0, L1, L2, L3, L4 = levels
    for level in (L3, L4):
        for name in ("K", "V"):
            ref = R[f"{name}{level.index}"]
            for i in range(ref.shape[0]):
                ref[i] = jnp.zeros(ref.shape[1:], F32)

    def fill(z, carry):
        weight = R["tissue"][z].astype(F32)
        for comp in range(3):
            R["K0"][comp, z + 1, pl.ds(RO, L0.rows), :] = R["conduct"][comp, z] * weight
            R["K0"][3 + comp, z + 1, pl.ds(RO, L0.rows), :] = R["cross"][comp, z] * weight
        return carry

    lax.fori_loop(0, L0.nz, fill, 0)
    pl.semaphore_wait(barrier, len(unique))
    faces0 = start_faces(L0)

    def coarser_tensor(level, lower):
        coarsen_rows(level, lower, lambda i, z, rows: R[f"K{level.index}"][i, z + 1, rows, :], 6)
        height = (level.nz // 2) * lower.rows
        values = coarsen_lanes(level, 6 * height)
        if lower.split:
            for i in range(6):
                for z in range(lower.nz):
                    start = i * height + z * lower.rows
                    R[f"K{lower.index}"][i, z + 1, pl.ds(RO, lower.rows), :] = values[start : start + lower.rows]
        return values

    R["stage"][...] = jnp.zeros(R["stage"].shape, F32)
    coarser_tensor(L0, L1)
    faces1 = start_faces(L1)
    coarser_tensor(L1, L2)
    faces2 = start_faces(L2)
    block3 = Level(3, 2, 2, 16, False)
    gather_k = Gather("k", 6)
    gather_k.phase_x(own_tile(coarser_tensor(L2, block3), 6, 16))

    zl = R["src_z"][...] - gz * L0.nz
    yl = R["src_y"][...] - gy * L0.ny
    xl = R["src_x"][...] - gx * L0.nx
    inside = (zl >= 0) & (zl < L0.nz) & (yl >= 0) & (yl < L0.ny)
    R["key"][0:1, :] = jnp.where(inside, zl * L0.ny + yl, -1)
    R["key"][1:2, :] = xl
    R["counts"][...] = jnp.zeros(R["counts"].shape, F32)
    chunk = 256

    def scatter(i, carry):
        start = pl.multiple_of(i * chunk, chunk)
        key = R["key"][0:1, pl.ds(start, chunk)]
        key_x = R["key"][1:2, pl.ds(start, chunk)]
        left = jnp.where(rows_of((L0.nz * L0.ny, chunk)) == key, 1.0, 0.0).astype(jnp.bfloat16)
        right = jnp.where(rows_of((LANES, chunk)) == key_x, 1.0, 0.0).astype(jnp.bfloat16)
        R["counts"][...] += lax.dot_general(left, right, (((1,), (1,)), ((), ())), preferred_element_type=F32)
        return carry

    lax.fori_loop(0, sources // chunk, scatter, 0)

    finish_faces(L0, faces0)
    coefficients(L0)

    def load0(z):
        return stim_height * R["counts"][pl.ds(pl.multiple_of(z * L0.ny, 8), L0.rows), :]

    def first_sweep(level, load):
        l = level.index

        def step(z, carry):
            value = load(z) * R[f"D{l}"][0, z]
            R[f"G{l}"][z] = value
            R[f"V{l}"][0, z + 1, pl.ds(RO, level.rows), :] = value
            return carry

        lax.fori_loop(0, level.nz, step, 0)

    def residual(level, slot, halo=True):
        l = level.index
        store = R[f"XR{l}"]

        def emit(z, value, delta):
            store[z, pl.ds(RO, level.rows), :] = delta * R[f"D{l}"][1, z]

        sweep(level, slot, emit, halo)

    def restricted(level, lower):
        coarsen_rows(level, lower, lambda i, z, rows: R[f"XR{level.index}"][z, rows, :], 1)
        return coarsen_lanes(level, (level.nz // 2) * lower.rows)

    def during_01():
        gather_k.phase_y()
        finish_faces(L1, faces1)
        coefficients(L1)

    def during_02():
        gather_k.phase_z()
        finish_faces(L2, faces2)
        coefficients(L2)

    def coarse_setup():
        def store(i, z, value):
            R["K3"][i, z + 1, pl.ds(RO, L3.rows), :] = clean(L3, value)

        gather_k.finish(store)
        coefficients(L3)
        coarsen_rows(L3, L4, lambda i, z, rows: R["K3"][i, z + 1, rows, :], 6)
        height = L4.nz * L4.rows
        values = coarsen_lanes(L3, 6 * height)
        for i in range(6):
            for z in range(L4.nz):
                start = i * height + z * L4.rows
                R["K4"][i, z + 1, pl.ds(RO, L4.rows), :] = clean(L4, values[start : start + L4.rows])
        coefficients(L4)

    during = {(0, 0): during_01, (0, 1): during_02, (2, 0): coarse_setup}

    first_sweep(L0, load0)
    for level, lower in ((L0, L1), (L1, L2), (L2, block3)):
        l = level.index
        exchange(level, 0, 0, during.get((l, 0)))
        sweep(level, 0, into(level, 1))
        exchange(level, 1, 1, during.get((l, 1)))
        residual(level, 1)
        values = restricted(level, lower)
        if lower.split:
            R["load"][pl.ds(0, lower.nz * lower.rows), :] = values
            first_sweep(lower, lambda z: R["load"][pl.ds(pl.multiple_of(z * lower.rows, 8), lower.rows), :])

    gather_f = Gather("f", 1)
    gather_f.phase_x(own_tile(values, 1, 8))
    gather_f.phase_y()
    gather_f.phase_z()

    def store_load(i, z, value):
        R["load"][pl.ds(z * L3.rows, L3.rows), :] = value

    gather_f.finish(store_load)

    def load_of(level):
        return lambda z: clean(level, R["load"][pl.ds(pl.multiple_of(z * level.rows, 8), level.rows), :])

    first_sweep(L3, load_of(L3))
    sweep(L3, 0, into(L3, 1), False)
    residual(L3, 1, False)
    values = restricted(L3, L4)
    R["load"][pl.ds(0, L4.nz * L4.rows), :] = values
    first_sweep(L4, load_of(L4))
    for i in range(COARSE - 1):
        sweep(L4, i % 2, into(L4, (i + 1) % 2), False)
    last4 = (COARSE - 1) % 2

    def spread(level, nz_c, ny_c, nx_c, stride_c, get, base, halo):
        l = level.index
        M, PV = R["merge"], R["spread"]
        a, b = rows_of((LANES, LANES)), lanes_of((LANES, LANES))
        main = (a == b // 2) & (b < level.nx)
        edges = ((a == nx_c) & (b == level.right)) | ((a == LANES - 1) & (b == LANES - 1))
        wide = halo and level.nx == LANES
        if halo and not wide:
            main = main | edges
        height = (nz_c + 2) * stride_c
        stacked = jnp.concatenate([get(ze) for ze in range(nz_c + 2)], axis=0)
        M[0, pl.ds(0, height), :] = dot(stacked, jnp.where(main, 1.0, 0.0).astype(F32))
        if wide:
            M[1, pl.ds(0, height), :] = dot(stacked, jnp.where(edges, 1.0, 0.0).astype(F32))
        V = R[f"V{l}"]
        for layer in range(2 if wide else 1):
            for ze in range(nz_c + 2):
                value = M[layer, pl.ds(ze * stride_c + RO - 1, ny_c + 2), :]
                slabs = [zf for zf in (2 * ze - 1, 2 * ze) if 0 <= zf <= level.nz + 1]
                for phase in range(2):
                    PV[layer, ze, pl.ds(RO - 2 + phase, ny_c + 2, stride=2), :] = value
        for ze in range(nz_c + 2):
            for zf in (2 * ze - 1, 2 * ze):
                if 0 <= zf <= level.nz + 1:
                    size = level.stride
                    V[2, zf] = V[1, zf] + PV[0, ze, pl.ds(0, size), :]
                    if halo:
                        H = R[f"H{l}"]
                        H[2, zf] = H[1, zf] + PV[1 if wide else 0, ze, pl.ds(0, size), :]

    def coarse_slab(level, slot):
        V = R[f"V{level.index}"]

        def get(ze):
            value = V[slot, ze]
            if level.split:
                lane = lanes_of(value.shape)
                edge = (lane == level.right) | (lane == LANES - 1)
                value = jnp.where(edge, R[f"H{level.index}"][slot, ze], value)
            return value

        return get

    spread(L3, L4.nz, L4.ny, L4.nx, L4.stride, coarse_slab(L4, last4), 0, False)
    sweep(L3, 2, into(L3, 0), False)
    sweep(L3, 0, into(L3, 1), False)

    def own_slab(ze):
        value = R["V3"][1, 2 * gz + ze]
        value = roll(value, L3.stride - 2 * gy, axis=0)
        value = roll(value, LANES - 16 * gx)
        return value[0:24]

    spread(L2, 2, 2, 16, 24, own_slab, 0, True)
    for level in (L2, L1):
        sweep(level, 2, into(level, 3))
        exchange(level, 3, 2)
        sweep(level, 3, into(level, 0))
        exchange(level, 0, 3)
        finer = levels[level.index - 1]
        spread(finer, level.nz, level.ny, level.nx, level.stride, coarse_slab(level, 0), 0, True)
    sweep(L0, 2, into(L0, 3))
    exchange(L0, 3, 2)

    def emit_out(z, value, delta):
        R["out"][z] = value + delta

    sweep(L0, 3, emit_out)
    drain()


def solution(mesh):
    sizes = (mesh.shape["gx"], mesh.shape["gy"], mesh.shape["gz"])
    GX, GY, GZ = sizes

    def body(conduct, cross, tissue, src_z, src_y, src_x):
        nz, ny, nx = tissue.shape
        sources = src_z.shape[0]
        levels = [Level(l, nz >> l, ny >> l, nx >> l, True) for l in range(3)]
        levels.append(Level(3, 2 * GZ, 2 * GY, 16 * GX, False))
        levels.append(Level(4, GZ, GY, 8 * GX, False))
        scratch = {}

        def vmem(name, *shape, dtype=F32):
            scratch[name] = pltpu.VMEM(shape, dtype)

        for level in levels:
            l, z, rows, stride, zrows = level.index, level.nz, level.rows, level.stride, level.zrows
            slots = 4 if level.split else 3
            vmem(f"K{l}", 6, z + 2, stride, LANES)
            vmem(f"C{l}", 18, z, rows, LANES)
            vmem(f"D{l}", 2, z, rows, LANES)
            vmem(f"G{l}", z, rows, LANES)
            vmem(f"V{l}", slots, z + 2, stride, LANES)
            vmem(f"XP{l}", z + 2, stride, LANES)
            vmem(f"XM{l}", z + 2, stride, LANES)
            vmem(f"XR{l}", z, stride, LANES)
            if level.split:
                vmem(f"H{l}", slots, z + 2, stride, LANES)
                vmem(f"KH{l}", 3, z, rows, LANES)
                vmem(f"YB{l}", 2, zrows, LANES)
                vmem(f"PB{l}", rows, LANES)
                vmem(f"ZB{l}", 2, rows, LANES)
                vmem(f"RZ{l}", 4, 2, rows, LANES)
                vmem(f"RY{l}", 4, 6, zrows, LANES)
                vmem(f"RP{l}", 4, 10, rows, LANES)
                vmem(f"KZ{l}", 2, 3, rows, LANES)
                vmem(f"KY{l}", 2, 3, zrows, LANES)
                vmem(f"KP{l}", 3, rows, LANES)
                vmem(f"RKZ{l}", 2, 3, rows, LANES)
                vmem(f"RKY{l}", 2, 3, zrows, LANES)
                vmem(f"RKP{l}", 2, 3, rows, LANES)
        vmem("PX", levels[0].stride, LANES)
        vmem("stage", 6 * 8 * 8, LANES)
        vmem("tile", 16, LANES)
        vmem("key", 2, sources, dtype=jnp.int32)
        vmem("counts", nz * ny, LANES)
        vmem("load", max(levels[3].nz * levels[3].rows, 64), LANES)
        vmem("merge", 2, 10 * 32, LANES)
        vmem("spread", 2, 10, 48, LANES)
        for tag, comps, height in (("k", 6, 16), ("f", 1, 8)):
            vmem(f"GX{tag}", height, LANES)
            vmem(f"RX{tag}", GX - 1, height, LANES)
            vmem(f"RY{tag}", GY, height, LANES)
            vmem(f"RZ{tag}", GZ, comps, levels[3].rows, LANES)
            most = max(sizes) - 1
            scratch[f"gs{tag}"] = pltpu.SemaphoreType.DMA((3, most))
            scratch[f"gr{tag}"] = pltpu.SemaphoreType.DMA((3, most))
        scratch["send"] = pltpu.SemaphoreType.DMA((len(MESSAGES),))
        scratch["recv"] = pltpu.SemaphoreType.DMA((2, len(MESSAGES)))
        scratch["ksend"] = pltpu.SemaphoreType.DMA((3, len(FACES)))
        scratch["krecv"] = pltpu.SemaphoreType.DMA((3, len(FACES)))
        names = ["conduct", "cross", "tissue", "src_z", "src_y", "src_x", "out"] + list(scratch)
        row = lambda value: value.reshape(1, sources)
        return pl.pallas_call(
            functools.partial(kernel, names, levels, sizes, sources),
            out_shape=jax.ShapeDtypeStruct((nz, ny, nx), F32),
            in_specs=[pl.BlockSpec(memory_space=pltpu.VMEM)] * 6,
            out_specs=pl.BlockSpec(memory_space=pltpu.VMEM),
            scratch_shapes=list(scratch.values()),
            compiler_params=pltpu.CompilerParams(
                collective_id=0, has_side_effects=True, vmem_limit_bytes=60 * 1024 * 1024
            ),
        )(conduct, cross, tissue, row(src_z), row(src_y), row(src_x))

    placed = (P(None, "gz", "gy", "gx"), P(None, "gz", "gy", "gx"), P("gz", "gy", "gx"), P(), P(), P())
    return jax.shard_map(body, mesh=mesh, in_specs=placed, out_specs=P("gz", "gy", "gx"), check_vma=False)
```

```python
import functools

import jax
import jax.numpy as jnp
from jax import lax
from jax.experimental import pallas as pl
from jax.experimental.pallas import tpu as pltpu
from jax.sharding import PartitionSpec as P

tau_step = 4000.0
relax = 0.55
stim_height = 64000.0
COARSE = 12
RO = 8
LANES = 128
MESH = pl.DeviceIdType.MESH
F32 = jnp.float32
PAIRS = ((0, 1, 3), (0, 2, 4), (1, 2, 5))


class Level:
    def __init__(self, index, nz, ny, nx, split):
        self.index, self.nz, self.ny, self.nx, self.split = index, nz, ny, nx, split
        self.rows = max(8, -(-ny // 8) * 8)
        self.zrows = max(8, -(-nz // 8) * 8)
        self.stride = RO + self.rows + 8
        self.tau = tau_step / 4.0**index
        self.right = nx % LANES


def lanes_of(shape):
    return lax.broadcasted_iota(jnp.int32, shape, len(shape) - 1)


def rows_of(shape):
    return lax.broadcasted_iota(jnp.int32, shape, len(shape) - 2)


def roll(value, shift, axis=None):
    axis = value.ndim - 1 if axis is None else axis
    if isinstance(shift, int):
        shift = shift % value.shape[axis]
        if shift == 0:
            return value
    return pltpu.roll(value, shift, axis)


def dot(a, b):
    return lax.dot_general(
        a, b, (((1,), (0,)), ((), ())), precision=lax.Precision.HIGHEST, preferred_element_type=F32
    )


MESSAGES = [("z", 1, (0, 0, -1)), ("z", 0, (0, 0, 1))]
for _face, _oy in ((0, -1), (1, 1)):
    for _part, _oz in ((0, 0), (1, -1), (2, 1)):
        MESSAGES.append(("y", 3 * _face + _part, (0, _oy, _oz)))
for _side, _ox in ((0, -1), (1, 1)):
    for _part, (_oy, _oz) in enumerate(((0, 0), (-1, 0), (1, 0), (0, -1), (0, 1))):
        MESSAGES.append(("p", 5 * _side + _part, (_ox, _oy, _oz)))
FACES = [("z", 1, (0, 0, -1)), ("z", 0, (0, 0, 1)), ("y", 0, (0, -1, 0)), ("y", 1, (0, 1, 0)), ("p", 0, (-1, 0, 0)), ("p", 1, (1, 0, 0))]


def kernel(names, levels, sizes, sources, *refs):
    R = dict(zip(names, refs))
    GX, GY, GZ = sizes
    gx, gy, gz = lax.axis_index("gx"), lax.axis_index("gy"), lax.axis_index("gz")

    def device(ox, oy, oz):
        return (lax.rem(gx + (ox + GX), GX), lax.rem(gy + (oy + GY), GY), lax.rem(gz + (oz + GZ), GZ))

    peers = [offset for _, _, offset in MESSAGES]
    peers += [(k, 0, 0) for k in range(1, GX)] + [(0, k, 0) for k in range(1, GY)] + [(0, 0, k) for k in range(1, GZ)]
    seen, unique = set(), []
    for ox, oy, oz in peers:
        key = (ox % GX, oy % GY, oz % GZ)
        if key not in seen:
            seen.add(key)
            unique.append(key)
    barrier = pltpu.get_barrier_semaphore()
    for ox, oy, oz in unique:
        pl.semaphore_signal(barrier, inc=1, device_id=device(ox, oy, oz), device_id_type=MESH)

    def flag(condition):
        return jnp.where(condition, 0.0, 1.0).astype(F32)

    in_xp, in_xm = flag(gx == GX - 1), flag(gx == 0)
    in_yp, in_ym = flag(gy == GY - 1), flag(gy == 0)
    in_zp, in_zm = flag(gz == GZ - 1), flag(gz == 0)

    def clean(level, value):
        return value if level.ny == level.rows else jnp.where(rows_of(value.shape) < level.ny, value, 0.0)

    def bounds(level):
        if level.split:
            return in_zp, in_zm, in_yp, in_ym, in_xp, in_xm
        return (jnp.zeros((), F32),) * 6

    def pack_x(level, get):
        shape = (level.rows, LANES)
        lane = lanes_of(shape)
        out = jnp.zeros(shape, F32)
        for z in range(level.nz):
            value = get(z)
            first = (level.right + 2 * (z + 1)) % LANES
            last = (2 * (z + 1) + LANES - 1) % LANES
            a = roll(value, first)
            b = roll(value, last - (level.nx - 1))
            out = jnp.where(lane == first, a, jnp.where(lane == last, b, out))
        return out

    def coarsen_rows(level, lower, get, count):
        stage = R["stage"]
        half = level.ny // 2
        for i in range(count):
            for z in range(level.nz // 2):
                total = None
                for dz in range(2):
                    for dy in range(2):
                        piece = get(i, 2 * z + dz, pl.ds(RO + dy, half, stride=2))
                        total = piece if total is None else total + piece
                stage[pl.ds((i * (level.nz // 2) + z) * lower.rows, half), :] = total

    def coarsen_lanes(level, rows):
        a, b = rows_of((LANES, LANES)), lanes_of((LANES, LANES))
        matrix = jnp.where((b == a // 2) & (b < level.nx // 2), 0.125, 0.0).astype(F32)
        return dot(R["stage"][pl.ds(0, rows), :], matrix)

    def coefficients(level):
        l = level.index
        K, C, D = R[f"K{l}"], R[f"C{l}"], R[f"D{l}"]
        n, rows = level.nz, level.rows
        shape = (rows, LANES)
        lane, row = lanes_of(shape), rows_of(shape)
        zp, zm, yp, ym, xp, xm = bounds(level)
        keep_yp = jnp.where(row == level.ny - 1, yp, 1.0)
        keep_ym = jnp.where(row == 0, ym, 1.0)
        keep_xp = jnp.where(lane == level.nx - 1, xp, 1.0)
        keep_xm = jnp.where(lane == 0, xm, 1.0)

        def step(z, carry):
            ze = z + 1

            def at(comp, dz=0, dy=0):
                return K[comp, ze + dz, pl.ds(RO + dy, rows), :]

            def along(comp, which, sign):
                value = at(comp)
                if level.split:
                    halo = R[f"KH{l}"][which, z]
                    value = jnp.where(lane == (level.right if sign > 0 else LANES - 1), halo, value)
                return roll(value, LANES - 1 if sign > 0 else 1)

            keep_zp = jnp.where(z == n - 1, zp, 1.0)
            keep_zm = jnp.where(z == 0, zm, 1.0)
            keep = ((keep_zp, keep_zm), (keep_yp, keep_ym), (keep_xp, keep_xm))
            weights = (
                (0.5 * (at(0) + at(0, 1)), 0.5 * (at(0) + at(0, -1))),
                (0.5 * (at(1) + at(1, 0, 1)), 0.5 * (at(1) + at(1, 0, -1))),
                (0.5 * (at(2) + along(2, 0, 1)), 0.5 * (at(2) + along(2, 0, -1))),
            )
            total = weights[0][0] + weights[0][1] + weights[1][0] + weights[1][1] + weights[2][0] + weights[2][1]
            diagonal = 1.0 + level.tau * total
            inverse = relax / diagonal
            scale = level.tau * inverse
            D[0, z] = inverse
            D[1, z] = diagonal * (1.0 / relax)
            for a in range(3):
                for s in range(2):
                    C[2 * a + s, z] = scale * weights[a][s] * keep[a][s]
            quarter = 0.25 * scale

            def shifted(comp, axis, sign):
                if axis == 0:
                    return at(comp, sign)
                if axis == 1:
                    return at(comp, 0, sign)
                return along(comp, 1 if comp == 4 else 2, sign)

            for number, (a, b, comp) in enumerate(PAIRS):
                ka = [shifted(comp, a, 1), shifted(comp, a, -1)]
                kb = [shifted(comp, b, 1), shifted(comp, b, -1)]
                for sa in range(2):
                    for sb in range(2):
                        value = quarter * (ka[sa] + kb[sb]) * keep[a][sa] * keep[b][sb]
                        C[6 + 4 * number + 2 * sa + sb, z] = value if sa == sb else -value
            return carry

        lax.fori_loop(0, n, step, 0, unroll=min(n, 4))

    def sweep(level, source, emit, halo=True):
        l = level.index
        V, C, G, XP, XM = R[f"V{l}"], R[f"C{l}"], R[f"G{l}"], R[f"XP{l}"], R[f"XM{l}"]
        rows = level.rows

        def shift(ze, carry):
            value = V[source, ze]
            up = down = value
            if halo:
                lane = lanes_of(value.shape)
                edge = R[f"H{l}"][source, ze]
                up = jnp.where(lane == level.right, edge, value)
                down = jnp.where(lane == LANES - 1, edge, value)
            XP[ze] = roll(up, LANES - 1)
            XM[ze] = roll(down, 1)
            return carry

        lax.fori_loop(0, level.nz + 2, shift, 0, unroll=level.nz + 2)

        def step(z, carry):
            ze = z + 1

            def at(dz, dy, dx):
                where_rows = pl.ds(RO + dy, rows)
                if dx == 0:
                    return V[source, ze + dz, where_rows, :]
                return (XP if dx > 0 else XM)[ze + dz, where_rows, :]

            center = at(0, 0, 0)
            parts = [G[z] - relax * center, None, None]
            offsets = [(1, 0, 0), (-1, 0, 0), (0, 1, 0), (0, -1, 0), (0, 0, 1), (0, 0, -1)]
            for a, b, _ in PAIRS:
                for sa in (1, -1):
                    for sb in (1, -1):
                        offset = [0, 0, 0]
                        offset[a], offset[b] = sa, sb
                        offsets.append(tuple(offset))
            for number, offset in enumerate(offsets):
                term = C[number, z] * at(*offset)
                slot = number % 3
                parts[slot] = term if parts[slot] is None else parts[slot] + term
            emit(z, center, (parts[0] + parts[1]) + parts[2])
            return carry

        lax.fori_loop(0, level.nz, step, 0, unroll=min(level.nz, 8))

    def into(level, slot):
        V = R[f"V{level.index}"]

        def emit(z, value, delta):
            V[slot, z + 1, pl.ds(RO, level.rows), :] = value + delta

        return emit

    pending = []
    count = [0]

    def drain():
        for copy in pending:
            copy.wait_send()
        pending.clear()

    def exchange(level, slot, step, during=None):
        l = level.index
        V, H, YB, PB, X = R[f"V{l}"], R[f"H{l}"], R[f"YB{l}"], R[f"PB{l}"], R["PX"]
        ZB = R[f"ZB{l}"]
        RZ, RY, RP = R[f"RZ{l}"], R[f"RY{l}"], R[f"RP{l}"]
        nz, ny, rows, zrows = level.nz, level.ny, level.rows, level.zrows
        drain()
        for z in range(nz):
            YB[0, pl.ds(z, 1), :] = V[slot, z + 1, pl.ds(RO, 1), :]
            YB[1, pl.ds(z, 1), :] = V[slot, z + 1, pl.ds(RO + ny - 1, 1), :]
        ZB[0] = V[slot, 1, pl.ds(RO, rows), :]
        ZB[1] = V[slot, nz, pl.ds(RO, rows), :]
        PB[...] = pack_x(level, lambda z: V[slot, z + 1, pl.ds(RO, rows), :])
        parity = count[0] % 2
        count[0] += 1
        copies = []
        ylow, zlow = rows - 8, zrows - 8
        for number, (kind, where, (ox, oy, oz)) in enumerate(MESSAGES):
            if kind == "z":
                src, dst = ZB.at[0 if where else 1], RZ.at[step, where]
            elif kind == "y":
                face = where // 3
                if where % 3 == 0:
                    src, dst = YB.at[face], RY.at[step, where]
                else:
                    low = 0 if where % 3 == 1 else zlow
                    src, dst = YB.at[face, pl.ds(low, 8)], RY.at[step, where, pl.ds(0, 8)]
            else:
                part = where % 5
                if part in (1, 2):
                    low = 0 if part == 1 else ylow
                    src, dst = PB.at[pl.ds(low, 8)], RP.at[step, where, pl.ds(0, 8)]
                else:
                    src, dst = PB, RP.at[step, where]
            copy = pltpu.make_async_remote_copy(
                src_ref=src, dst_ref=dst, send_sem=R["send"].at[number], recv_sem=R["recv"].at[parity, number],
                device_id=device(ox, oy, oz), device_id_type=MESH,
            )
            copy.start()
            copies.append(copy)
        pending.extend(copies)
        if during is not None:
            during()
        for copy in copies:
            copy.wait_recv()
        V[slot, nz + 1, pl.ds(RO, rows), :] = RZ[step, 1]
        V[slot, 0, pl.ds(RO, rows), :] = RZ[step, 0]
        for face in range(2):
            place = RO + ny if face == 0 else RO - 1
            for z in range(nz):
                V[slot, z + 1, pl.ds(place, 1), :] = RY[step, 3 * face, pl.ds(z, 1), :]
            V[slot, nz + 1, pl.ds(place, 1), :] = RY[step, 3 * face + 1, pl.ds(0, 1), :]
            V[slot, 0, pl.ds(place, 1), :] = RY[step, 3 * face + 2, pl.ds(nz - 1 - zlow, 1), :]

        def merged(part, size):
            even = lanes_of((size, LANES)) % 2 == 0
            return jnp.where(even, RP[step, part, pl.ds(0, size), :], RP[step, 5 + part, pl.ds(0, size), :])

        lane = lanes_of((rows, LANES))
        middle = merged(0, rows)
        above = roll(merged(3, rows), 2 * nz)
        below = roll(merged(4, rows), -2 * nz)

        def slab_lanes(ze):
            return (lane == (level.right + 2 * ze) % LANES) | (lane == (2 * ze + LANES - 1) % LANES)

        middle = jnp.where(slab_lanes(nz + 1), above, jnp.where(slab_lanes(0), below, middle))
        size = level.stride
        X[pl.ds(RO, rows), :] = middle
        X[pl.ds(RO + ny, 1), :] = merged(1, 8)[0:1]
        X[pl.ds(RO - 1, 1), :] = merged(2, 8)[ny - 1 - ylow : ny - ylow]
        whole = X[pl.ds(0, size), :]
        for ze in range(nz + 2):
            H[slot, ze] = roll(whole, -2 * ze)

    def start_faces(level):
        l = level.index
        K, KY, KP, KZ = R[f"K{l}"], R[f"KY{l}"], R[f"KP{l}"], R[f"KZ{l}"]
        nz, ny, rows = level.nz, level.ny, level.rows
        for i, comp in enumerate((0, 3, 4)):
            KZ[0, i] = K[comp, 1, pl.ds(RO, rows), :]
            KZ[1, i] = K[comp, nz, pl.ds(RO, rows), :]
        for i, comp in enumerate((1, 3, 5)):
            for z in range(nz):
                KY[0, i, pl.ds(z, 1), :] = K[comp, z + 1, pl.ds(RO, 1), :]
                KY[1, i, pl.ds(z, 1), :] = K[comp, z + 1, pl.ds(RO + ny - 1, 1), :]
        for i, comp in enumerate((2, 4, 5)):
            KP[i] = pack_x(level, lambda z: K[comp, z + 1, pl.ds(RO, rows), :])
        copies = []
        for number, (kind, where, (ox, oy, oz)) in enumerate(FACES):
            if kind == "z":
                src, dst = KZ.at[0 if where else 1], R[f"RKZ{l}"].at[where]
            elif kind == "y":
                src, dst = KY.at[where], R[f"RKY{l}"].at[where]
            else:
                src, dst = KP, R[f"RKP{l}"].at[where]
            copy = pltpu.make_async_remote_copy(
                src_ref=src, dst_ref=dst, send_sem=R["ksend"].at[l, number], recv_sem=R["krecv"].at[l, number],
                device_id=device(ox, oy, oz), device_id_type=MESH,
            )
            copy.start()
            copies.append(copy)
        return copies

    def finish_faces(level, copies):
        l = level.index
        K, KH = R[f"K{l}"], R[f"KH{l}"]
        nz, ny, rows = level.nz, level.ny, level.rows
        for copy in copies:
            copy.wait()
        for i, comp in enumerate((0, 3, 4)):
            K[comp, nz + 1, pl.ds(RO, rows), :] = R[f"RKZ{l}"][1, i] * in_zp
            K[comp, 0, pl.ds(RO, rows), :] = R[f"RKZ{l}"][0, i] * in_zm
        for i, comp in enumerate((1, 3, 5)):
            for z in range(nz):
                K[comp, z + 1, pl.ds(RO + ny, 1), :] = R[f"RKY{l}"][0, i, pl.ds(z, 1), :] * in_yp
                K[comp, z + 1, pl.ds(RO - 1, 1), :] = R[f"RKY{l}"][1, i, pl.ds(z, 1), :] * in_ym
        even = lanes_of((rows, LANES)) % 2 == 0
        for i in range(3):
            both = jnp.where(even, R[f"RKP{l}"][0, i] * in_xp, R[f"RKP{l}"][1, i] * in_xm)
            for z in range(nz):
                KH[i, z] = roll(both, -2 * (z + 1))

    class Gather:
        def __init__(self, tag, comps):
            self.tag, self.comps = tag, comps
            self.copies = []

        def send(self, phase, src, dst_of, targets):
            self.copies = []
            for number, offset in enumerate(targets):
                copy = pltpu.make_async_remote_copy(
                    src_ref=src, dst_ref=dst_of(number), send_sem=R[f"gs{self.tag}"].at[phase, number],
                    recv_sem=R[f"gr{self.tag}"].at[phase, number], device_id=device(*offset), device_id_type=MESH,
                )
                copy.start()
                self.copies.append(copy)

        def wait(self):
            for copy in self.copies:
                copy.wait()

        def phase_x(self, tiles):
            own, received = R[f"GX{self.tag}"], R[f"RX{self.tag}"]
            own[...] = tiles
            self.send(0, own, lambda number: received.at[number], [(k, 0, 0) for k in range(1, GX)])

        def phase_y(self):
            self.wait()
            slots = R[f"RY{self.tag}"]
            total = R[f"GX{self.tag}"][...]
            for k in range(GX - 1):
                total = total + R[f"RX{self.tag}"][k]
            slots[gy] = total
            self.send(1, slots.at[gy], lambda number: slots.at[gy], [(0, k, 0) for k in range(1, GY)])

        def phase_z(self):
            self.wait()
            slots, out = R[f"RY{self.tag}"], R[f"RZ{self.tag}"]
            for i in range(self.comps):
                for y in range(GY):
                    out[gz, i, pl.ds(2 * y, 2), :] = slots[y, pl.ds(2 * i, 2), :]
            self.send(2, out.at[gz], lambda number: out.at[gz], [(0, 0, k) for k in range(1, GZ)])

        def finish(self, store):
            self.wait()
            out = R[f"RZ{self.tag}"]
            for i in range(self.comps):
                for z in range(GZ):
                    value = out[z, i]
                    left = lanes_of(value.shape) < 64
                    store(i, 2 * z, jnp.where(left, value, 0.0))
                    store(i, 2 * z + 1, jnp.where(left, roll(value, 64), 0.0))

    def own_tile(values, comps, total_rows):
        T = R["tile"]
        T[...] = jnp.zeros(T.shape, F32)
        for i in range(comps):
            low = values[(2 * i) * 8 : (2 * i) * 8 + 8]
            high = values[(2 * i + 1) * 8 : (2 * i + 1) * 8 + 8]
            T[pl.ds(2 * i, 2), :] = (low + roll(high, 64))[0:2]
        return roll(T[pl.ds(0, total_rows), :], 16 * gx)

    L0, L1, L2, L3, L4 = levels
    for level in (L3, L4):
        for name in ("K", "V"):
            ref = R[f"{name}{level.index}"]
            for i in range(ref.shape[0]):
                ref[i] = jnp.zeros(ref.shape[1:], F32)

    def fill(z, carry):
        weight = R["tissue"][z].astype(F32)
        for comp in range(3):
            R["K0"][comp, z + 1, pl.ds(RO, L0.rows), :] = R["conduct"][comp, z] * weight
            R["K0"][3 + comp, z + 1, pl.ds(RO, L0.rows), :] = R["cross"][comp, z] * weight
        return carry

    lax.fori_loop(0, L0.nz, fill, 0, unroll=4)
    pl.semaphore_wait(barrier, len(unique))
    faces0 = start_faces(L0)

    def coarser_tensor(level, lower):
        coarsen_rows(level, lower, lambda i, z, rows: R[f"K{level.index}"][i, z + 1, rows, :], 6)
        height = (level.nz // 2) * lower.rows
        values = coarsen_lanes(level, 6 * height)
        if lower.split:
            for i in range(6):
                for z in range(lower.nz):
                    start = i * height + z * lower.rows
                    R[f"K{lower.index}"][i, z + 1, pl.ds(RO, lower.rows), :] = values[start : start + lower.rows]
        return values

    R["stage"][...] = jnp.zeros(R["stage"].shape, F32)
    coarser_tensor(L0, L1)
    faces1 = start_faces(L1)
    coarser_tensor(L1, L2)
    faces2 = start_faces(L2)
    block3 = Level(3, 2, 2, 16, False)
    gather_k = Gather("k", 6)
    gather_k.phase_x(own_tile(coarser_tensor(L2, block3), 6, 16))

    zl = R["src_z"][...] - gz * L0.nz
    yl = R["src_y"][...] - gy * L0.ny
    xl = R["src_x"][...] - gx * L0.nx
    inside = (zl >= 0) & (zl < L0.nz) & (yl >= 0) & (yl < L0.ny)
    R["key"][0:1, :] = jnp.where(inside, zl * L0.ny + yl, -1)
    R["key"][1:2, :] = xl
    R["counts"][...] = jnp.zeros(R["counts"].shape, F32)
    chunk = 256

    def scatter(i, carry):
        start = pl.multiple_of(i * chunk, chunk)
        key = R["key"][0:1, pl.ds(start, chunk)]
        key_x = R["key"][1:2, pl.ds(start, chunk)]
        left = jnp.where(rows_of((L0.nz * L0.ny, chunk)) == key, 1.0, 0.0).astype(jnp.bfloat16)
        right = jnp.where(rows_of((LANES, chunk)) == key_x, 1.0, 0.0).astype(jnp.bfloat16)
        R["counts"][...] += lax.dot_general(left, right, (((1,), (1,)), ((), ())), preferred_element_type=F32)
        return carry

    lax.fori_loop(0, sources // chunk, scatter, 0, unroll=2)

    finish_faces(L0, faces0)
    coefficients(L0)

    def load0(z):
        return stim_height * R["counts"][pl.ds(pl.multiple_of(z * L0.ny, 8), L0.rows), :]

    def first_sweep(level, load):
        l = level.index

        def step(z, carry):
            value = load(z) * R[f"D{l}"][0, z]
            R[f"G{l}"][z] = value
            R[f"V{l}"][0, z + 1, pl.ds(RO, level.rows), :] = value
            return carry

        lax.fori_loop(0, level.nz, step, 0, unroll=min(level.nz, 8))

    def residual(level, slot, halo=True):
        l = level.index
        store = R[f"XR{l}"]

        def emit(z, value, delta):
            store[z, pl.ds(RO, level.rows), :] = delta * R[f"D{l}"][1, z]

        sweep(level, slot, emit, halo)

    def restricted(level, lower):
        coarsen_rows(level, lower, lambda i, z, rows: R[f"XR{level.index}"][z, rows, :], 1)
        return coarsen_lanes(level, (level.nz // 2) * lower.rows)

    def during_01():
        gather_k.phase_y()
        finish_faces(L1, faces1)
        coefficients(L1)

    def during_02():
        gather_k.phase_z()
        finish_faces(L2, faces2)
        coefficients(L2)

    def coarse_setup():
        def store(i, z, value):
            R["K3"][i, z + 1, pl.ds(RO, L3.rows), :] = clean(L3, value)

        gather_k.finish(store)
        coefficients(L3)
        coarsen_rows(L3, L4, lambda i, z, rows: R["K3"][i, z + 1, rows, :], 6)
        height = L4.nz * L4.rows
        values = coarsen_lanes(L3, 6 * height)
        for i in range(6):
            for z in range(L4.nz):
                start = i * height + z * L4.rows
                R["K4"][i, z + 1, pl.ds(RO, L4.rows), :] = clean(L4, values[start : start + L4.rows])
        coefficients(L4)

    during = {(0, 0): during_01, (0, 1): during_02, (2, 0): coarse_setup}

    first_sweep(L0, load0)
    for level, lower in ((L0, L1), (L1, L2), (L2, block3)):
        l = level.index
        exchange(level, 0, 0, during.get((l, 0)))
        sweep(level, 0, into(level, 1))
        exchange(level, 1, 1, during.get((l, 1)))
        residual(level, 1)
        values = restricted(level, lower)
        if lower.split:
            R["load"][pl.ds(0, lower.nz * lower.rows), :] = values
            first_sweep(lower, lambda z: R["load"][pl.ds(pl.multiple_of(z * lower.rows, 8), lower.rows), :])

    gather_f = Gather("f", 1)
    gather_f.phase_x(own_tile(values, 1, 8))
    gather_f.phase_y()
    gather_f.phase_z()

    def store_load(i, z, value):
        R["load"][pl.ds(z * L3.rows, L3.rows), :] = value

    gather_f.finish(store_load)

    def load_of(level):
        return lambda z: clean(level, R["load"][pl.ds(pl.multiple_of(z * level.rows, 8), level.rows), :])

    first_sweep(L3, load_of(L3))
    sweep(L3, 0, into(L3, 1), False)
    residual(L3, 1, False)
    values = restricted(L3, L4)
    R["load"][pl.ds(0, L4.nz * L4.rows), :] = values
    first_sweep(L4, load_of(L4))
    for i in range(COARSE - 1):
        sweep(L4, i % 2, into(L4, (i + 1) % 2), False)
    last4 = (COARSE - 1) % 2

    def spread(level, nz_c, ny_c, nx_c, stride_c, get, base, halo):
        l = level.index
        M, PV = R["merge"], R["spread"]
        a, b = rows_of((LANES, LANES)), lanes_of((LANES, LANES))
        main = (a == b // 2) & (b < level.nx)
        edges = ((a == nx_c) & (b == level.right)) | ((a == LANES - 1) & (b == LANES - 1))
        wide = halo and level.nx == LANES
        if halo and not wide:
            main = main | edges
        height = (nz_c + 2) * stride_c
        stacked = jnp.concatenate([get(ze) for ze in range(nz_c + 2)], axis=0)
        M[0, pl.ds(0, height), :] = dot(stacked, jnp.where(main, 1.0, 0.0).astype(F32))
        if wide:
            M[1, pl.ds(0, height), :] = dot(stacked, jnp.where(edges, 1.0, 0.0).astype(F32))
        V = R[f"V{l}"]
        for layer in range(2 if wide else 1):
            for ze in range(nz_c + 2):
                value = M[layer, pl.ds(ze * stride_c + RO - 1, ny_c + 2), :]
                slabs = [zf for zf in (2 * ze - 1, 2 * ze) if 0 <= zf <= level.nz + 1]
                for phase in range(2):
                    PV[layer, ze, pl.ds(RO - 2 + phase, ny_c + 2, stride=2), :] = value
        for ze in range(nz_c + 2):
            for zf in (2 * ze - 1, 2 * ze):
                if 0 <= zf <= level.nz + 1:
                    size = level.stride
                    V[2, zf] = V[1, zf] + PV[0, ze, pl.ds(0, size), :]
                    if halo:
                        H = R[f"H{l}"]
                        H[2, zf] = H[1, zf] + PV[1 if wide else 0, ze, pl.ds(0, size), :]

    def coarse_slab(level, slot):
        V = R[f"V{level.index}"]

        def get(ze):
            value = V[slot, ze]
            if level.split:
                lane = lanes_of(value.shape)
                edge = (lane == level.right) | (lane == LANES - 1)
                value = jnp.where(edge, R[f"H{level.index}"][slot, ze], value)
            return value

        return get

    spread(L3, L4.nz, L4.ny, L4.nx, L4.stride, coarse_slab(L4, last4), 0, False)
    sweep(L3, 2, into(L3, 0), False)
    sweep(L3, 0, into(L3, 1), False)

    def own_slab(ze):
        value = R["V3"][1, 2 * gz + ze]
        value = roll(value, L3.stride - 2 * gy, axis=0)
        value = roll(value, LANES - 16 * gx)
        return value[0:24]

    spread(L2, 2, 2, 16, 24, own_slab, 0, True)
    for level in (L2, L1):
        sweep(level, 2, into(level, 3))
        exchange(level, 3, 2)
        sweep(level, 3, into(level, 0))
        exchange(level, 0, 3)
        finer = levels[level.index - 1]
        spread(finer, level.nz, level.ny, level.nx, level.stride, coarse_slab(level, 0), 0, True)
    sweep(L0, 2, into(L0, 3))
    exchange(L0, 3, 2)

    def emit_out(z, value, delta):
        R["out"][z] = value + delta

    sweep(L0, 3, emit_out)
    drain()


def solution(mesh):
    sizes = (mesh.shape["gx"], mesh.shape["gy"], mesh.shape["gz"])
    GX, GY, GZ = sizes

    def body(conduct, cross, tissue, src_z, src_y, src_x):
        nz, ny, nx = tissue.shape
        sources = src_z.shape[0]
        levels = [Level(l, nz >> l, ny >> l, nx >> l, True) for l in range(3)]
        levels.append(Level(3, 2 * GZ, 2 * GY, 16 * GX, False))
        levels.append(Level(4, GZ, GY, 8 * GX, False))
        scratch = {}

        def vmem(name, *shape, dtype=F32):
            scratch[name] = pltpu.VMEM(shape, dtype)

        for level in levels:
            l, z, rows, stride, zrows = level.index, level.nz, level.rows, level.stride, level.zrows
            slots = 4 if level.split else 3
            vmem(f"K{l}", 6, z + 2, stride, LANES)
            vmem(f"C{l}", 18, z, rows, LANES)
            vmem(f"D{l}", 2, z, rows, LANES)
            vmem(f"G{l}", z, rows, LANES)
            vmem(f"V{l}", slots, z + 2, stride, LANES)
            vmem(f"XP{l}", z + 2, stride, LANES)
            vmem(f"XM{l}", z + 2, stride, LANES)
            vmem(f"XR{l}", z, stride, LANES)
            if level.split:
                vmem(f"H{l}", slots, z + 2, stride, LANES)
                vmem(f"KH{l}", 3, z, rows, LANES)
                vmem(f"YB{l}", 2, zrows, LANES)
                vmem(f"PB{l}", rows, LANES)
                vmem(f"ZB{l}", 2, rows, LANES)
                vmem(f"RZ{l}", 4, 2, rows, LANES)
                vmem(f"RY{l}", 4, 6, zrows, LANES)
                vmem(f"RP{l}", 4, 10, rows, LANES)
                vmem(f"KZ{l}", 2, 3, rows, LANES)
                vmem(f"KY{l}", 2, 3, zrows, LANES)
                vmem(f"KP{l}", 3, rows, LANES)
                vmem(f"RKZ{l}", 2, 3, rows, LANES)
                vmem(f"RKY{l}", 2, 3, zrows, LANES)
                vmem(f"RKP{l}", 2, 3, rows, LANES)
        vmem("PX", levels[0].stride, LANES)
        vmem("stage", 6 * 8 * 8, LANES)
        vmem("tile", 16, LANES)
        vmem("key", 2, sources, dtype=jnp.int32)
        vmem("counts", nz * ny, LANES)
        vmem("load", max(levels[3].nz * levels[3].rows, 64), LANES)
        vmem("merge", 2, 10 * 32, LANES)
        vmem("spread", 2, 10, 48, LANES)
        for tag, comps, height in (("k", 6, 16), ("f", 1, 8)):
            vmem(f"GX{tag}", height, LANES)
            vmem(f"RX{tag}", GX - 1, height, LANES)
            vmem(f"RY{tag}", GY, height, LANES)
            vmem(f"RZ{tag}", GZ, comps, levels[3].rows, LANES)
            most = max(sizes) - 1
            scratch[f"gs{tag}"] = pltpu.SemaphoreType.DMA((3, most))
            scratch[f"gr{tag}"] = pltpu.SemaphoreType.DMA((3, most))
        scratch["send"] = pltpu.SemaphoreType.DMA((len(MESSAGES),))
        scratch["recv"] = pltpu.SemaphoreType.DMA((2, len(MESSAGES)))
        scratch["ksend"] = pltpu.SemaphoreType.DMA((3, len(FACES)))
        scratch["krecv"] = pltpu.SemaphoreType.DMA((3, len(FACES)))
        names = ["conduct", "cross", "tissue", "src_z", "src_y", "src_x", "out"] + list(scratch)
        row = lambda value: value.reshape(1, sources)
        return pl.pallas_call(
            functools.partial(kernel, names, levels, sizes, sources),
            out_shape=jax.ShapeDtypeStruct((nz, ny, nx), F32),
            in_specs=[pl.BlockSpec(memory_space=pltpu.VMEM)] * 6,
            out_specs=pl.BlockSpec(memory_space=pltpu.VMEM),
            scratch_shapes=list(scratch.values()),
            compiler_params=pltpu.CompilerParams(
                collective_id=0, has_side_effects=True, vmem_limit_bytes=60 * 1024 * 1024
            ),
        )(conduct, cross, tissue, row(src_z), row(src_y), row(src_x))

    placed = (P(None, "gz", "gy", "gx"), P(None, "gz", "gy", "gx"), P("gz", "gy", "gx"), P(), P(), P())
    return jax.shard_map(body, mesh=mesh, in_specs=placed, out_specs=P("gz", "gy", "gx"), check_vma=False)
```

```python
import functools

import jax
import jax.numpy as jnp
from jax import lax
from jax.experimental import pallas as pl
from jax.experimental.pallas import tpu as pltpu
from jax.sharding import PartitionSpec as P

tau_step = 4000.0
relax = 0.55
stim_height = 64000.0
COARSE = 12
RO = 8
LANES = 128
MESH = pl.DeviceIdType.MESH
F32 = jnp.float32
PAIRS = ((0, 1, 3), (0, 2, 4), (1, 2, 5))


class Level:
    def __init__(self, index, nz, ny, nx, split, region=False):
        self.index, self.nz, self.ny, self.nx, self.split, self.region = index, nz, ny, nx, split, region
        self.rows = max(8, -(-ny // 8) * 8)
        self.zrows = max(8, -(-nz // 8) * 8)
        self.stride = RO + self.rows + 8
        self.tau = tau_step / 4.0**index
        self.right = nx % LANES


def lanes_of(shape):
    return lax.broadcasted_iota(jnp.int32, shape, len(shape) - 1)


def rows_of(shape):
    return lax.broadcasted_iota(jnp.int32, shape, len(shape) - 2)


def roll(value, shift, axis=None):
    axis = value.ndim - 1 if axis is None else axis
    if isinstance(shift, int):
        shift = shift % value.shape[axis]
        if shift == 0:
            return value
    return pltpu.roll(value, shift, axis)


def dot(a, b):
    return lax.dot_general(
        a, b, (((1,), (0,)), ((), ())), precision=lax.Precision.HIGHEST, preferred_element_type=F32
    )


MESSAGES = [("z", 1, (0, 0, -1)), ("z", 0, (0, 0, 1))]
for _face, _oy in ((0, -1), (1, 1)):
    for _part, _oz in ((0, 0), (1, -1), (2, 1)):
        MESSAGES.append(("y", 3 * _face + _part, (0, _oy, _oz)))
for _side, _ox in ((0, -1), (1, 1)):
    for _part, (_oy, _oz) in enumerate(((0, 0), (-1, 0), (1, 0), (0, -1), (0, 1))):
        MESSAGES.append(("p", 5 * _side + _part, (_ox, _oy, _oz)))
AROUND = [(dx, dy, dz) for dz in (-1, 0, 1) for dy in (-1, 0, 1) for dx in (-1, 0, 1) if (dx, dy, dz) != (0, 0, 0)]
FACES = [("z", 1, (0, 0, -1)), ("z", 0, (0, 0, 1)), ("y", 0, (0, -1, 0)), ("y", 1, (0, 1, 0)), ("p", 0, (-1, 0, 0)), ("p", 1, (1, 0, 0))]


def kernel(names, levels, sizes, sources, *refs):
    R = dict(zip(names, refs))
    GX, GY, GZ = sizes
    gx, gy, gz = lax.axis_index("gx"), lax.axis_index("gy"), lax.axis_index("gz")

    def device(ox, oy, oz):
        return (lax.rem(gx + (ox + GX), GX), lax.rem(gy + (oy + GY), GY), lax.rem(gz + (oz + GZ), GZ))

    peers = list(AROUND)
    peers += [(k, 0, 0) for k in range(1, GX)] + [(0, k, 0) for k in range(1, GY)] + [(0, 0, k) for k in range(1, GZ)]
    seen, unique = set(), []
    for ox, oy, oz in peers:
        key = (ox % GX, oy % GY, oz % GZ)
        if key not in seen:
            seen.add(key)
            unique.append(key)
    barrier = pltpu.get_barrier_semaphore()
    for ox, oy, oz in unique:
        pl.semaphore_signal(barrier, inc=1, device_id=device(ox, oy, oz), device_id_type=MESH)

    def flag(condition):
        return jnp.where(condition, 0.0, 1.0).astype(F32)

    in_xp, in_xm = flag(gx == GX - 1), flag(gx == 0)
    in_yp, in_ym = flag(gy == GY - 1), flag(gy == 0)
    in_zp, in_zm = flag(gz == GZ - 1), flag(gz == 0)

    def clean(level, value):
        return value if level.ny == level.rows else jnp.where(rows_of(value.shape) < level.ny, value, 0.0)

    def bounds(level):
        if level.split:
            return in_zp, in_zm, in_yp, in_ym, in_xp, in_xm
        return (jnp.zeros((), F32),) * 6

    def inside(level, z):
        third_z, third_y, third_x = level.nz // 3, level.ny // 3, level.nx // 3
        shape = (level.rows, LANES)
        lane, row = lanes_of(shape), rows_of(shape)
        mask_z = jnp.where(z < third_z, in_zm, jnp.where(z >= 2 * third_z, in_zp, 1.0))
        mask_y = jnp.where(row < third_y, in_ym, jnp.where(row >= 2 * third_y, in_yp, 1.0))
        mask_x = jnp.where(lane < third_x, in_xm, jnp.where(lane >= 2 * third_x, in_xp, 1.0))
        return jnp.where((row < level.ny) & (lane < level.nx), mask_z * mask_y * mask_x, 0.0)

    def pack_x(level, get):
        shape = (level.rows, LANES)
        lane = lanes_of(shape)
        out = jnp.zeros(shape, F32)
        for z in range(level.nz):
            value = get(z)
            first = (level.right + 2 * (z + 1)) % LANES
            last = (2 * (z + 1) + LANES - 1) % LANES
            a = roll(value, first)
            b = roll(value, last - (level.nx - 1))
            out = jnp.where(lane == first, a, jnp.where(lane == last, b, out))
        return out

    def coarsen_rows(level, lower, get, count):
        stage = R["stage"]
        half = level.ny // 2
        for i in range(count):
            for z in range(level.nz // 2):
                total = None
                for dz in range(2):
                    for dy in range(2):
                        piece = get(i, 2 * z + dz, dy, half)
                        total = piece if total is None else total + piece
                stage[pl.ds((i * (level.nz // 2) + z) * lower.rows, half), :] = total

    def coarsen_lanes(level, rows, first=0):
        a, b = rows_of((LANES, LANES)), lanes_of((LANES, LANES))
        matrix = jnp.where((b == (a - first) // 2) & (a >= first) & (b < level.nx // 2), 0.125, 0.0).astype(F32)
        return dot(R["stage"][pl.ds(0, rows), :], matrix)

    def coefficients(level):
        l = level.index
        K, C, D = R[f"K{l}"], R[f"C{l}"], R[f"D{l}"]
        n, rows = level.nz, level.rows
        shape = (rows, LANES)
        lane, row = lanes_of(shape), rows_of(shape)
        zp, zm, yp, ym, xp, xm = bounds(level)
        keep_yp = jnp.where(row == level.ny - 1, yp, 1.0)
        keep_ym = jnp.where(row == 0, ym, 1.0)
        keep_xp = jnp.where(lane == level.nx - 1, xp, 1.0)
        keep_xm = jnp.where(lane == 0, xm, 1.0)

        def step(z, carry):
            ze = z + 1

            def at(comp, dz=0, dy=0):
                return K[comp, ze + dz, pl.ds(RO + dy, rows), :]

            def along(comp, which, sign):
                value = at(comp)
                if level.split:
                    halo = R[f"KH{l}"][which, z]
                    value = jnp.where(lane == (level.right if sign > 0 else LANES - 1), halo, value)
                return roll(value, LANES - 1 if sign > 0 else 1)

            keep_zp = jnp.where(z == n - 1, zp, 1.0)
            keep_zm = jnp.where(z == 0, zm, 1.0)
            keep = ((keep_zp, keep_zm), (keep_yp, keep_ym), (keep_xp, keep_xm))
            weights = (
                (0.5 * (at(0) + at(0, 1)), 0.5 * (at(0) + at(0, -1))),
                (0.5 * (at(1) + at(1, 0, 1)), 0.5 * (at(1) + at(1, 0, -1))),
                (0.5 * (at(2) + along(2, 0, 1)), 0.5 * (at(2) + along(2, 0, -1))),
            )
            total = weights[0][0] + weights[0][1] + weights[1][0] + weights[1][1] + weights[2][0] + weights[2][1]
            diagonal = 1.0 + level.tau * total
            inverse = relax / diagonal
            scale = level.tau * inverse
            if level.region:
                scale = scale * inside(level, z)
            D[0, z] = inverse
            D[1, z] = diagonal * (1.0 / relax)
            for a in range(3):
                for s in range(2):
                    C[2 * a + s, z] = scale * weights[a][s] * keep[a][s]
            quarter = 0.25 * scale

            def shifted(comp, axis, sign):
                if axis == 0:
                    return at(comp, sign)
                if axis == 1:
                    return at(comp, 0, sign)
                return along(comp, 1 if comp == 4 else 2, sign)

            for number, (a, b, comp) in enumerate(PAIRS):
                ka = [shifted(comp, a, 1), shifted(comp, a, -1)]
                kb = [shifted(comp, b, 1), shifted(comp, b, -1)]
                for sa in range(2):
                    for sb in range(2):
                        value = quarter * (ka[sa] + kb[sb]) * keep[a][sa] * keep[b][sb]
                        C[6 + 4 * number + 2 * sa + sb, z] = value if sa == sb else -value
            return carry

        lax.fori_loop(0, n, step, 0, unroll=min(n, 4))

    def sweep(level, source, emit, halo=True, first=0, last=None):
        l = level.index
        V, C, G, XP, XM = R[f"V{l}"], R[f"C{l}"], R[f"G{l}"], R[f"XP{l}"], R[f"XM{l}"]
        rows = level.rows

        def shift(ze, carry):
            value = V[source, ze]
            up = down = value
            if halo:
                lane = lanes_of(value.shape)
                edge = R[f"H{l}"][source, ze]
                up = jnp.where(lane == level.right, edge, value)
                down = jnp.where(lane == LANES - 1, edge, value)
            XP[ze] = roll(up, LANES - 1)
            XM[ze] = roll(down, 1)
            return carry

        last = level.nz if last is None else last
        lax.fori_loop(first, last + 2, shift, 0, unroll=last + 2 - first)

        def step(z, carry):
            ze = z + 1

            def at(dz, dy, dx):
                where_rows = pl.ds(RO + dy, rows)
                if dx == 0:
                    return V[source, ze + dz, where_rows, :]
                return (XP if dx > 0 else XM)[ze + dz, where_rows, :]

            center = at(0, 0, 0)
            parts = [G[z] - relax * center, None, None]
            offsets = [(1, 0, 0), (-1, 0, 0), (0, 1, 0), (0, -1, 0), (0, 0, 1), (0, 0, -1)]
            for a, b, _ in PAIRS:
                for sa in (1, -1):
                    for sb in (1, -1):
                        offset = [0, 0, 0]
                        offset[a], offset[b] = sa, sb
                        offsets.append(tuple(offset))
            for number, offset in enumerate(offsets):
                term = C[number, z] * at(*offset)
                slot = number % 3
                parts[slot] = term if parts[slot] is None else parts[slot] + term
            emit(z, center, (parts[0] + parts[1]) + parts[2])
            return carry

        lax.fori_loop(first, last, step, 0, unroll=min(last - first, 8))

    def into(level, slot):
        V = R[f"V{level.index}"]

        def emit(z, value, delta):
            V[slot, z + 1, pl.ds(RO, level.rows), :] = value + delta

        return emit

    pending = []
    count = [0]

    def drain():
        for copy in pending:
            copy.wait_send()
        pending.clear()

    def exchange(level, slot, step, during=None):
        l = level.index
        V, H, YB, PB, X = R[f"V{l}"], R[f"H{l}"], R[f"YB{l}"], R[f"PB{l}"], R["PX"]
        ZB = R[f"ZB{l}"]
        RZ, RY, RP = R[f"RZ{l}"], R[f"RY{l}"], R[f"RP{l}"]
        nz, ny, rows, zrows = level.nz, level.ny, level.rows, level.zrows
        drain()
        for z in range(nz):
            YB[0, pl.ds(z, 1), :] = V[slot, z + 1, pl.ds(RO, 1), :]
            YB[1, pl.ds(z, 1), :] = V[slot, z + 1, pl.ds(RO + ny - 1, 1), :]
        ZB[0] = V[slot, 1, pl.ds(RO, rows), :]
        ZB[1] = V[slot, nz, pl.ds(RO, rows), :]
        PB[...] = pack_x(level, lambda z: V[slot, z + 1, pl.ds(RO, rows), :])
        parity = count[0] % 2
        count[0] += 1
        copies = []
        ylow, zlow = rows - 8, zrows - 8
        for number, (kind, where, (ox, oy, oz)) in enumerate(MESSAGES):
            if kind == "z":
                src, dst = ZB.at[0 if where else 1], RZ.at[step, where]
            elif kind == "y":
                face = where // 3
                if where % 3 == 0:
                    src, dst = YB.at[face], RY.at[step, where]
                else:
                    low = 0 if where % 3 == 1 else zlow
                    src, dst = YB.at[face, pl.ds(low, 8)], RY.at[step, where, pl.ds(0, 8)]
            else:
                part = where % 5
                if part in (1, 2):
                    low = 0 if part == 1 else ylow
                    src, dst = PB.at[pl.ds(low, 8)], RP.at[step, where, pl.ds(0, 8)]
                else:
                    src, dst = PB, RP.at[step, where]
            copy = pltpu.make_async_remote_copy(
                src_ref=src, dst_ref=dst, send_sem=R["send"].at[number], recv_sem=R["recv"].at[parity, number],
                device_id=device(ox, oy, oz), device_id_type=MESH,
            )
            copy.start()
            copies.append(copy)
        pending.extend(copies)
        if during is not None:
            during()
        for copy in copies:
            copy.wait_recv()
        V[slot, nz + 1, pl.ds(RO, rows), :] = RZ[step, 1]
        V[slot, 0, pl.ds(RO, rows), :] = RZ[step, 0]
        for face in range(2):
            place = RO + ny if face == 0 else RO - 1
            for z in range(nz):
                V[slot, z + 1, pl.ds(place, 1), :] = RY[step, 3 * face, pl.ds(z, 1), :]
            V[slot, nz + 1, pl.ds(place, 1), :] = RY[step, 3 * face + 1, pl.ds(0, 1), :]
            V[slot, 0, pl.ds(place, 1), :] = RY[step, 3 * face + 2, pl.ds(nz - 1 - zlow, 1), :]

        def merged(part, size):
            even = lanes_of((size, LANES)) % 2 == 0
            return jnp.where(even, RP[step, part, pl.ds(0, size), :], RP[step, 5 + part, pl.ds(0, size), :])

        lane = lanes_of((rows, LANES))
        middle = merged(0, rows)
        above = roll(merged(3, rows), 2 * nz)
        below = roll(merged(4, rows), -2 * nz)

        def slab_lanes(ze):
            return (lane == (level.right + 2 * ze) % LANES) | (lane == (2 * ze + LANES - 1) % LANES)

        middle = jnp.where(slab_lanes(nz + 1), above, jnp.where(slab_lanes(0), below, middle))
        size = level.stride
        X[pl.ds(RO, rows), :] = middle
        X[pl.ds(RO + ny, 1), :] = merged(1, 8)[0:1]
        X[pl.ds(RO - 1, 1), :] = merged(2, 8)[ny - 1 - ylow : ny - ylow]
        whole = X[pl.ds(0, size), :]
        for ze in range(nz + 2):
            H[slot, ze] = roll(whole, -2 * ze)

    def start_faces(level):
        l = level.index
        K, KY, KP, KZ = R[f"K{l}"], R[f"KY{l}"], R[f"KP{l}"], R[f"KZ{l}"]
        nz, ny, rows = level.nz, level.ny, level.rows
        for i, comp in enumerate((0, 3, 4)):
            KZ[0, i] = K[comp, 1, pl.ds(RO, rows), :]
            KZ[1, i] = K[comp, nz, pl.ds(RO, rows), :]
        for i, comp in enumerate((1, 3, 5)):
            for z in range(nz):
                KY[0, i, pl.ds(z, 1), :] = K[comp, z + 1, pl.ds(RO, 1), :]
                KY[1, i, pl.ds(z, 1), :] = K[comp, z + 1, pl.ds(RO + ny - 1, 1), :]
        for i, comp in enumerate((2, 4, 5)):
            KP[i] = pack_x(level, lambda z: K[comp, z + 1, pl.ds(RO, rows), :])
        copies = []
        for number, (kind, where, (ox, oy, oz)) in enumerate(FACES):
            if kind == "z":
                src, dst = KZ.at[0 if where else 1], R[f"RKZ{l}"].at[where]
            elif kind == "y":
                src, dst = KY.at[where], R[f"RKY{l}"].at[where]
            else:
                src, dst = KP, R[f"RKP{l}"].at[where]
            copy = pltpu.make_async_remote_copy(
                src_ref=src, dst_ref=dst, send_sem=R["ksend"].at[l, number], recv_sem=R["krecv"].at[l, number],
                device_id=device(ox, oy, oz), device_id_type=MESH,
            )
            copy.start()
            copies.append(copy)
        return copies

    def finish_faces(level, copies):
        l = level.index
        K, KH = R[f"K{l}"], R[f"KH{l}"]
        nz, ny, rows = level.nz, level.ny, level.rows
        for copy in copies:
            copy.wait()
        for i, comp in enumerate((0, 3, 4)):
            K[comp, nz + 1, pl.ds(RO, rows), :] = R[f"RKZ{l}"][1, i] * in_zp
            K[comp, 0, pl.ds(RO, rows), :] = R[f"RKZ{l}"][0, i] * in_zm
        for i, comp in enumerate((1, 3, 5)):
            for z in range(nz):
                K[comp, z + 1, pl.ds(RO + ny, 1), :] = R[f"RKY{l}"][0, i, pl.ds(z, 1), :] * in_yp
                K[comp, z + 1, pl.ds(RO - 1, 1), :] = R[f"RKY{l}"][1, i, pl.ds(z, 1), :] * in_ym
        even = lanes_of((rows, LANES)) % 2 == 0
        for i in range(3):
            both = jnp.where(even, R[f"RKP{l}"][0, i] * in_xp, R[f"RKP{l}"][1, i] * in_xm)
            for z in range(nz):
                KH[i, z] = roll(both, -2 * (z + 1))

    def start_around(tag):
        tag_index = "kfp".index(tag)
        copies = []
        for number, (dx, dy, dz) in enumerate(AROUND):
            copy = pltpu.make_async_remote_copy(
                src_ref=R[f"TA{tag}"], dst_ref=R[f"RA{tag}"].at[number], send_sem=R["asend"].at[tag_index, number],
                recv_sem=R["arecv"].at[tag_index, number], device_id=device(-dx, -dy, -dz), device_id_type=MESH,
            )
            copy.start()
            copies.append(copy)
        return copies

    def finish_around(tag, copies, comps, store):
        for copy in copies:
            copy.wait()
        tile = R[f"TA{tag}"]
        lane = lanes_of(tile.shape)
        for dz in (-1, 0, 1):
            for dy in (-1, 0, 1):
                row_tiles = []
                for dx in (-1, 0, 1):
                    if (dx, dy, dz) == (0, 0, 0):
                        row_tiles.append(tile[...])
                        continue
                    value = R[f"RA{tag}"][AROUND.index((dx, dy, dz))]
                    valid = None
                    for d, plus, minus in ((dx, in_xp, in_xm), (dy, in_yp, in_ym), (dz, in_zp, in_zm)):
                        if d:
                            factor = plus if d > 0 else minus
                            valid = factor if valid is None else valid * factor
                    row_tiles.append(value * valid)
                for z in range(4):
                    low, mid, high = (roll(row_tiles[i], 32 * i - 32 * z) for i in range(3))
                    value = jnp.where(lane < 32, low, jnp.where(lane < 64, mid, jnp.where(lane < 96, high, 0.0)))
                    for comp in range(comps):
                        store(comp, 4 * (dz + 1) + z, 4 * (dy + 1), value[4 * comp : 4 * comp + 4])

    class Gather:
        def __init__(self, tag, comps):
            self.tag, self.comps = tag, comps
            self.copies = []

        def send(self, phase, src, dst_of, targets):
            self.copies = []
            for number, offset in enumerate(targets):
                copy = pltpu.make_async_remote_copy(
                    src_ref=src, dst_ref=dst_of(number), send_sem=R[f"gs{self.tag}"].at[phase, number],
                    recv_sem=R[f"gr{self.tag}"].at[phase, number], device_id=device(*offset), device_id_type=MESH,
                )
                copy.start()
                self.copies.append(copy)

        def wait(self):
            for copy in self.copies:
                copy.wait()

        def phase_x(self, tiles):
            own, received = R[f"GX{self.tag}"], R[f"RX{self.tag}"]
            own[...] = tiles
            self.send(0, own, lambda number: received.at[number], [(k, 0, 0) for k in range(1, GX)])

        def phase_y(self):
            self.wait()
            slots = R[f"RY{self.tag}"]
            total = R[f"GX{self.tag}"][...]
            for k in range(GX - 1):
                total = total + R[f"RX{self.tag}"][k]
            slots[gy] = total
            self.send(1, slots.at[gy], lambda number: slots.at[gy], [(0, k, 0) for k in range(1, GY)])

        def phase_z(self):
            self.wait()
            slots, out = R[f"RY{self.tag}"], R[f"RZ{self.tag}"]
            for i in range(self.comps):
                for y in range(GY):
                    out[gz, i, pl.ds(2 * y, 2), :] = slots[y, pl.ds(2 * i, 2), :]
            self.send(2, out.at[gz], lambda number: out.at[gz], [(0, 0, k) for k in range(1, GZ)])

        def finish(self, store):
            self.wait()
            out = R[f"RZ{self.tag}"]
            for i in range(self.comps):
                for z in range(GZ):
                    value = out[z, i]
                    left = lanes_of(value.shape) < 64
                    store(i, 2 * z, jnp.where(left, value, 0.0))
                    store(i, 2 * z + 1, jnp.where(left, roll(value, 64), 0.0))

    def own_tile(values, comps, total_rows):
        T = R["tile"]
        T[...] = jnp.zeros(T.shape, F32)
        for i in range(comps):
            low = values[(2 * i) * 8 : (2 * i) * 8 + 8]
            high = values[(2 * i + 1) * 8 : (2 * i + 1) * 8 + 8]
            T[pl.ds(2 * i, 2), :] = (low + roll(high, 64))[0:2]
        return roll(T[pl.ds(0, total_rows), :], 16 * gx)

    L0, L1, L2, L3, L4 = levels
    block2, block3 = Level(2, 4, 4, 32, True), Level(3, 2, 2, 16, False)

    def fill(z, carry):
        weight = R["tissue"][z].astype(F32)
        for comp in range(3):
            R["K0"][comp, z + 1, pl.ds(RO, L0.rows), :] = R["conduct"][comp, z] * weight
            R["K0"][3 + comp, z + 1, pl.ds(RO, L0.rows), :] = R["cross"][comp, z] * weight
        return carry

    lax.fori_loop(0, L0.nz, fill, 0, unroll=4)
    pl.semaphore_wait(barrier, len(unique))
    faces0 = start_faces(L0)

    R["stage"][...] = jnp.zeros(R["stage"].shape, F32)

    def tensor_rows(l, offset):
        return lambda i, z, dy, n: R[f"K{l}"][i, z + 1, pl.ds(offset + dy, n, stride=2), :]

    coarsen_rows(L0, L1, tensor_rows(0, RO), 6)
    values = coarsen_lanes(L0, 6 * L1.nz * L1.rows)
    for i in range(6):
        for z in range(L1.nz):
            start = (i * L1.nz + z) * L1.rows
            R["K1"][i, z + 1, pl.ds(RO, L1.rows), :] = values[start : start + L1.rows]
    faces1 = start_faces(L1)
    coarsen_rows(L1, block2, tensor_rows(1, RO), 6)
    values = coarsen_lanes(L1, 6 * block2.nz * block2.rows)

    def block2_tile(ref, comps, values):
        for i in range(comps):
            total = None
            for z in range(4):
                start = (i * 4 + z) * 8
                piece = roll(values[start : start + 8], 32 * z)
                total = piece if total is None else total + piece
            ref[pl.ds(4 * i, 4), :] = total[0:4]

    R["TAf"][...] = jnp.zeros(R["TAf"].shape, F32)
    R["TAp"][...] = jnp.zeros(R["TAp"].shape, F32)
    block2_tile(R["TAk"], 6, values)
    around_k = start_around("k")
    for i in range(6):
        for z in range(4):
            start = (i * 4 + z) * 8
            R["KB2"][i, z] = values[start : start + 8]
    coarsen_rows(block2, block3, lambda i, z, dy, n: R["KB2"][i, z, pl.ds(dy, n, stride=2), :], 6)
    gather_k = Gather("k", 6)
    gather_k.phase_x(own_tile(coarsen_lanes(block2, 6 * 2 * 8), 6, 16))

    for level in (L2, L3, L4):
        for name in ("K", "V"):
            ref = R[f"{name}{level.index}"]
            for i in range(ref.shape[0]):
                ref[i] = jnp.zeros(ref.shape[1:], F32)
    R["load"][...] = jnp.zeros(R["load"].shape, F32)

    zl = R["src_z"][...] - gz * L0.nz
    yl = R["src_y"][...] - gy * L0.ny
    xl = R["src_x"][...] - gx * L0.nx
    here = (zl >= 0) & (zl < L0.nz) & (yl >= 0) & (yl < L0.ny)
    R["key"][0:1, :] = jnp.where(here, zl * L0.ny + yl, -1)
    R["key"][1:2, :] = xl
    R["counts"][...] = jnp.zeros(R["counts"].shape, F32)
    chunk = 256

    def scatter(i, carry):
        start = pl.multiple_of(i * chunk, chunk)
        key = R["key"][0:1, pl.ds(start, chunk)]
        key_x = R["key"][1:2, pl.ds(start, chunk)]
        left = jnp.where(rows_of((L0.nz * L0.ny, chunk)) == key, 1.0, 0.0).astype(jnp.bfloat16)
        right = jnp.where(rows_of((LANES, chunk)) == key_x, 1.0, 0.0).astype(jnp.bfloat16)
        R["counts"][...] += lax.dot_general(left, right, (((1,), (1,)), ((), ())), preferred_element_type=F32)
        return carry

    lax.fori_loop(0, sources // chunk, scatter, 0, unroll=2)

    finish_faces(L0, faces0)
    coefficients(L0)

    def load0(z):
        return stim_height * R["counts"][pl.ds(pl.multiple_of(z * L0.ny, 8), L0.rows), :]

    def first_sweep(level, load):
        l = level.index

        def step(z, carry):
            value = load(z) * R[f"D{l}"][0, z]
            R[f"G{l}"][z] = value
            R[f"V{l}"][0, z + 1, pl.ds(RO, level.rows), :] = value
            return carry

        lax.fori_loop(0, level.nz, step, 0, unroll=min(level.nz, 8))

    def residual(level, slot, halo=True, first=0, last=None):
        l = level.index
        store = R[f"XR{l}"]

        def emit(z, value, delta):
            store[z, pl.ds(RO, level.rows), :] = delta * R[f"D{l}"][1, z]

        sweep(level, slot, emit, halo, first, last)

    def restricted(level, lower, z0=0, y0=0, x0=0):
        def get(i, z, dy, n):
            return R[f"XR{level.index}"][z + z0, pl.ds(RO + y0 + dy, n, stride=2), :]

        coarsen_rows(level, lower, get, 1)
        return coarsen_lanes(level, (level.nz // 2) * lower.rows, x0)

    def during_01():
        gather_k.phase_y()
        finish_faces(L1, faces1)
        coefficients(L1)

    def during_02():
        gather_k.phase_z()

    def during_10():
        def store(i, z, row, value):
            R["K2"][i, z + 1, pl.ds(RO + row, 4), :] = value

        finish_around("k", around_k, 6, store)
        coefficients(L2)

    def coarse_setup():
        def store(i, z, value):
            R["K3"][i, z + 1, pl.ds(RO, L3.rows), :] = clean(L3, value)

        gather_k.finish(store)
        coefficients(L3)
        coarsen_rows(L3, L4, tensor_rows(3, RO), 6)
        height = L4.nz * L4.rows
        values = coarsen_lanes(L3, 6 * height)
        for i in range(6):
            for z in range(L4.nz):
                start = i * height + z * L4.rows
                R["K4"][i, z + 1, pl.ds(RO, L4.rows), :] = clean(L4, values[start : start + L4.rows])
        coefficients(L4)

    during = {(0, 0): during_01, (0, 1): during_02, (1, 0): during_10, (1, 1): coarse_setup}

    first_sweep(L0, load0)
    for level, lower in ((L0, L1), (L1, block2)):
        l = level.index
        exchange(level, 0, 0, during.get((l, 0)))
        sweep(level, 0, into(level, 1))
        exchange(level, 1, 1, during.get((l, 1)))
        residual(level, 1)
        values = restricted(level, lower)
        if l == 0:
            R["load"][pl.ds(0, lower.nz * lower.rows), :] = values
            first_sweep(lower, lambda z: R["load"][pl.ds(pl.multiple_of(z * lower.rows, 8), lower.rows), :])

    def store_region(i, z, row, value):
        R["load"][pl.ds(z * L2.rows + row, 4), :] = value

    block2_tile(R["TAf"], 1, values)
    R["load"][...] = jnp.zeros(R["load"].shape, F32)
    finish_around("f", start_around("f"), 1, store_region)
    first_sweep(L2, lambda z: R["load"][pl.ds(pl.multiple_of(z * L2.rows, 8), L2.rows), :])
    sweep(L2, 0, into(L2, 1), False, 3, 9)
    residual(L2, 1, False, 4, 8)
    values = restricted(block2, block3, 4, 4, 32)

    gather_f = Gather("f", 1)
    gather_f.phase_x(own_tile(values, 1, 8))
    tile_lane = lanes_of((8, LANES))
    total = jnp.zeros((8, LANES), F32)
    for z in range(4):
        piece = roll(R["V2"][1, 5 + z, pl.ds(RO + 4, 8), :], 32 * z - 32)
        total = jnp.where((tile_lane >= 32 * z) & (tile_lane < 32 * z + 32), piece, total)
    R["TAp"][0:4, :] = total[0:4]
    around_p = start_around("p")
    gather_f.phase_y()
    gather_f.phase_z()

    def store_load(i, z, value):
        R["load"][pl.ds(z * L3.rows, L3.rows), :] = value

    gather_f.finish(store_load)

    def load_of(level):
        return lambda z: clean(level, R["load"][pl.ds(pl.multiple_of(z * level.rows, 8), level.rows), :])

    first_sweep(L3, load_of(L3))
    sweep(L3, 0, into(L3, 1), False)
    residual(L3, 1, False)
    values = restricted(L3, L4)
    R["load"][pl.ds(0, L4.nz * L4.rows), :] = values
    first_sweep(L4, load_of(L4))
    for i in range(COARSE - 1):
        sweep(L4, i % 2, into(L4, (i + 1) % 2), False)
    last4 = (COARSE - 1) % 2

    def spread(level, nz_c, ny_c, nx_c, stride_c, get, base, halo):
        l = level.index
        M, PV = R["merge"], R["spread"]
        a, b = rows_of((LANES, LANES)), lanes_of((LANES, LANES))
        main = (a == b // 2) & (b < level.nx)
        edges = ((a == nx_c) & (b == level.right)) | ((a == LANES - 1) & (b == LANES - 1))
        wide = halo and level.nx == LANES
        if halo and not wide:
            main = main | edges
        height = (nz_c + 2) * stride_c
        stacked = jnp.concatenate([get(ze) for ze in range(nz_c + 2)], axis=0)
        M[0, pl.ds(0, height), :] = dot(stacked, jnp.where(main, 1.0, 0.0).astype(F32))
        if wide:
            M[1, pl.ds(0, height), :] = dot(stacked, jnp.where(edges, 1.0, 0.0).astype(F32))
        V = R[f"V{l}"]
        for layer in range(2 if wide else 1):
            for ze in range(nz_c + 2):
                value = M[layer, pl.ds(ze * stride_c + RO - 1, ny_c + 2), :]
                slabs = [zf for zf in (2 * ze - 1, 2 * ze) if 0 <= zf <= level.nz + 1]
                for phase in range(2):
                    PV[layer, ze, pl.ds(RO - 2 + phase, ny_c + 2, stride=2), :] = value
        for ze in range(nz_c + 2):
            for zf in (2 * ze - 1, 2 * ze):
                if 0 <= zf <= level.nz + 1:
                    size = level.stride
                    V[2, zf] = V[1, zf] + PV[0, ze, pl.ds(0, size), :]
                    if halo:
                        H = R[f"H{l}"]
                        H[2, zf] = H[1, zf] + PV[1 if wide else 0, ze, pl.ds(0, size), :]

    def coarse_slab(level, slot):
        V = R[f"V{level.index}"]

        def get(ze):
            value = V[slot, ze]
            if level.split:
                lane = lanes_of(value.shape)
                edge = (lane == level.right) | (lane == LANES - 1)
                value = jnp.where(edge, R[f"H{level.index}"][slot, ze], value)
            return value

        return get

    spread(L3, L4.nz, L4.ny, L4.nx, L4.stride, coarse_slab(L4, last4), 0, False)
    sweep(L3, 2, into(L3, 0), False)
    sweep(L3, 0, into(L3, 1), False)

    def store_pre(i, z, row, value):
        R["V2"][2, z + 1, pl.ds(RO + row, 4), :] = value

    finish_around("p", around_p, 1, store_pre)
    slabs = []
    count3 = L3.nz + 2
    for i in range(6):
        value = R["V3"][1, lax.rem(2 * gz + (count3 - 1 + i), count3)]
        value = roll(value, lax.rem(2 * L3.stride - RO + 2 - 2 * gy, L3.stride), axis=0)
        value = roll(value, lax.rem(LANES + 16 - 16 * gx, LANES))
        slabs.append(value[0:8])
    a, b = rows_of((LANES, LANES)), lanes_of((LANES, LANES))
    copied = dot(jnp.concatenate(slabs, axis=0), jnp.where((a == b // 2) & (b < L2.nx), 1.0, 0.0).astype(F32))
    for i in range(6):
        for phase in range(2):
            R["spread"][0, i, pl.ds(phase, 8, stride=2), :] = copied[8 * i : 8 * i + 8]
    for z in range(L2.nz):
        where_rows = pl.ds(RO, L2.rows)
        added = jnp.where(inside(L2, z) > 0.5, R["spread"][0, z // 2, pl.ds(0, L2.rows), :], 0.0)
        R["V2"][2, z + 1, where_rows, :] = R["V2"][2, z + 1, where_rows, :] + added
    sweep(L2, 2, into(L2, 3), False, 2, 10)
    sweep(L2, 3, into(L2, 0), False, 3, 9)

    def region_slab(ze):
        return roll(R["V2"][0, 4 + ze, pl.ds(4, 24), :], -32)

    spread(L1, 4, 4, 32, 24, region_slab, 0, True)
    sweep(L1, 2, into(L1, 3))
    exchange(L1, 3, 2)
    sweep(L1, 3, into(L1, 0))
    exchange(L1, 0, 3)
    spread(L0, L1.nz, L1.ny, L1.nx, L1.stride, coarse_slab(L1, 0), 0, True)
    sweep(L0, 2, into(L0, 3))
    exchange(L0, 3, 2)

    def emit_out(z, value, delta):
        R["out"][z] = value + delta

    sweep(L0, 3, emit_out)
    drain()


def solution(mesh):
    sizes = (mesh.shape["gx"], mesh.shape["gy"], mesh.shape["gz"])
    GX, GY, GZ = sizes

    def body(conduct, cross, tissue, src_z, src_y, src_x):
        nz, ny, nx = tissue.shape
        sources = src_z.shape[0]
        levels = [Level(l, nz >> l, ny >> l, nx >> l, True) for l in range(2)]
        levels.append(Level(2, 12, 12, 96, False, True))
        levels.append(Level(3, 2 * GZ, 2 * GY, 16 * GX, False))
        levels.append(Level(4, GZ, GY, 8 * GX, False))
        scratch = {}

        def vmem(name, *shape, dtype=F32):
            scratch[name] = pltpu.VMEM(shape, dtype)

        for level in levels:
            l, z, rows, stride, zrows = level.index, level.nz, level.rows, level.stride, level.zrows
            slots = 4 if l < 3 else 3
            vmem(f"K{l}", 6, z + 2, stride, LANES)
            vmem(f"C{l}", 18, z, rows, LANES)
            vmem(f"D{l}", 2, z, rows, LANES)
            vmem(f"G{l}", z, rows, LANES)
            vmem(f"V{l}", slots, z + 2, stride, LANES)
            vmem(f"XP{l}", z + 2, stride, LANES)
            vmem(f"XM{l}", z + 2, stride, LANES)
            vmem(f"XR{l}", z, stride, LANES)
            if level.split:
                vmem(f"H{l}", slots, z + 2, stride, LANES)
                vmem(f"KH{l}", 3, z, rows, LANES)
                vmem(f"YB{l}", 2, zrows, LANES)
                vmem(f"PB{l}", rows, LANES)
                vmem(f"ZB{l}", 2, rows, LANES)
                vmem(f"RZ{l}", 4, 2, rows, LANES)
                vmem(f"RY{l}", 4, 6, zrows, LANES)
                vmem(f"RP{l}", 4, 10, rows, LANES)
                vmem(f"KZ{l}", 2, 3, rows, LANES)
                vmem(f"KY{l}", 2, 3, zrows, LANES)
                vmem(f"KP{l}", 3, rows, LANES)
                vmem(f"RKZ{l}", 2, 3, rows, LANES)
                vmem(f"RKY{l}", 2, 3, zrows, LANES)
                vmem(f"RKP{l}", 2, 3, rows, LANES)
        for tag, height in (("k", 24), ("f", 8), ("p", 8)):
            vmem(f"TA{tag}", height, LANES)
            vmem(f"RA{tag}", len(AROUND), height, LANES)
        scratch["asend"] = pltpu.SemaphoreType.DMA((3, len(AROUND)))
        scratch["arecv"] = pltpu.SemaphoreType.DMA((3, len(AROUND)))
        vmem("KB2", 6, 4, 8, LANES)
        vmem("PX", levels[0].stride, LANES)
        vmem("stage", 6 * 8 * 8, LANES)
        vmem("tile", 16, LANES)
        vmem("key", 2, sources, dtype=jnp.int32)
        vmem("counts", nz * ny, LANES)
        vmem("load", max(levels[3].nz * levels[3].rows, 64), LANES)
        vmem("merge", 2, 10 * 32, LANES)
        vmem("spread", 2, 10, 48, LANES)
        for tag, comps, height in (("k", 6, 16), ("f", 1, 8)):
            vmem(f"GX{tag}", height, LANES)
            vmem(f"RX{tag}", GX - 1, height, LANES)
            vmem(f"RY{tag}", GY, height, LANES)
            vmem(f"RZ{tag}", GZ, comps, levels[3].rows, LANES)
            most = max(sizes) - 1
            scratch[f"gs{tag}"] = pltpu.SemaphoreType.DMA((3, most))
            scratch[f"gr{tag}"] = pltpu.SemaphoreType.DMA((3, most))
        scratch["send"] = pltpu.SemaphoreType.DMA((len(MESSAGES),))
        scratch["recv"] = pltpu.SemaphoreType.DMA((2, len(MESSAGES)))
        scratch["ksend"] = pltpu.SemaphoreType.DMA((2, len(FACES)))
        scratch["krecv"] = pltpu.SemaphoreType.DMA((2, len(FACES)))
        names = ["conduct", "cross", "tissue", "src_z", "src_y", "src_x", "out"] + list(scratch)
        row = lambda value: value.reshape(1, sources)
        return pl.pallas_call(
            functools.partial(kernel, names, levels, sizes, sources),
            out_shape=jax.ShapeDtypeStruct((nz, ny, nx), F32),
            in_specs=[pl.BlockSpec(memory_space=pltpu.VMEM)] * 6,
            out_specs=pl.BlockSpec(memory_space=pltpu.VMEM),
            scratch_shapes=list(scratch.values()),
            compiler_params=pltpu.CompilerParams(
                collective_id=0, has_side_effects=True, vmem_limit_bytes=60 * 1024 * 1024
            ),
        )(conduct, cross, tissue, row(src_z), row(src_y), row(src_x))

    placed = (P(None, "gz", "gy", "gx"), P(None, "gz", "gy", "gx"), P("gz", "gy", "gx"), P(), P(), P())
    return jax.shard_map(body, mesh=mesh, in_specs=placed, out_specs=P("gz", "gy", "gx"), check_vma=False)
```

```python
import functools

import jax
import jax.numpy as jnp
from jax import lax
from jax.experimental import pallas as pl
from jax.experimental.pallas import tpu as pltpu
from jax.sharding import PartitionSpec as P

tau_step = 4000.0
relax = 0.55
stim_height = 64000.0
COARSE = 12
RO = 8
LANES = 128
MESH = pl.DeviceIdType.MESH
F32 = jnp.float32
PAIRS = ((0, 1, 3), (0, 2, 4), (1, 2, 5))


class Level:
    def __init__(self, index, nz, ny, nx, split, margin=None):
        self.index, self.nz, self.ny, self.nx, self.split, self.margin = index, nz, ny, nx, split, margin
        self.rows = max(8, -(-ny // 8) * 8)
        self.zrows = max(8, -(-nz // 8) * 8)
        self.stride = RO + self.rows + 8
        self.tau = tau_step / 4.0**index
        self.right = nx % LANES


def lanes_of(shape):
    return lax.broadcasted_iota(jnp.int32, shape, len(shape) - 1)


def rows_of(shape):
    return lax.broadcasted_iota(jnp.int32, shape, len(shape) - 2)


def roll(value, shift, axis=None):
    axis = value.ndim - 1 if axis is None else axis
    if isinstance(shift, int):
        shift = shift % value.shape[axis]
        if shift == 0:
            return value
    return pltpu.roll(value, shift, axis)


def dot(a, b):
    return lax.dot_general(
        a, b, (((1,), (0,)), ((), ())), precision=lax.Precision.HIGHEST, preferred_element_type=F32
    )


MESSAGES = [("z", 1, (0, 0, -1)), ("z", 0, (0, 0, 1))]
for _face, _oy in ((0, -1), (1, 1)):
    for _part, _oz in ((0, 0), (1, -1), (2, 1)):
        MESSAGES.append(("y", 3 * _face + _part, (0, _oy, _oz)))
for _side, _ox in ((0, -1), (1, 1)):
    for _part, (_oy, _oz) in enumerate(((0, 0), (-1, 0), (1, 0), (0, -1), (0, 1))):
        MESSAGES.append(("p", 5 * _side + _part, (_ox, _oy, _oz)))
AROUND = [(dx, dy, dz) for dz in (-1, 0, 1) for dy in (-1, 0, 1) for dx in (-1, 0, 1) if (dx, dy, dz) != (0, 0, 0)]
FACES = [("z", 1, (0, 0, -1)), ("z", 0, (0, 0, 1)), ("y", 0, (0, -1, 0)), ("y", 1, (0, 1, 0)), ("p", 0, (-1, 0, 0)), ("p", 1, (1, 0, 0))]


def kernel(names, levels, sizes, sources, *refs):
    R = dict(zip(names, refs))
    GX, GY, GZ = sizes
    gx, gy, gz = lax.axis_index("gx"), lax.axis_index("gy"), lax.axis_index("gz")

    def device(ox, oy, oz):
        return (lax.rem(gx + (ox + GX), GX), lax.rem(gy + (oy + GY), GY), lax.rem(gz + (oz + GZ), GZ))

    peers = list(AROUND)
    peers += [(k, 0, 0) for k in range(1, GX)] + [(0, k, 0) for k in range(1, GY)] + [(0, 0, k) for k in range(1, GZ)]
    seen, unique = set(), []
    for ox, oy, oz in peers:
        key = (ox % GX, oy % GY, oz % GZ)
        if key not in seen:
            seen.add(key)
            unique.append(key)
    barrier = pltpu.get_barrier_semaphore()
    for ox, oy, oz in unique:
        pl.semaphore_signal(barrier, inc=1, device_id=device(ox, oy, oz), device_id_type=MESH)

    def flag(condition):
        return jnp.where(condition, 0.0, 1.0).astype(F32)

    in_xp, in_xm = flag(gx == GX - 1), flag(gx == 0)
    in_yp, in_ym = flag(gy == GY - 1), flag(gy == 0)
    in_zp, in_zm = flag(gz == GZ - 1), flag(gz == 0)

    def clean(level, value):
        return value if level.ny == level.rows else jnp.where(rows_of(value.shape) < level.ny, value, 0.0)

    def bounds(level):
        if level.split:
            return in_zp, in_zm, in_yp, in_ym, in_xp, in_xm
        return (jnp.zeros((), F32),) * 6

    def inside(level, z):
        mz, my, mx = level.margin
        shape = (level.rows, LANES)
        lane, row = lanes_of(shape), rows_of(shape)
        mask_z = jnp.where(z < mz, in_zm, jnp.where(z >= level.nz - mz, in_zp, 1.0))
        mask_y = jnp.where(row < my, in_ym, jnp.where(row >= level.ny - my, in_yp, 1.0))
        mask_x = jnp.where(lane < mx, in_xm, jnp.where(lane >= level.nx - mx, in_xp, 1.0))
        return jnp.where((row < level.ny) & (lane < level.nx), mask_z * mask_y * mask_x, 0.0)

    def valid(dx, dy, dz):
        factor = None
        for d, plus, minus in ((dx, in_xp, in_xm), (dy, in_yp, in_ym), (dz, in_zp, in_zm)):
            if d:
                one = plus if d > 0 else minus
                factor = one if factor is None else factor * one
        return factor

    def times(value, factor):
        return value if factor is None else value * factor

    def pack_x(level, get):
        shape = (level.rows, LANES)
        lane = lanes_of(shape)
        out = jnp.zeros(shape, F32)
        for z in range(level.nz):
            value = get(z)
            first = (level.right + 2 * (z + 1)) % LANES
            last = (2 * (z + 1) + LANES - 1) % LANES
            a = roll(value, first)
            b = roll(value, last - (level.nx - 1))
            out = jnp.where(lane == first, a, jnp.where(lane == last, b, out))
        return out

    def coarsen_rows(level, lower, get, count):
        stage = R["stage"]
        half = level.ny // 2
        for i in range(count):
            for z in range(level.nz // 2):
                total = None
                for dz in range(2):
                    for dy in range(2):
                        piece = get(i, 2 * z + dz, dy, half)
                        total = piece if total is None else total + piece
                stage[pl.ds((i * (level.nz // 2) + z) * lower.rows, half), :] = total

    def coarsen_lanes(level, rows, first=0):
        a, b = rows_of((LANES, LANES)), lanes_of((LANES, LANES))
        matrix = jnp.where((b == (a - first) // 2) & (a >= first) & (b < level.nx // 2), 0.125, 0.0).astype(F32)
        return dot(R["stage"][pl.ds(0, rows), :], matrix)

    def coefficients(level):
        l = level.index
        K, C, D = R[f"K{l}"], R[f"C{l}"], R[f"D{l}"]
        n, rows = level.nz, level.rows
        shape = (rows, LANES)
        lane, row = lanes_of(shape), rows_of(shape)
        zp, zm, yp, ym, xp, xm = bounds(level)
        keep_yp = jnp.where(row == level.ny - 1, yp, 1.0)
        keep_ym = jnp.where(row == 0, ym, 1.0)
        keep_xp = jnp.where(lane == level.nx - 1, xp, 1.0)
        keep_xm = jnp.where(lane == 0, xm, 1.0)

        def step(z, carry):
            ze = z + 1

            def at(comp, dz=0, dy=0):
                return K[comp, ze + dz, pl.ds(RO + dy, rows), :]

            def along(comp, which, sign):
                value = at(comp)
                if level.split:
                    halo = R[f"KH{l}"][which, z]
                    value = jnp.where(lane == (level.right if sign > 0 else LANES - 1), halo, value)
                return roll(value, LANES - 1 if sign > 0 else 1)

            keep_zp = jnp.where(z == n - 1, zp, 1.0)
            keep_zm = jnp.where(z == 0, zm, 1.0)
            keep = ((keep_zp, keep_zm), (keep_yp, keep_ym), (keep_xp, keep_xm))
            weights = (
                (0.5 * (at(0) + at(0, 1)), 0.5 * (at(0) + at(0, -1))),
                (0.5 * (at(1) + at(1, 0, 1)), 0.5 * (at(1) + at(1, 0, -1))),
                (0.5 * (at(2) + along(2, 0, 1)), 0.5 * (at(2) + along(2, 0, -1))),
            )
            total = weights[0][0] + weights[0][1] + weights[1][0] + weights[1][1] + weights[2][0] + weights[2][1]
            diagonal = 1.0 + level.tau * total
            inverse = relax / diagonal
            scale = level.tau * inverse
            if level.margin:
                scale = scale * inside(level, z)
            D[0, z] = inverse
            D[1, z] = diagonal * (1.0 / relax)
            for a in range(3):
                for s in range(2):
                    C[2 * a + s, z] = scale * weights[a][s] * keep[a][s]
            quarter = 0.25 * scale

            def shifted(comp, axis, sign):
                if axis == 0:
                    return at(comp, sign)
                if axis == 1:
                    return at(comp, 0, sign)
                return along(comp, 1 if comp == 4 else 2, sign)

            for number, (a, b, comp) in enumerate(PAIRS):
                ka = [shifted(comp, a, 1), shifted(comp, a, -1)]
                kb = [shifted(comp, b, 1), shifted(comp, b, -1)]
                for sa in range(2):
                    for sb in range(2):
                        value = quarter * (ka[sa] + kb[sb]) * keep[a][sa] * keep[b][sb]
                        C[6 + 4 * number + 2 * sa + sb, z] = value if sa == sb else -value
            return carry

        lax.fori_loop(0, n, step, 0, unroll=min(n, 4))

    def sweep(level, source, emit, halo=True, first=0, last=None):
        l = level.index
        V, C, G, XP, XM = R[f"V{l}"], R[f"C{l}"], R[f"G{l}"], R[f"XP{l}"], R[f"XM{l}"]
        rows = level.rows

        def shift(ze, carry):
            value = V[source, ze]
            up = down = value
            if halo:
                lane = lanes_of(value.shape)
                edge = R[f"H{l}"][source, ze]
                up = jnp.where(lane == level.right, edge, value)
                down = jnp.where(lane == LANES - 1, edge, value)
            XP[ze] = roll(up, LANES - 1)
            XM[ze] = roll(down, 1)
            return carry

        last = level.nz if last is None else last
        lax.fori_loop(first, last + 2, shift, 0, unroll=last + 2 - first)

        def step(z, carry):
            ze = z + 1

            def at(dz, dy, dx):
                where_rows = pl.ds(RO + dy, rows)
                if dx == 0:
                    return V[source, ze + dz, where_rows, :]
                return (XP if dx > 0 else XM)[ze + dz, where_rows, :]

            center = at(0, 0, 0)
            parts = [G[z] - relax * center, None, None]
            offsets = [(1, 0, 0), (-1, 0, 0), (0, 1, 0), (0, -1, 0), (0, 0, 1), (0, 0, -1)]
            for a, b, _ in PAIRS:
                for sa in (1, -1):
                    for sb in (1, -1):
                        offset = [0, 0, 0]
                        offset[a], offset[b] = sa, sb
                        offsets.append(tuple(offset))
            for number, offset in enumerate(offsets):
                term = C[number, z] * at(*offset)
                slot = number % 3
                parts[slot] = term if parts[slot] is None else parts[slot] + term
            emit(z, center, (parts[0] + parts[1]) + parts[2])
            return carry

        lax.fori_loop(first, last, step, 0, unroll=min(last - first, 8))

    def into(level, slot):
        V = R[f"V{level.index}"]

        def emit(z, value, delta):
            V[slot, z + 1, pl.ds(RO, level.rows), :] = value + delta

        return emit

    pending = []
    count = [0]

    def drain():
        for copy in pending:
            copy.wait_send()
        pending.clear()

    def exchange(level, slot, step, during=None):
        l = level.index
        V, H, YB, PB, X = R[f"V{l}"], R[f"H{l}"], R[f"YB{l}"], R[f"PB{l}"], R["PX"]
        ZB = R[f"ZB{l}"]
        RZ, RY, RP = R[f"RZ{l}"], R[f"RY{l}"], R[f"RP{l}"]
        nz, ny, rows, zrows = level.nz, level.ny, level.rows, level.zrows
        drain()
        for z in range(nz):
            YB[0, pl.ds(z, 1), :] = V[slot, z + 1, pl.ds(RO, 1), :]
            YB[1, pl.ds(z, 1), :] = V[slot, z + 1, pl.ds(RO + ny - 1, 1), :]
        ZB[0] = V[slot, 1, pl.ds(RO, rows), :]
        ZB[1] = V[slot, nz, pl.ds(RO, rows), :]
        PB[...] = pack_x(level, lambda z: V[slot, z + 1, pl.ds(RO, rows), :])
        parity = count[0] % 2
        count[0] += 1
        copies = []
        ylow, zlow = rows - 8, zrows - 8
        for number, (kind, where, (ox, oy, oz)) in enumerate(MESSAGES):
            if kind == "z":
                src, dst = ZB.at[0 if where else 1], RZ.at[step, where]
            elif kind == "y":
                face = where // 3
                if where % 3 == 0:
                    src, dst = YB.at[face], RY.at[step, where]
                else:
                    low = 0 if where % 3 == 1 else zlow
                    src, dst = YB.at[face, pl.ds(low, 8)], RY.at[step, where, pl.ds(0, 8)]
            else:
                part = where % 5
                if part in (1, 2):
                    low = 0 if part == 1 else ylow
                    src, dst = PB.at[pl.ds(low, 8)], RP.at[step, where, pl.ds(0, 8)]
                else:
                    src, dst = PB, RP.at[step, where]
            copy = pltpu.make_async_remote_copy(
                src_ref=src, dst_ref=dst, send_sem=R["send"].at[number], recv_sem=R["recv"].at[parity, number],
                device_id=device(ox, oy, oz), device_id_type=MESH,
            )
            copy.start()
            copies.append(copy)
        pending.extend(copies)
        if during is not None:
            during()
        for copy in copies:
            copy.wait_recv()
        V[slot, nz + 1, pl.ds(RO, rows), :] = RZ[step, 1]
        V[slot, 0, pl.ds(RO, rows), :] = RZ[step, 0]
        for face in range(2):
            place = RO + ny if face == 0 else RO - 1
            for z in range(nz):
                V[slot, z + 1, pl.ds(place, 1), :] = RY[step, 3 * face, pl.ds(z, 1), :]
            V[slot, nz + 1, pl.ds(place, 1), :] = RY[step, 3 * face + 1, pl.ds(0, 1), :]
            V[slot, 0, pl.ds(place, 1), :] = RY[step, 3 * face + 2, pl.ds(nz - 1 - zlow, 1), :]

        def merged(part, size):
            even = lanes_of((size, LANES)) % 2 == 0
            return jnp.where(even, RP[step, part, pl.ds(0, size), :], RP[step, 5 + part, pl.ds(0, size), :])

        lane = lanes_of((rows, LANES))
        middle = merged(0, rows)
        above = roll(merged(3, rows), 2 * nz)
        below = roll(merged(4, rows), -2 * nz)

        def slab_lanes(ze):
            return (lane == (level.right + 2 * ze) % LANES) | (lane == (2 * ze + LANES - 1) % LANES)

        middle = jnp.where(slab_lanes(nz + 1), above, jnp.where(slab_lanes(0), below, middle))
        size = level.stride
        X[pl.ds(RO, rows), :] = middle
        X[pl.ds(RO + ny, 1), :] = merged(1, 8)[0:1]
        X[pl.ds(RO - 1, 1), :] = merged(2, 8)[ny - 1 - ylow : ny - ylow]
        whole = X[pl.ds(0, size), :]
        for ze in range(nz + 2):
            H[slot, ze] = roll(whole, -2 * ze)

    def start_faces(level):
        l = level.index
        K, KY, KP, KZ = R[f"K{l}"], R[f"KY{l}"], R[f"KP{l}"], R[f"KZ{l}"]
        nz, ny, rows = level.nz, level.ny, level.rows
        for i, comp in enumerate((0, 3, 4)):
            KZ[0, i] = K[comp, 1, pl.ds(RO, rows), :]
            KZ[1, i] = K[comp, nz, pl.ds(RO, rows), :]
        for i, comp in enumerate((1, 3, 5)):
            for z in range(nz):
                KY[0, i, pl.ds(z, 1), :] = K[comp, z + 1, pl.ds(RO, 1), :]
                KY[1, i, pl.ds(z, 1), :] = K[comp, z + 1, pl.ds(RO + ny - 1, 1), :]
        for i, comp in enumerate((2, 4, 5)):
            KP[i] = pack_x(level, lambda z: K[comp, z + 1, pl.ds(RO, rows), :])
        copies = []
        for number, (kind, where, (ox, oy, oz)) in enumerate(FACES):
            if kind == "z":
                src, dst = KZ.at[0 if where else 1], R[f"RKZ{l}"].at[where]
            elif kind == "y":
                src, dst = KY.at[where], R[f"RKY{l}"].at[where]
            else:
                src, dst = KP, R[f"RKP{l}"].at[where]
            copy = pltpu.make_async_remote_copy(
                src_ref=src, dst_ref=dst, send_sem=R["ksend"].at[l, number], recv_sem=R["krecv"].at[l, number],
                device_id=device(ox, oy, oz), device_id_type=MESH,
            )
            copy.start()
            copies.append(copy)
        return copies

    def finish_faces(level, copies):
        l = level.index
        K, KH = R[f"K{l}"], R[f"KH{l}"]
        nz, ny, rows = level.nz, level.ny, level.rows
        for copy in copies:
            copy.wait()
        for i, comp in enumerate((0, 3, 4)):
            K[comp, nz + 1, pl.ds(RO, rows), :] = R[f"RKZ{l}"][1, i] * in_zp
            K[comp, 0, pl.ds(RO, rows), :] = R[f"RKZ{l}"][0, i] * in_zm
        for i, comp in enumerate((1, 3, 5)):
            for z in range(nz):
                K[comp, z + 1, pl.ds(RO + ny, 1), :] = R[f"RKY{l}"][0, i, pl.ds(z, 1), :] * in_yp
                K[comp, z + 1, pl.ds(RO - 1, 1), :] = R[f"RKY{l}"][1, i, pl.ds(z, 1), :] * in_ym
        even = lanes_of((rows, LANES)) % 2 == 0
        for i in range(3):
            both = jnp.where(even, R[f"RKP{l}"][0, i] * in_xp, R[f"RKP{l}"][1, i] * in_xm)
            for z in range(nz):
                KH[i, z] = roll(both, -2 * (z + 1))

    def start_around(tag):
        tag_index = "kfp".index(tag)
        copies = []
        for number, (dx, dy, dz) in enumerate(AROUND):
            copy = pltpu.make_async_remote_copy(
                src_ref=R[f"TA{tag}"], dst_ref=R[f"RA{tag}"].at[number], send_sem=R["asend"].at[tag_index, number],
                recv_sem=R["arecv"].at[tag_index, number], device_id=device(-dx, -dy, -dz), device_id_type=MESH,
            )
            copy.start()
            copies.append(copy)
        return copies

    def finish_around(tag, copies, comps, store):
        for copy in copies:
            copy.wait()
        tile = R[f"TA{tag}"]
        lane = lanes_of(tile.shape)
        for dz in (-1, 0, 1):
            for dy in (-1, 0, 1):
                row_tiles = []
                for dx in (-1, 0, 1):
                    if (dx, dy, dz) == (0, 0, 0):
                        row_tiles.append(tile[...])
                        continue
                    value = R[f"RA{tag}"][AROUND.index((dx, dy, dz))]
                    row_tiles.append(times(value, valid(dx, dy, dz)))
                for z in range(4):
                    low, mid, high = (roll(row_tiles[i], 32 * i - 32 * z) for i in range(3))
                    value = jnp.where(lane < 32, low, jnp.where(lane < 64, mid, jnp.where(lane < 96, high, 0.0)))
                    for comp in range(comps):
                        store(comp, 4 * (dz + 1) + z, 4 * (dy + 1), value[4 * comp : 4 * comp + 4])

    def start_wide(tag, comps, get):
        tag_index = "kfp".index(tag)
        A, B, S, S2 = (R[f"{name}{tag}"] for name in ("WA", "WB", "WS", "WT"))
        shape = (8, LANES)
        lane = lanes_of(shape)
        for c in range(comps):
            slabs = [get(c, z) for z in range(8)]
            strip = jnp.zeros(shape, F32)
            for z in range(8):
                low, high = 68 + 8 * z, 8 * z
                strip = jnp.where((lane >= low) & (lane < low + 4), roll(slabs[z], low), strip)
                strip = jnp.where((lane >= high) & (lane < high + 4), roll(slabs[z], high - 60), strip)
            S[c] = strip
            for h in range(2):
                S2[h, c // 2, pl.ds(4 * (c % 2), 4), :] = strip[4 * h : 4 * h + 4]
            for p in range(4):
                pair = slabs[2 * p] + roll(slabs[2 * p + 1], 64)
                A[p, c] = pair
                for h in range(2):
                    B[h, p // 2, c, pl.ds(4 * (p % 2), 4), :] = pair[4 * h : 4 * h + 4]
        copies = []
        for number, (dx, dy, dz) in enumerate(AROUND):
            t, h = int(dz < 0), int(dy < 0)
            iz, iy, ix = int(dz > 0), int(dy > 0), int(dx > 0)
            if dx == 0 and dy == 0:
                src, dst = A.at[pl.ds(2 * t, 2)], R[f"WRA{tag}"].at[iz]
            elif dx == 0 and dz == 0:
                src, dst = B.at[h], R[f"WRB{tag}"].at[iy]
            elif dx == 0:
                src, dst = B.at[h, t], R[f"WRC{tag}"].at[2 * iy + iz]
            elif dy == 0:
                src, dst = S, R[f"WRS{tag}"].at[3 * ix + dz + 1]
            else:
                src, dst = S2.at[h], R[f"WRT{tag}"].at[3 * (2 * ix + iy) + dz + 1]
            copy = pltpu.make_async_remote_copy(
                src_ref=src, dst_ref=dst, send_sem=R["wsend"].at[tag_index, number],
                recv_sem=R["wrecv"].at[tag_index, number], device_id=device(-dx, -dy, -dz), device_id_type=MESH,
            )
            copy.start()
            copies.append(copy)
        return copies

    def finish_wide(tag, copies, comps, load, store):
        for copy in copies:
            copy.wait()
        A = R[f"WA{tag}"]
        MS = R["strips"]
        lane8, lane16 = lanes_of((8, LANES)), lanes_of((16, LANES))
        edge = (lane16 < 4) | ((lane16 >= 68) & (lane16 < 72))
        for c in range(comps):
            for dz in (-1, 0, 1):
                iz = int(dz > 0)
                zs = range(4, 8) if dz < 0 else range(0, 8) if dz == 0 else range(0, 4)
                base = {-1: -4, 0: 4, 1: 12}[dz]
                for z in zs:
                    tile = A[z // 2, c] if dz == 0 else R[f"WRA{tag}"][iz, z // 2 - (2 if dz < 0 else 0), c]
                    store(c, z + base, 4, roll(times(tile, valid(0, 0, dz)), 4 - 64 * (z % 2)))
                for dy in (-1, 1):
                    iy = int(dy > 0)
                    for z in zs:
                        tile = R[f"WRB{tag}"][iy, z // 4, c] if dz == 0 else R[f"WRC{tag}"][2 * iy + iz, c]
                        part = 4 * ((z % 4) // 2)
                        piece = roll(times(tile, valid(0, dy, dz)), 4 - 64 * (z % 2))
                        store(c, z + base, 0 if dy < 0 else 12, piece[part : part + 4])
                for dy in (-1, 0, 1):
                    iy = int(dy > 0)
                    sides = []
                    for ix, dx in enumerate((-1, 1)):
                        if dy == 0:
                            tile = R[f"WRS{tag}"][3 * ix + dz + 1, c]
                        else:
                            tile = R[f"WRT{tag}"][3 * (2 * ix + iy) + dz + 1, c // 2]
                        sides.append(times(tile, valid(dx, dy, dz)))
                    both = jnp.where(lane8 < 64, sides[0], sides[1])
                    if dy == 0:
                        MS[dz + 1, pl.ds(4, 8), :] = both
                    else:
                        MS[dz + 1, pl.ds(0 if dy < 0 else 12, 4), :] = both[4 * (c % 2) : 4 * (c % 2) + 4]
                strip = MS[dz + 1]
                for z in zs:
                    store(c, z + base, 0, jnp.where(edge, roll(strip, -8 * z), load(c, z + base)))

    class Gather:
        def __init__(self, tag, comps):
            self.tag, self.comps = tag, comps
            self.copies = []

        def send(self, phase, src, dst_of, targets):
            self.copies = []
            for number, offset in enumerate(targets):
                copy = pltpu.make_async_remote_copy(
                    src_ref=src, dst_ref=dst_of(number), send_sem=R[f"gs{self.tag}"].at[phase, number],
                    recv_sem=R[f"gr{self.tag}"].at[phase, number], device_id=device(*offset), device_id_type=MESH,
                )
                copy.start()
                self.copies.append(copy)

        def wait(self):
            for copy in self.copies:
                copy.wait()

        def phase_x(self, tiles):
            own, received = R[f"GX{self.tag}"], R[f"RX{self.tag}"]
            own[...] = tiles
            self.send(0, own, lambda number: received.at[number], [(k, 0, 0) for k in range(1, GX)])

        def phase_y(self):
            self.wait()
            slots = R[f"RY{self.tag}"]
            total = R[f"GX{self.tag}"][...]
            for k in range(GX - 1):
                total = total + R[f"RX{self.tag}"][k]
            slots[gy] = total
            self.send(1, slots.at[gy], lambda number: slots.at[gy], [(0, k, 0) for k in range(1, GY)])

        def phase_z(self):
            self.wait()
            slots, out = R[f"RY{self.tag}"], R[f"RZ{self.tag}"]
            for i in range(self.comps):
                for y in range(GY):
                    out[gz, i, pl.ds(2 * y, 2), :] = slots[y, pl.ds(2 * i, 2), :]
            self.send(2, out.at[gz], lambda number: out.at[gz], [(0, 0, k) for k in range(1, GZ)])

        def finish(self, store):
            self.wait()
            out = R[f"RZ{self.tag}"]
            for i in range(self.comps):
                for z in range(GZ):
                    value = out[z, i]
                    left = lanes_of(value.shape) < 64
                    store(i, 2 * z, jnp.where(left, value, 0.0))
                    store(i, 2 * z + 1, jnp.where(left, roll(value, 64), 0.0))

    def own_tile(values, comps, total_rows):
        T = R["tile"]
        T[...] = jnp.zeros(T.shape, F32)
        for i in range(comps):
            low = values[(2 * i) * 8 : (2 * i) * 8 + 8]
            high = values[(2 * i + 1) * 8 : (2 * i + 1) * 8 + 8]
            T[pl.ds(2 * i, 2), :] = (low + roll(high, 64))[0:2]
        return roll(T[pl.ds(0, total_rows), :], 16 * gx)

    L0, L1, L2, L3, L4 = levels
    block1, block2, block3 = Level(1, 8, 8, 64, True), Level(2, 4, 4, 32, True), Level(3, 2, 2, 16, False)

    def fill(z, carry):
        weight = R["tissue"][z].astype(F32)
        for comp in range(3):
            R["K0"][comp, z + 1, pl.ds(RO, L0.rows), :] = R["conduct"][comp, z] * weight
            R["K0"][3 + comp, z + 1, pl.ds(RO, L0.rows), :] = R["cross"][comp, z] * weight
        return carry

    lax.fori_loop(0, L0.nz, fill, 0, unroll=4)
    pl.semaphore_wait(barrier, len(unique))
    faces0 = start_faces(L0)

    R["stage"][...] = jnp.zeros(R["stage"].shape, F32)

    def tensor_rows(l, offset):
        return lambda i, z, dy, n: R[f"K{l}"][i, z + 1, pl.ds(offset + dy, n, stride=2), :]

    coarsen_rows(L0, block1, tensor_rows(0, RO), 6)
    values = coarsen_lanes(L0, 6 * 8 * 8)

    def slab_of(values):
        return lambda c, z: values[(c * 8 + z) * 8 : (c * 8 + z) * 8 + 8]

    wide_k = start_wide("k", 6, slab_of(values))
    for i in range(6):
        for z in range(8):
            R["KB1"][i, z] = values[(i * 8 + z) * 8 : (i * 8 + z) * 8 + 8]
    coarsen_rows(block1, block2, lambda i, z, dy, n: R["KB1"][i, z, pl.ds(dy, n, stride=2), :], 6)
    values = coarsen_lanes(block1, 6 * 4 * 8)

    def block2_tile(ref, comps, values):
        for i in range(comps):
            total = None
            for z in range(4):
                start = (i * 4 + z) * 8
                piece = roll(values[start : start + 8], 32 * z)
                total = piece if total is None else total + piece
            ref[pl.ds(4 * i, 4), :] = total[0:4]

    R["TAf"][...] = jnp.zeros(R["TAf"].shape, F32)
    R["TAp"][...] = jnp.zeros(R["TAp"].shape, F32)
    block2_tile(R["TAk"], 6, values)
    around_k = start_around("k")
    for i in range(6):
        for z in range(4):
            start = (i * 4 + z) * 8
            R["KB2"][i, z] = values[start : start + 8]
    coarsen_rows(block2, block3, lambda i, z, dy, n: R["KB2"][i, z, pl.ds(dy, n, stride=2), :], 6)
    gather_k = Gather("k", 6)
    gather_k.phase_x(own_tile(coarsen_lanes(block2, 6 * 2 * 8), 6, 16))

    for level in (L1, L2, L3, L4):
        for name in ("K", "V"):
            ref = R[f"{name}{level.index}"]
            for i in range(ref.shape[0]):
                ref[i] = jnp.zeros(ref.shape[1:], F32)
    R["load"][...] = jnp.zeros(R["load"].shape, F32)

    zl = R["src_z"][...] - gz * L0.nz
    yl = R["src_y"][...] - gy * L0.ny
    xl = R["src_x"][...] - gx * L0.nx
    here = (zl >= 0) & (zl < L0.nz) & (yl >= 0) & (yl < L0.ny)
    R["key"][0:1, :] = jnp.where(here, zl * L0.ny + yl, -1)
    R["key"][1:2, :] = xl
    R["counts"][...] = jnp.zeros(R["counts"].shape, F32)
    chunk = 256

    def scatter(i, carry):
        start = pl.multiple_of(i * chunk, chunk)
        key = R["key"][0:1, pl.ds(start, chunk)]
        key_x = R["key"][1:2, pl.ds(start, chunk)]
        left = jnp.where(rows_of((L0.nz * L0.ny, chunk)) == key, 1.0, 0.0).astype(jnp.bfloat16)
        right = jnp.where(rows_of((LANES, chunk)) == key_x, 1.0, 0.0).astype(jnp.bfloat16)
        R["counts"][...] += lax.dot_general(left, right, (((1,), (1,)), ((), ())), preferred_element_type=F32)
        return carry

    lax.fori_loop(0, sources // chunk, scatter, 0, unroll=2)

    finish_faces(L0, faces0)
    coefficients(L0)

    def load0(z):
        return stim_height * R["counts"][pl.ds(pl.multiple_of(z * L0.ny, 8), L0.rows), :]

    def first_sweep(level, load):
        l = level.index

        def step(z, carry):
            value = load(z) * R[f"D{l}"][0, z]
            R[f"G{l}"][z] = value
            R[f"V{l}"][0, z + 1, pl.ds(RO, level.rows), :] = value
            return carry

        lax.fori_loop(0, level.nz, step, 0, unroll=min(level.nz, 8))

    def residual(level, slot, halo=True, first=0, last=None):
        l = level.index
        store = R[f"XR{l}"]

        def emit(z, value, delta):
            store[z, pl.ds(RO, level.rows), :] = delta * R[f"D{l}"][1, z]

        sweep(level, slot, emit, halo, first, last)

    def restricted(level, lower, z0=0, y0=0, x0=0):
        def get(i, z, dy, n):
            return R[f"XR{level.index}"][z + z0, pl.ds(RO + y0 + dy, n, stride=2), :]

        coarsen_rows(level, lower, get, 1)
        return coarsen_lanes(level, (level.nz // 2) * lower.rows, x0)

    def tensor_region(l):
        def store(i, z, row, value):
            R[f"K{l}"][i, z + 1, pl.ds(RO + row, value.shape[0]), :] = value

        return store

    def iterate_region(l):
        def store(i, z, row, value):
            R[f"V{l}"][2, z + 1, pl.ds(RO + row, value.shape[0]), :] = value

        return store

    def load_region(level):
        def store(i, z, row, value):
            R["load"][pl.ds(z * level.rows + row, value.shape[0]), :] = value

        return store

    def during_01():
        gather_k.phase_y()

    def during_02():
        gather_k.phase_z()
        finish_wide("k", wide_k, 6, lambda i, z: R["K1"][i, z + 1, pl.ds(RO, 16), :], tensor_region(1))
        coefficients(L1)

    def during_10():
        finish_around("k", around_k, 6, tensor_region(2))
        coefficients(L2)

    def coarse_setup():
        def store(i, z, value):
            R["K3"][i, z + 1, pl.ds(RO, L3.rows), :] = clean(L3, value)

        gather_k.finish(store)
        coefficients(L3)
        coarsen_rows(L3, L4, tensor_rows(3, RO), 6)
        height = L4.nz * L4.rows
        values = coarsen_lanes(L3, 6 * height)
        for i in range(6):
            for z in range(L4.nz):
                start = i * height + z * L4.rows
                R["K4"][i, z + 1, pl.ds(RO, L4.rows), :] = clean(L4, values[start : start + L4.rows])
        coefficients(L4)

    def load_of(level):
        return lambda z: clean(level, R["load"][pl.ds(pl.multiple_of(z * level.rows, 8), level.rows), :])

    first_sweep(L0, load0)
    exchange(L0, 0, 0, during_01)
    sweep(L0, 0, into(L0, 1))
    exchange(L0, 1, 1, during_02)
    residual(L0, 1)
    values = restricted(L0, block1)

    wide_f = start_wide("f", 1, slab_of(values))
    during_10()
    finish_wide("f", wide_f, 1, lambda i, z: R["load"][pl.ds(16 * z, 16), :], load_region(L1))
    first_sweep(L1, load_of(L1))
    sweep(L1, 0, into(L1, 1), False, 3, 13)
    residual(L1, 1, False, 4, 12)
    values = restricted(block1, block2, 4, 4, 4)

    block2_tile(R["TAf"], 1, values)
    around_f = start_around("f")
    lane8 = lanes_of((8, LANES))

    def pre_slab(c, z):
        return jnp.where(lane8 < 64, roll(R["V1"][1, 5 + z, pl.ds(RO + 4, 8), :], -4), 0.0)

    wide_p = start_wide("p", 1, pre_slab)
    coarse_setup()
    R["load"][...] = jnp.zeros(R["load"].shape, F32)
    finish_around("f", around_f, 1, load_region(L2))
    first_sweep(L2, load_of(L2))
    sweep(L2, 0, into(L2, 1), False, 3, 9)
    residual(L2, 1, False, 4, 8)
    values = restricted(block2, block3, 4, 4, 32)

    gather_f = Gather("f", 1)
    gather_f.phase_x(own_tile(values, 1, 8))
    tile_lane = lanes_of((8, LANES))
    total = jnp.zeros((8, LANES), F32)
    for z in range(4):
        piece = roll(R["V2"][1, 5 + z, pl.ds(RO + 4, 8), :], 32 * z - 32)
        total = jnp.where((tile_lane >= 32 * z) & (tile_lane < 32 * z + 32), piece, total)
    R["TAp"][0:4, :] = total[0:4]
    around_p = start_around("p")
    gather_f.phase_y()
    gather_f.phase_z()

    def store_load(i, z, value):
        R["load"][pl.ds(z * L3.rows, L3.rows), :] = value

    gather_f.finish(store_load)

    first_sweep(L3, load_of(L3))
    sweep(L3, 0, into(L3, 1), False)
    residual(L3, 1, False)
    values = restricted(L3, L4)
    R["load"][pl.ds(0, L4.nz * L4.rows), :] = values
    first_sweep(L4, load_of(L4))
    for i in range(COARSE - 1):
        sweep(L4, i % 2, into(L4, (i + 1) % 2), False)
    last4 = (COARSE - 1) % 2

    def spread(level, nz_c, ny_c, nx_c, stride_c, get, base, halo):
        l = level.index
        M, PV = R["merge"], R["spread"]
        a, b = rows_of((LANES, LANES)), lanes_of((LANES, LANES))
        main = (a == b // 2) & (b < level.nx)
        edges = ((a == nx_c) & (b == level.right)) | ((a == LANES - 1) & (b == LANES - 1))
        wide = halo and level.nx == LANES
        if halo and not wide:
            main = main | edges
        height = (nz_c + 2) * stride_c
        stacked = jnp.concatenate([get(ze) for ze in range(nz_c + 2)], axis=0)
        M[0, pl.ds(0, height), :] = dot(stacked, jnp.where(main, 1.0, 0.0).astype(F32))
        if wide:
            M[1, pl.ds(0, height), :] = dot(stacked, jnp.where(edges, 1.0, 0.0).astype(F32))
        V = R[f"V{l}"]
        for layer in range(2 if wide else 1):
            for ze in range(nz_c + 2):
                value = M[layer, pl.ds(ze * stride_c + RO - 1, ny_c + 2), :]
                slabs = [zf for zf in (2 * ze - 1, 2 * ze) if 0 <= zf <= level.nz + 1]
                for phase in range(2):
                    PV[layer, ze, pl.ds(RO - 2 + phase, ny_c + 2, stride=2), :] = value
        for ze in range(nz_c + 2):
            for zf in (2 * ze - 1, 2 * ze):
                if 0 <= zf <= level.nz + 1:
                    size = level.stride
                    V[2, zf] = V[1, zf] + PV[0, ze, pl.ds(0, size), :]
                    if halo:
                        H = R[f"H{l}"]
                        H[2, zf] = H[1, zf] + PV[1 if wide else 0, ze, pl.ds(0, size), :]

    def coarse_slab(level, slot):
        V = R[f"V{level.index}"]

        def get(ze):
            value = V[slot, ze]
            if level.split:
                lane = lanes_of(value.shape)
                edge = (lane == level.right) | (lane == LANES - 1)
                value = jnp.where(edge, R[f"H{level.index}"][slot, ze], value)
            return value

        return get

    spread(L3, L4.nz, L4.ny, L4.nx, L4.stride, coarse_slab(L4, last4), 0, False)
    sweep(L3, 2, into(L3, 0), False)
    sweep(L3, 0, into(L3, 1), False)

    def start_region(level, slabs):
        a, b = rows_of((LANES, LANES)), lanes_of((LANES, LANES))
        copied = dot(jnp.concatenate(slabs, axis=0), jnp.where((a == b // 2) & (b < level.nx), 1.0, 0.0).astype(F32))
        V = R[f"V{level.index}"]
        for i in range(len(slabs)):
            for phase in range(2):
                R["spread"][0, i, pl.ds(phase, 8, stride=2), :] = copied[8 * i : 8 * i + 8]
        for z in range(level.nz):
            where_rows = pl.ds(RO, level.rows)
            added = jnp.where(inside(level, z) > 0.5, R["spread"][0, z // 2, pl.ds(0, level.rows), :], 0.0)
            V[2, z + 1, where_rows, :] = V[2, z + 1, where_rows, :] + added

    finish_around("p", around_p, 1, iterate_region(2))
    finish_wide("p", wide_p, 1, lambda i, z: R["V1"][2, z + 1, pl.ds(RO, 16), :], iterate_region(1))
    slabs = []
    count3 = L3.nz + 2
    for i in range(6):
        value = R["V3"][1, lax.rem(2 * gz + (count3 - 1 + i), count3)]
        value = roll(value, lax.rem(2 * L3.stride - RO + 2 - 2 * gy, L3.stride), axis=0)
        value = roll(value, lax.rem(LANES + 16 - 16 * gx, LANES))
        slabs.append(value[0:8])
    start_region(L2, slabs)
    sweep(L2, 2, into(L2, 3), False, 1, 11)
    sweep(L2, 3, into(L2, 0), False, 2, 10)
    start_region(L1, [roll(R["V2"][0, 3 + i, pl.ds(RO + 2, 8), :], -30) for i in range(8)])
    sweep(L1, 2, into(L1, 3), False, 2, 14)
    sweep(L1, 3, into(L1, 0), False, 3, 13)

    def region_slab(ze):
        return roll(R["V1"][0, 4 + ze, pl.ds(4, 24), :], -4)

    spread(L0, 8, 8, 64, 24, region_slab, 0, True)
    sweep(L0, 2, into(L0, 3))
    exchange(L0, 3, 2)

    def emit_out(z, value, delta):
        R["out"][z] = value + delta

    sweep(L0, 3, emit_out)
    drain()


def solution(mesh):
    sizes = (mesh.shape["gx"], mesh.shape["gy"], mesh.shape["gz"])
    GX, GY, GZ = sizes

    def body(conduct, cross, tissue, src_z, src_y, src_x):
        nz, ny, nx = tissue.shape
        sources = src_z.shape[0]
        levels = [Level(0, nz, ny, nx, True)]
        levels.append(Level(1, 16, 16, 72, False, (4, 4, 4)))
        levels.append(Level(2, 12, 12, 96, False, (4, 4, 32)))
        levels.append(Level(3, 2 * GZ, 2 * GY, 16 * GX, False))
        levels.append(Level(4, GZ, GY, 8 * GX, False))
        scratch = {}

        def vmem(name, *shape, dtype=F32):
            scratch[name] = pltpu.VMEM(shape, dtype)

        for level in levels:
            l, z, rows, stride, zrows = level.index, level.nz, level.rows, level.stride, level.zrows
            slots = 4 if l < 3 else 3
            vmem(f"K{l}", 6, z + 2, stride, LANES)
            vmem(f"C{l}", 18, z, rows, LANES)
            vmem(f"D{l}", 2, z, rows, LANES)
            vmem(f"G{l}", z, rows, LANES)
            vmem(f"V{l}", slots, z + 2, stride, LANES)
            vmem(f"XP{l}", z + 2, stride, LANES)
            vmem(f"XM{l}", z + 2, stride, LANES)
            vmem(f"XR{l}", z, stride, LANES)
            if level.split:
                vmem(f"H{l}", slots, z + 2, stride, LANES)
                vmem(f"KH{l}", 3, z, rows, LANES)
                vmem(f"YB{l}", 2, zrows, LANES)
                vmem(f"PB{l}", rows, LANES)
                vmem(f"ZB{l}", 2, rows, LANES)
                vmem(f"RZ{l}", 4, 2, rows, LANES)
                vmem(f"RY{l}", 4, 6, zrows, LANES)
                vmem(f"RP{l}", 4, 10, rows, LANES)
                vmem(f"KZ{l}", 2, 3, rows, LANES)
                vmem(f"KY{l}", 2, 3, zrows, LANES)
                vmem(f"KP{l}", 3, rows, LANES)
                vmem(f"RKZ{l}", 2, 3, rows, LANES)
                vmem(f"RKY{l}", 2, 3, zrows, LANES)
                vmem(f"RKP{l}", 2, 3, rows, LANES)
        for tag, height in (("k", 24), ("f", 8), ("p", 8)):
            vmem(f"TA{tag}", height, LANES)
            vmem(f"RA{tag}", len(AROUND), height, LANES)
        scratch["asend"] = pltpu.SemaphoreType.DMA((3, len(AROUND)))
        scratch["arecv"] = pltpu.SemaphoreType.DMA((3, len(AROUND)))
        for tag, comps in (("k", 6), ("f", 1), ("p", 1)):
            half = (comps + 1) // 2
            vmem(f"WA{tag}", 4, comps, 8, LANES)
            vmem(f"WB{tag}", 2, 2, comps, 8, LANES)
            vmem(f"WS{tag}", comps, 8, LANES)
            vmem(f"WT{tag}", 2, half, 8, LANES)
            vmem(f"WRA{tag}", 2, 2, comps, 8, LANES)
            vmem(f"WRB{tag}", 2, 2, comps, 8, LANES)
            vmem(f"WRC{tag}", 4, comps, 8, LANES)
            vmem(f"WRS{tag}", 6, comps, 8, LANES)
            vmem(f"WRT{tag}", 12, half, 8, LANES)
        scratch["wsend"] = pltpu.SemaphoreType.DMA((3, len(AROUND)))
        scratch["wrecv"] = pltpu.SemaphoreType.DMA((3, len(AROUND)))
        vmem("strips", 3, 16, LANES)
        vmem("KB1", 6, 8, 8, LANES)
        vmem("KB2", 6, 4, 8, LANES)
        vmem("PX", levels[0].stride, LANES)
        vmem("stage", 6 * 8 * 8, LANES)
        vmem("tile", 16, LANES)
        vmem("key", 2, sources, dtype=jnp.int32)
        vmem("counts", nz * ny, LANES)
        vmem("load", max(levels[3].nz * levels[3].rows, 64), LANES)
        vmem("merge", 2, 10 * 32, LANES)
        vmem("spread", 2, 10, 48, LANES)
        for tag, comps, height in (("k", 6, 16), ("f", 1, 8)):
            vmem(f"GX{tag}", height, LANES)
            vmem(f"RX{tag}", GX - 1, height, LANES)
            vmem(f"RY{tag}", GY, height, LANES)
            vmem(f"RZ{tag}", GZ, comps, levels[3].rows, LANES)
            most = max(sizes) - 1
            scratch[f"gs{tag}"] = pltpu.SemaphoreType.DMA((3, most))
            scratch[f"gr{tag}"] = pltpu.SemaphoreType.DMA((3, most))
        scratch["send"] = pltpu.SemaphoreType.DMA((len(MESSAGES),))
        scratch["recv"] = pltpu.SemaphoreType.DMA((2, len(MESSAGES)))
        scratch["ksend"] = pltpu.SemaphoreType.DMA((2, len(FACES)))
        scratch["krecv"] = pltpu.SemaphoreType.DMA((2, len(FACES)))
        names = ["conduct", "cross", "tissue", "src_z", "src_y", "src_x", "out"] + list(scratch)
        row = lambda value: value.reshape(1, sources)
        return pl.pallas_call(
            functools.partial(kernel, names, levels, sizes, sources),
            out_shape=jax.ShapeDtypeStruct((nz, ny, nx), F32),
            in_specs=[pl.BlockSpec(memory_space=pltpu.VMEM)] * 6,
            out_specs=pl.BlockSpec(memory_space=pltpu.VMEM),
            scratch_shapes=list(scratch.values()),
            compiler_params=pltpu.CompilerParams(
                collective_id=0, has_side_effects=True, vmem_limit_bytes=60 * 1024 * 1024
            ),
        )(conduct, cross, tissue, row(src_z), row(src_y), row(src_x))

    placed = (P(None, "gz", "gy", "gx"), P(None, "gz", "gy", "gx"), P("gz", "gy", "gx"), P(), P(), P())
    return jax.shard_map(body, mesh=mesh, in_specs=placed, out_specs=P("gz", "gy", "gx"), check_vma=False)
```

```python
import functools

import jax
import jax.numpy as jnp
from jax import lax
from jax.experimental import pallas as pl
from jax.experimental.pallas import tpu as pltpu
from jax.sharding import PartitionSpec as P

tau_step = 4000.0
relax = 0.55
stim_height = 64000.0
COARSE = 12
RO = 8
LANES = 128
MESH = pl.DeviceIdType.MESH
F32 = jnp.float32
PAIRS = ((0, 1, 3), (0, 2, 4), (1, 2, 5))


class Level:
    def __init__(self, index, nz, ny, nx, split, margin=None):
        self.index, self.nz, self.ny, self.nx, self.split, self.margin = index, nz, ny, nx, split, margin
        self.rows = max(8, -(-ny // 8) * 8)
        self.zrows = max(8, -(-nz // 8) * 8)
        self.stride = RO + self.rows + 8
        self.tau = tau_step / 4.0**index
        self.right = nx % LANES


def lanes_of(shape):
    return lax.broadcasted_iota(jnp.int32, shape, len(shape) - 1)


def rows_of(shape):
    return lax.broadcasted_iota(jnp.int32, shape, len(shape) - 2)


def roll(value, shift, axis=None):
    axis = value.ndim - 1 if axis is None else axis
    if isinstance(shift, int):
        shift = shift % value.shape[axis]
        if shift == 0:
            return value
    return pltpu.roll(value, shift, axis)


def dot(a, b):
    return lax.dot_general(
        a, b, (((1,), (0,)), ((), ())), precision=lax.Precision.HIGHEST, preferred_element_type=F32
    )


MESSAGES = [("z", 1, (0, 0, -1)), ("z", 0, (0, 0, 1))]
for _face, _oy in ((0, -1), (1, 1)):
    for _part, _oz in ((0, 0), (1, -1), (2, 1)):
        MESSAGES.append(("y", 3 * _face + _part, (0, _oy, _oz)))
for _side, _ox in ((0, -1), (1, 1)):
    for _part, (_oy, _oz) in enumerate(((0, 0), (-1, 0), (1, 0), (0, -1), (0, 1))):
        MESSAGES.append(("p", 5 * _side + _part, (_ox, _oy, _oz)))
AROUND = [(dx, dy, dz) for dz in (-1, 0, 1) for dy in (-1, 0, 1) for dx in (-1, 0, 1) if (dx, dy, dz) != (0, 0, 0)]
AROUND.sort(key=lambda offset: -sum(map(abs, offset)))
MESSAGES.sort(key=lambda message: -sum(map(abs, message[2])))
FACES = [("z", 1, (0, 0, -1)), ("z", 0, (0, 0, 1)), ("y", 0, (0, -1, 0)), ("y", 1, (0, 1, 0)), ("p", 0, (-1, 0, 0)), ("p", 1, (1, 0, 0))]


def kernel(names, levels, sizes, sources, *refs):
    R = dict(zip(names, refs))
    GX, GY, GZ = sizes
    gx, gy, gz = lax.axis_index("gx"), lax.axis_index("gy"), lax.axis_index("gz")

    def device(ox, oy, oz):
        return (lax.rem(gx + (ox + GX), GX), lax.rem(gy + (oy + GY), GY), lax.rem(gz + (oz + GZ), GZ))

    peers = list(AROUND)
    peers += [(k, 0, 0) for k in range(1, GX)] + [(0, k, 0) for k in range(1, GY)] + [(0, 0, k) for k in range(1, GZ)]
    seen, unique = set(), []
    for ox, oy, oz in peers:
        key = (ox % GX, oy % GY, oz % GZ)
        if key not in seen:
            seen.add(key)
            unique.append(key)
    barrier = pltpu.get_barrier_semaphore()
    for ox, oy, oz in unique:
        pl.semaphore_signal(barrier, inc=1, device_id=device(ox, oy, oz), device_id_type=MESH)

    def flag(condition):
        return jnp.where(condition, 0.0, 1.0).astype(F32)

    in_xp, in_xm = flag(gx == GX - 1), flag(gx == 0)
    in_yp, in_ym = flag(gy == GY - 1), flag(gy == 0)
    in_zp, in_zm = flag(gz == GZ - 1), flag(gz == 0)

    def clean(level, value):
        return value if level.ny == level.rows else jnp.where(rows_of(value.shape) < level.ny, value, 0.0)

    def bounds(level):
        if level.split:
            return in_zp, in_zm, in_yp, in_ym, in_xp, in_xm
        return (jnp.zeros((), F32),) * 6

    def inside(level, z):
        mz, my, mx = level.margin
        shape = (level.rows, LANES)
        lane, row = lanes_of(shape), rows_of(shape)
        mask_z = jnp.where(z < mz, in_zm, jnp.where(z >= level.nz - mz, in_zp, 1.0))
        mask_y = jnp.where(row < my, in_ym, jnp.where(row >= level.ny - my, in_yp, 1.0))
        mask_x = jnp.where(lane < mx, in_xm, jnp.where(lane >= level.nx - mx, in_xp, 1.0))
        return jnp.where((row < level.ny) & (lane < level.nx), mask_z * mask_y * mask_x, 0.0)

    def valid(dx, dy, dz):
        factor = None
        for d, plus, minus in ((dx, in_xp, in_xm), (dy, in_yp, in_ym), (dz, in_zp, in_zm)):
            if d:
                one = plus if d > 0 else minus
                factor = one if factor is None else factor * one
        return factor

    def times(value, factor):
        return value if factor is None else value * factor

    def pack_x(level, get):
        shape = (level.rows, LANES)
        lane = lanes_of(shape)
        out = jnp.zeros(shape, F32)
        for z in range(level.nz):
            value = get(z)
            first = (level.right + 2 * (z + 1)) % LANES
            last = (2 * (z + 1) + LANES - 1) % LANES
            a = roll(value, first)
            b = roll(value, last - (level.nx - 1))
            out = jnp.where(lane == first, a, jnp.where(lane == last, b, out))
        return out

    def coarsen_rows(level, lower, get, count):
        stage = R["stage"]
        half = level.ny // 2
        for i in range(count):
            for z in range(level.nz // 2):
                total = None
                for dz in range(2):
                    for dy in range(2):
                        piece = get(i, 2 * z + dz, dy, half)
                        total = piece if total is None else total + piece
                stage[pl.ds((i * (level.nz // 2) + z) * lower.rows, half), :] = total

    def coarsen_lanes(level, rows, first=0):
        a, b = rows_of((LANES, LANES)), lanes_of((LANES, LANES))
        matrix = jnp.where((b == (a - first) // 2) & (a >= first) & (b < level.nx // 2), 0.125, 0.0).astype(F32)
        return dot(R["stage"][pl.ds(0, rows), :], matrix)

    def coefficients(level):
        l = level.index
        K, C, D = R[f"K{l}"], R[f"C{l}"], R[f"D{l}"]
        n, rows = level.nz, level.rows
        shape = (rows, LANES)
        lane, row = lanes_of(shape), rows_of(shape)
        zp, zm, yp, ym, xp, xm = bounds(level)
        keep_yp = jnp.where(row == level.ny - 1, yp, 1.0)
        keep_ym = jnp.where(row == 0, ym, 1.0)
        keep_xp = jnp.where(lane == level.nx - 1, xp, 1.0)
        keep_xm = jnp.where(lane == 0, xm, 1.0)

        def step(z, carry):
            ze = z + 1

            def at(comp, dz=0, dy=0):
                return K[comp, ze + dz, pl.ds(RO + dy, rows), :]

            def along(comp, which, sign):
                value = at(comp)
                if level.split:
                    halo = R[f"KH{l}"][which, z]
                    value = jnp.where(lane == (level.right if sign > 0 else LANES - 1), halo, value)
                return roll(value, LANES - 1 if sign > 0 else 1)

            keep_zp = jnp.where(z == n - 1, zp, 1.0)
            keep_zm = jnp.where(z == 0, zm, 1.0)
            keep = ((keep_zp, keep_zm), (keep_yp, keep_ym), (keep_xp, keep_xm))
            weights = (
                (0.5 * (at(0) + at(0, 1)), 0.5 * (at(0) + at(0, -1))),
                (0.5 * (at(1) + at(1, 0, 1)), 0.5 * (at(1) + at(1, 0, -1))),
                (0.5 * (at(2) + along(2, 0, 1)), 0.5 * (at(2) + along(2, 0, -1))),
            )
            total = weights[0][0] + weights[0][1] + weights[1][0] + weights[1][1] + weights[2][0] + weights[2][1]
            diagonal = 1.0 + level.tau * total
            inverse = relax / diagonal
            scale = level.tau * inverse
            if level.margin:
                scale = scale * inside(level, z)
            D[0, z] = inverse
            D[1, z] = diagonal * (1.0 / relax)
            for a in range(3):
                for s in range(2):
                    C[2 * a + s, z] = scale * weights[a][s] * keep[a][s]
            quarter = 0.25 * scale

            def shifted(comp, axis, sign):
                if axis == 0:
                    return at(comp, sign)
                if axis == 1:
                    return at(comp, 0, sign)
                return along(comp, 1 if comp == 4 else 2, sign)

            for number, (a, b, comp) in enumerate(PAIRS):
                ka = [shifted(comp, a, 1), shifted(comp, a, -1)]
                kb = [shifted(comp, b, 1), shifted(comp, b, -1)]
                for sa in range(2):
                    for sb in range(2):
                        value = quarter * (ka[sa] + kb[sb]) * keep[a][sa] * keep[b][sb]
                        C[6 + 4 * number + 2 * sa + sb, z] = value if sa == sb else -value
            return carry

        lax.fori_loop(0, n, step, 0, unroll=min(n, 4))

    def sweep(level, source, emit, halo=True, first=0, last=None):
        l = level.index
        V, C, G, XP, XM = R[f"V{l}"], R[f"C{l}"], R[f"G{l}"], R[f"XP{l}"], R[f"XM{l}"]
        rows = level.rows

        def shift(ze, carry):
            value = V[source, ze]
            up = down = value
            if halo:
                lane = lanes_of(value.shape)
                edge = R[f"H{l}"][source, ze]
                up = jnp.where(lane == level.right, edge, value)
                down = jnp.where(lane == LANES - 1, edge, value)
            XP[ze] = roll(up, LANES - 1)
            XM[ze] = roll(down, 1)
            return carry

        last = level.nz if last is None else last
        lax.fori_loop(first, last + 2, shift, 0, unroll=last + 2 - first)

        def step(z, carry):
            ze = z + 1

            def at(dz, dy, dx):
                where_rows = pl.ds(RO + dy, rows)
                if dx == 0:
                    return V[source, ze + dz, where_rows, :]
                return (XP if dx > 0 else XM)[ze + dz, where_rows, :]

            center = at(0, 0, 0)
            parts = [G[z] - relax * center, None, None]
            offsets = [(1, 0, 0), (-1, 0, 0), (0, 1, 0), (0, -1, 0), (0, 0, 1), (0, 0, -1)]
            for a, b, _ in PAIRS:
                for sa in (1, -1):
                    for sb in (1, -1):
                        offset = [0, 0, 0]
                        offset[a], offset[b] = sa, sb
                        offsets.append(tuple(offset))
            for number, offset in enumerate(offsets):
                term = C[number, z] * at(*offset)
                slot = number % 3
                parts[slot] = term if parts[slot] is None else parts[slot] + term
            emit(z, center, (parts[0] + parts[1]) + parts[2])
            return carry

        lax.fori_loop(first, last, step, 0, unroll=min(last - first, 8))

    def into(level, slot):
        V = R[f"V{level.index}"]

        def emit(z, value, delta):
            V[slot, z + 1, pl.ds(RO, level.rows), :] = value + delta

        return emit

    pending = []
    count = [0]

    def drain():
        for copy in pending:
            copy.wait_send()
        pending.clear()

    def exchange(level, slot, step, during=None):
        l = level.index
        V, H, YB, PB, X = R[f"V{l}"], R[f"H{l}"], R[f"YB{l}"], R[f"PB{l}"], R["PX"]
        ZB = R[f"ZB{l}"]
        RZ, RY, RP = R[f"RZ{l}"], R[f"RY{l}"], R[f"RP{l}"]
        nz, ny, rows, zrows = level.nz, level.ny, level.rows, level.zrows
        drain()
        for z in range(nz):
            YB[0, pl.ds(z, 1), :] = V[slot, z + 1, pl.ds(RO, 1), :]
            YB[1, pl.ds(z, 1), :] = V[slot, z + 1, pl.ds(RO + ny - 1, 1), :]
        ZB[0] = V[slot, 1, pl.ds(RO, rows), :]
        ZB[1] = V[slot, nz, pl.ds(RO, rows), :]
        PB[...] = pack_x(level, lambda z: V[slot, z + 1, pl.ds(RO, rows), :])
        parity = count[0] % 2
        count[0] += 1
        copies = []
        ylow, zlow = rows - 8, zrows - 8
        for number, (kind, where, (ox, oy, oz)) in enumerate(MESSAGES):
            if kind == "z":
                src, dst = ZB.at[0 if where else 1], RZ.at[step, where]
            elif kind == "y":
                face = where // 3
                if where % 3 == 0:
                    src, dst = YB.at[face], RY.at[step, where]
                else:
                    low = 0 if where % 3 == 1 else zlow
                    src, dst = YB.at[face, pl.ds(low, 8)], RY.at[step, where, pl.ds(0, 8)]
            else:
                part = where % 5
                if part in (1, 2):
                    low = 0 if part == 1 else ylow
                    src, dst = PB.at[pl.ds(low, 8)], RP.at[step, where, pl.ds(0, 8)]
                else:
                    src, dst = PB, RP.at[step, where]
            copy = pltpu.make_async_remote_copy(
                src_ref=src, dst_ref=dst, send_sem=R["send"].at[number], recv_sem=R["recv"].at[parity, number],
                device_id=device(ox, oy, oz), device_id_type=MESH,
            )
            copy.start()
            copies.append(copy)
        pending.extend(copies)
        if during is not None:
            during()
        for copy in copies:
            copy.wait_recv()
        V[slot, nz + 1, pl.ds(RO, rows), :] = RZ[step, 1]
        V[slot, 0, pl.ds(RO, rows), :] = RZ[step, 0]
        for face in range(2):
            place = RO + ny if face == 0 else RO - 1
            for z in range(nz):
                V[slot, z + 1, pl.ds(place, 1), :] = RY[step, 3 * face, pl.ds(z, 1), :]
            V[slot, nz + 1, pl.ds(place, 1), :] = RY[step, 3 * face + 1, pl.ds(0, 1), :]
            V[slot, 0, pl.ds(place, 1), :] = RY[step, 3 * face + 2, pl.ds(nz - 1 - zlow, 1), :]

        def merged(part, size):
            even = lanes_of((size, LANES)) % 2 == 0
            return jnp.where(even, RP[step, part, pl.ds(0, size), :], RP[step, 5 + part, pl.ds(0, size), :])

        lane = lanes_of((rows, LANES))
        middle = merged(0, rows)
        above = roll(merged(3, rows), 2 * nz)
        below = roll(merged(4, rows), -2 * nz)

        def slab_lanes(ze):
            return (lane == (level.right + 2 * ze) % LANES) | (lane == (2 * ze + LANES - 1) % LANES)

        middle = jnp.where(slab_lanes(nz + 1), above, jnp.where(slab_lanes(0), below, middle))
        size = level.stride
        X[pl.ds(RO, rows), :] = middle
        X[pl.ds(RO + ny, 1), :] = merged(1, 8)[0:1]
        X[pl.ds(RO - 1, 1), :] = merged(2, 8)[ny - 1 - ylow : ny - ylow]
        whole = X[pl.ds(0, size), :]
        for ze in range(nz + 2):
            H[slot, ze] = roll(whole, -2 * ze)

    def start_faces(level):
        l = level.index
        K, KY, KP, KZ = R[f"K{l}"], R[f"KY{l}"], R[f"KP{l}"], R[f"KZ{l}"]
        nz, ny, rows = level.nz, level.ny, level.rows
        for i, comp in enumerate((0, 3, 4)):
            KZ[0, i] = K[comp, 1, pl.ds(RO, rows), :]
            KZ[1, i] = K[comp, nz, pl.ds(RO, rows), :]
        for i, comp in enumerate((1, 3, 5)):
            for z in range(nz):
                KY[0, i, pl.ds(z, 1), :] = K[comp, z + 1, pl.ds(RO, 1), :]
                KY[1, i, pl.ds(z, 1), :] = K[comp, z + 1, pl.ds(RO + ny - 1, 1), :]
        for i, comp in enumerate((2, 4, 5)):
            KP[i] = pack_x(level, lambda z: K[comp, z + 1, pl.ds(RO, rows), :])
        copies = []
        for number, (kind, where, (ox, oy, oz)) in enumerate(FACES):
            if kind == "z":
                src, dst = KZ.at[0 if where else 1], R[f"RKZ{l}"].at[where]
            elif kind == "y":
                src, dst = KY.at[where], R[f"RKY{l}"].at[where]
            else:
                src, dst = KP, R[f"RKP{l}"].at[where]
            copy = pltpu.make_async_remote_copy(
                src_ref=src, dst_ref=dst, send_sem=R["ksend"].at[l, number], recv_sem=R["krecv"].at[l, number],
                device_id=device(ox, oy, oz), device_id_type=MESH,
            )
            copy.start()
            copies.append(copy)
        return copies

    def finish_faces(level, copies):
        l = level.index
        K, KH = R[f"K{l}"], R[f"KH{l}"]
        nz, ny, rows = level.nz, level.ny, level.rows
        for copy in copies:
            copy.wait()
        for i, comp in enumerate((0, 3, 4)):
            K[comp, nz + 1, pl.ds(RO, rows), :] = R[f"RKZ{l}"][1, i] * in_zp
            K[comp, 0, pl.ds(RO, rows), :] = R[f"RKZ{l}"][0, i] * in_zm
        for i, comp in enumerate((1, 3, 5)):
            for z in range(nz):
                K[comp, z + 1, pl.ds(RO + ny, 1), :] = R[f"RKY{l}"][0, i, pl.ds(z, 1), :] * in_yp
                K[comp, z + 1, pl.ds(RO - 1, 1), :] = R[f"RKY{l}"][1, i, pl.ds(z, 1), :] * in_ym
        even = lanes_of((rows, LANES)) % 2 == 0
        for i in range(3):
            both = jnp.where(even, R[f"RKP{l}"][0, i] * in_xp, R[f"RKP{l}"][1, i] * in_xm)
            for z in range(nz):
                KH[i, z] = roll(both, -2 * (z + 1))

    def start_around(tag):
        tag_index = "kfp".index(tag)
        copies = []
        for number, (dx, dy, dz) in enumerate(AROUND):
            copy = pltpu.make_async_remote_copy(
                src_ref=R[f"TA{tag}"], dst_ref=R[f"RA{tag}"].at[number], send_sem=R["asend"].at[tag_index, number],
                recv_sem=R["arecv"].at[tag_index, number], device_id=device(-dx, -dy, -dz), device_id_type=MESH,
            )
            copy.start()
            copies.append(copy)
        return copies

    def finish_around(tag, copies, comps, store):
        for copy in copies:
            copy.wait()
        tile = R[f"TA{tag}"]
        lane = lanes_of(tile.shape)
        for dz in (-1, 0, 1):
            for dy in (-1, 0, 1):
                row_tiles = []
                for dx in (-1, 0, 1):
                    if (dx, dy, dz) == (0, 0, 0):
                        row_tiles.append(tile[...])
                        continue
                    value = R[f"RA{tag}"][AROUND.index((dx, dy, dz))]
                    row_tiles.append(times(value, valid(dx, dy, dz)))
                for z in range(4):
                    low, mid, high = (roll(row_tiles[i], 32 * i - 32 * z) for i in range(3))
                    value = jnp.where(lane < 32, low, jnp.where(lane < 64, mid, jnp.where(lane < 96, high, 0.0)))
                    for comp in range(comps):
                        store(comp, 4 * (dz + 1) + z, 4 * (dy + 1), value[4 * comp : 4 * comp + 4])

    def start_wide(tag, comps, get):
        tag_index = "kfp".index(tag)
        A, B, S, S2 = (R[f"{name}{tag}"] for name in ("WA", "WB", "WS", "WT"))
        shape = (8, LANES)
        lane = lanes_of(shape)
        for c in range(comps):
            slabs = [get(c, z) for z in range(8)]
            strip = jnp.zeros(shape, F32)
            for z in range(8):
                low, high = 68 + 8 * z, 8 * z
                strip = jnp.where((lane >= low) & (lane < low + 4), roll(slabs[z], low), strip)
                strip = jnp.where((lane >= high) & (lane < high + 4), roll(slabs[z], high - 60), strip)
            S[c] = strip
            for h in range(2):
                S2[h, c // 2, pl.ds(4 * (c % 2), 4), :] = strip[4 * h : 4 * h + 4]
            for p in range(4):
                pair = slabs[2 * p] + roll(slabs[2 * p + 1], 64)
                A[p, c] = pair
                for h in range(2):
                    B[h, p // 2, c, pl.ds(4 * (p % 2), 4), :] = pair[4 * h : 4 * h + 4]
        copies = []
        for number, (dx, dy, dz) in enumerate(AROUND):
            t, h = int(dz < 0), int(dy < 0)
            iz, iy, ix = int(dz > 0), int(dy > 0), int(dx > 0)
            if dx == 0 and dy == 0:
                src, dst = A.at[pl.ds(2 * t, 2)], R[f"WRA{tag}"].at[iz]
            elif dx == 0 and dz == 0:
                src, dst = B.at[h], R[f"WRB{tag}"].at[iy]
            elif dx == 0:
                src, dst = B.at[h, t], R[f"WRC{tag}"].at[2 * iy + iz]
            elif dy == 0:
                src, dst = S, R[f"WRS{tag}"].at[3 * ix + dz + 1]
            else:
                src, dst = S2.at[h], R[f"WRT{tag}"].at[3 * (2 * ix + iy) + dz + 1]
            copy = pltpu.make_async_remote_copy(
                src_ref=src, dst_ref=dst, send_sem=R["wsend"].at[tag_index, number],
                recv_sem=R["wrecv"].at[tag_index, number], device_id=device(-dx, -dy, -dz), device_id_type=MESH,
            )
            copy.start()
            copies.append(copy)
        return copies

    def finish_wide(tag, copies, comps, load, store):
        for copy in copies:
            copy.wait()
        A = R[f"WA{tag}"]
        MS = R["strips"]
        lane8, lane16 = lanes_of((8, LANES)), lanes_of((16, LANES))
        edge = (lane16 < 4) | ((lane16 >= 68) & (lane16 < 72))
        for c in range(comps):
            for dz in (-1, 0, 1):
                iz = int(dz > 0)
                zs = range(4, 8) if dz < 0 else range(0, 8) if dz == 0 else range(0, 4)
                base = {-1: -4, 0: 4, 1: 12}[dz]
                for z in zs:
                    tile = A[z // 2, c] if dz == 0 else R[f"WRA{tag}"][iz, z // 2 - (2 if dz < 0 else 0), c]
                    store(c, z + base, 4, roll(times(tile, valid(0, 0, dz)), 4 - 64 * (z % 2)))
                for dy in (-1, 1):
                    iy = int(dy > 0)
                    for z in zs:
                        tile = R[f"WRB{tag}"][iy, z // 4, c] if dz == 0 else R[f"WRC{tag}"][2 * iy + iz, c]
                        part = 4 * ((z % 4) // 2)
                        piece = roll(times(tile, valid(0, dy, dz)), 4 - 64 * (z % 2))
                        store(c, z + base, 0 if dy < 0 else 12, piece[part : part + 4])
                for dy in (-1, 0, 1):
                    iy = int(dy > 0)
                    sides = []
                    for ix, dx in enumerate((-1, 1)):
                        if dy == 0:
                            tile = R[f"WRS{tag}"][3 * ix + dz + 1, c]
                        else:
                            tile = R[f"WRT{tag}"][3 * (2 * ix + iy) + dz + 1, c // 2]
                        sides.append(times(tile, valid(dx, dy, dz)))
                    both = jnp.where(lane8 < 64, sides[0], sides[1])
                    if dy == 0:
                        MS[dz + 1, pl.ds(4, 8), :] = both
                    else:
                        MS[dz + 1, pl.ds(0 if dy < 0 else 12, 4), :] = both[4 * (c % 2) : 4 * (c % 2) + 4]
                strip = MS[dz + 1]
                for z in zs:
                    store(c, z + base, 0, jnp.where(edge, roll(strip, -8 * z), load(c, z + base)))

    class Gather:
        def __init__(self, tag, comps):
            self.tag, self.comps = tag, comps
            self.copies = []

        def send(self, phase, src, dst_of, targets):
            self.copies = []
            for number, offset in enumerate(targets):
                copy = pltpu.make_async_remote_copy(
                    src_ref=src, dst_ref=dst_of(number), send_sem=R[f"gs{self.tag}"].at[phase, number],
                    recv_sem=R[f"gr{self.tag}"].at[phase, number], device_id=device(*offset), device_id_type=MESH,
                )
                copy.start()
                self.copies.append(copy)

        def wait(self):
            for copy in self.copies:
                copy.wait()

        def phase_x(self, tiles):
            own, received = R[f"GX{self.tag}"], R[f"RX{self.tag}"]
            own[...] = tiles
            self.send(0, own, lambda number: received.at[number], [(k, 0, 0) for k in range(1, GX)])

        def phase_y(self):
            self.wait()
            slots = R[f"RY{self.tag}"]
            total = R[f"GX{self.tag}"][...]
            for k in range(GX - 1):
                total = total + R[f"RX{self.tag}"][k]
            slots[gy] = total
            self.send(1, slots.at[gy], lambda number: slots.at[gy], [(0, k, 0) for k in range(1, GY)])

        def phase_z(self):
            self.wait()
            slots, out = R[f"RY{self.tag}"], R[f"RZ{self.tag}"]
            for i in range(self.comps):
                for y in range(GY):
                    out[gz, i, pl.ds(2 * y, 2), :] = slots[y, pl.ds(2 * i, 2), :]
            self.send(2, out.at[gz], lambda number: out.at[gz], [(0, 0, k) for k in range(1, GZ)])

        def finish(self, store):
            self.wait()
            out = R[f"RZ{self.tag}"]
            for i in range(self.comps):
                for z in range(GZ):
                    value = out[z, i]
                    left = lanes_of(value.shape) < 64
                    store(i, 2 * z, jnp.where(left, value, 0.0))
                    store(i, 2 * z + 1, jnp.where(left, roll(value, 64), 0.0))

    def own_tile(values, comps, total_rows):
        T = R["tile"]
        T[...] = jnp.zeros(T.shape, F32)
        for i in range(comps):
            low = values[(2 * i) * 8 : (2 * i) * 8 + 8]
            high = values[(2 * i + 1) * 8 : (2 * i + 1) * 8 + 8]
            T[pl.ds(2 * i, 2), :] = (low + roll(high, 64))[0:2]
        return roll(T[pl.ds(0, total_rows), :], 16 * gx)

    L0, L1, L2, L3, L4 = levels
    block1, block2, block3 = Level(1, 8, 8, 64, True), Level(2, 4, 4, 32, True), Level(3, 2, 2, 16, False)

    def fill(z, carry):
        weight = R["tissue"][z].astype(F32)
        for comp in range(3):
            R["K0"][comp, z + 1, pl.ds(RO, L0.rows), :] = R["conduct"][comp, z] * weight
            R["K0"][3 + comp, z + 1, pl.ds(RO, L0.rows), :] = R["cross"][comp, z] * weight
        return carry

    lax.fori_loop(0, L0.nz, fill, 0, unroll=4)
    pl.semaphore_wait(barrier, len(unique))
    faces0 = start_faces(L0)

    R["stage"][...] = jnp.zeros(R["stage"].shape, F32)

    def tensor_rows(l, offset):
        return lambda i, z, dy, n: R[f"K{l}"][i, z + 1, pl.ds(offset + dy, n, stride=2), :]

    coarsen_rows(L0, block1, tensor_rows(0, RO), 6)
    values = coarsen_lanes(L0, 6 * 8 * 8)

    def slab_of(values):
        return lambda c, z: values[(c * 8 + z) * 8 : (c * 8 + z) * 8 + 8]

    wide_k = start_wide("k", 6, slab_of(values))
    for i in range(6):
        for z in range(8):
            R["KB1"][i, z] = values[(i * 8 + z) * 8 : (i * 8 + z) * 8 + 8]
    coarsen_rows(block1, block2, lambda i, z, dy, n: R["KB1"][i, z, pl.ds(dy, n, stride=2), :], 6)
    values = coarsen_lanes(block1, 6 * 4 * 8)

    def block2_tile(ref, comps, values):
        for i in range(comps):
            total = None
            for z in range(4):
                start = (i * 4 + z) * 8
                piece = roll(values[start : start + 8], 32 * z)
                total = piece if total is None else total + piece
            ref[pl.ds(4 * i, 4), :] = total[0:4]

    R["TAf"][...] = jnp.zeros(R["TAf"].shape, F32)
    R["TAp"][...] = jnp.zeros(R["TAp"].shape, F32)
    block2_tile(R["TAk"], 6, values)
    around_k = start_around("k")
    for i in range(6):
        for z in range(4):
            start = (i * 4 + z) * 8
            R["KB2"][i, z] = values[start : start + 8]
    coarsen_rows(block2, block3, lambda i, z, dy, n: R["KB2"][i, z, pl.ds(dy, n, stride=2), :], 6)
    gather_k = Gather("k", 6)
    gather_k.phase_x(own_tile(coarsen_lanes(block2, 6 * 2 * 8), 6, 16))

    for level in (L1, L2, L3, L4):
        for name in ("K", "V"):
            ref = R[f"{name}{level.index}"]
            for i in range(ref.shape[0]):
                ref[i] = jnp.zeros(ref.shape[1:], F32)
    R["load"][...] = jnp.zeros(R["load"].shape, F32)

    zl = R["src_z"][...] - gz * L0.nz
    yl = R["src_y"][...] - gy * L0.ny
    xl = R["src_x"][...] - gx * L0.nx
    here = (zl >= 0) & (zl < L0.nz) & (yl >= 0) & (yl < L0.ny)
    R["key"][0:1, :] = jnp.where(here, zl * L0.ny + yl, -1)
    R["key"][1:2, :] = xl
    R["counts"][...] = jnp.zeros(R["counts"].shape, F32)
    chunk = 256

    def scatter(i, carry):
        start = pl.multiple_of(i * chunk, chunk)
        key = R["key"][0:1, pl.ds(start, chunk)]
        key_x = R["key"][1:2, pl.ds(start, chunk)]
        left = jnp.where(rows_of((L0.nz * L0.ny, chunk)) == key, 1.0, 0.0).astype(jnp.bfloat16)
        right = jnp.where(rows_of((LANES, chunk)) == key_x, 1.0, 0.0).astype(jnp.bfloat16)
        R["counts"][...] += lax.dot_general(left, right, (((1,), (1,)), ((), ())), preferred_element_type=F32)
        return carry

    lax.fori_loop(0, sources // chunk, scatter, 0, unroll=2)

    finish_faces(L0, faces0)
    coefficients(L0)

    def load0(z):
        return stim_height * R["counts"][pl.ds(pl.multiple_of(z * L0.ny, 8), L0.rows), :]

    def first_sweep(level, load):
        l = level.index

        def step(z, carry):
            value = load(z) * R[f"D{l}"][0, z]
            R[f"G{l}"][z] = value
            R[f"V{l}"][0, z + 1, pl.ds(RO, level.rows), :] = value
            return carry

        lax.fori_loop(0, level.nz, step, 0, unroll=min(level.nz, 8))

    def residual(level, slot, halo=True, first=0, last=None):
        l = level.index
        store = R[f"XR{l}"]

        def emit(z, value, delta):
            store[z, pl.ds(RO, level.rows), :] = delta * R[f"D{l}"][1, z]

        sweep(level, slot, emit, halo, first, last)

    def restricted(level, lower, z0=0, y0=0, x0=0):
        def get(i, z, dy, n):
            return R[f"XR{level.index}"][z + z0, pl.ds(RO + y0 + dy, n, stride=2), :]

        coarsen_rows(level, lower, get, 1)
        return coarsen_lanes(level, (level.nz // 2) * lower.rows, x0)

    def tensor_region(l):
        def store(i, z, row, value):
            R[f"K{l}"][i, z + 1, pl.ds(RO + row, value.shape[0]), :] = value

        return store

    def iterate_region(l):
        def store(i, z, row, value):
            R[f"V{l}"][2, z + 1, pl.ds(RO + row, value.shape[0]), :] = value

        return store

    def load_region(level):
        def store(i, z, row, value):
            R["load"][pl.ds(z * level.rows + row, value.shape[0]), :] = value

        return store

    def during_01():
        gather_k.phase_y()

    def during_02():
        gather_k.phase_z()
        finish_wide("k", wide_k, 6, lambda i, z: R["K1"][i, z + 1, pl.ds(RO, 16), :], tensor_region(1))
        coefficients(L1)

    def during_10():
        finish_around("k", around_k, 6, tensor_region(2))
        coefficients(L2)

    def coarse_setup():
        def store(i, z, value):
            R["K3"][i, z + 1, pl.ds(RO, L3.rows), :] = clean(L3, value)

        gather_k.finish(store)
        coefficients(L3)
        coarsen_rows(L3, L4, tensor_rows(3, RO), 6)
        height = L4.nz * L4.rows
        values = coarsen_lanes(L3, 6 * height)
        for i in range(6):
            for z in range(L4.nz):
                start = i * height + z * L4.rows
                R["K4"][i, z + 1, pl.ds(RO, L4.rows), :] = clean(L4, values[start : start + L4.rows])
        coefficients(L4)

    def load_of(level):
        return lambda z: clean(level, R["load"][pl.ds(pl.multiple_of(z * level.rows, 8), level.rows), :])

    first_sweep(L0, load0)
    exchange(L0, 0, 0, during_01)
    sweep(L0, 0, into(L0, 1))
    exchange(L0, 1, 1, during_02)
    residual(L0, 1)
    values = restricted(L0, block1)

    wide_f = start_wide("f", 1, slab_of(values))
    during_10()
    finish_wide("f", wide_f, 1, lambda i, z: R["load"][pl.ds(16 * z, 16), :], load_region(L1))
    first_sweep(L1, load_of(L1))
    sweep(L1, 0, into(L1, 1), False, 3, 13)
    residual(L1, 1, False, 4, 12)
    values = restricted(block1, block2, 4, 4, 4)

    block2_tile(R["TAf"], 1, values)
    around_f = start_around("f")
    lane8 = lanes_of((8, LANES))

    def pre_slab(c, z):
        return jnp.where(lane8 < 64, roll(R["V1"][1, 5 + z, pl.ds(RO + 4, 8), :], -4), 0.0)

    wide_p = start_wide("p", 1, pre_slab)
    coarse_setup()
    R["load"][...] = jnp.zeros(R["load"].shape, F32)
    finish_around("f", around_f, 1, load_region(L2))
    first_sweep(L2, load_of(L2))
    sweep(L2, 0, into(L2, 1), False, 3, 9)
    residual(L2, 1, False, 4, 8)
    values = restricted(block2, block3, 4, 4, 32)

    gather_f = Gather("f", 1)
    gather_f.phase_x(own_tile(values, 1, 8))
    tile_lane = lanes_of((8, LANES))
    total = jnp.zeros((8, LANES), F32)
    for z in range(4):
        piece = roll(R["V2"][1, 5 + z, pl.ds(RO + 4, 8), :], 32 * z - 32)
        total = jnp.where((tile_lane >= 32 * z) & (tile_lane < 32 * z + 32), piece, total)
    R["TAp"][0:4, :] = total[0:4]
    around_p = start_around("p")
    gather_f.phase_y()
    gather_f.phase_z()

    def store_load(i, z, value):
        R["load"][pl.ds(z * L3.rows, L3.rows), :] = value

    gather_f.finish(store_load)

    first_sweep(L3, load_of(L3))
    sweep(L3, 0, into(L3, 1), False)
    residual(L3, 1, False)
    values = restricted(L3, L4)
    R["load"][pl.ds(0, L4.nz * L4.rows), :] = values
    first_sweep(L4, load_of(L4))
    for i in range(COARSE - 1):
        sweep(L4, i % 2, into(L4, (i + 1) % 2), False)
    last4 = (COARSE - 1) % 2

    def spread(level, nz_c, ny_c, nx_c, stride_c, get, base, halo):
        l = level.index
        M, PV = R["merge"], R["spread"]
        a, b = rows_of((LANES, LANES)), lanes_of((LANES, LANES))
        main = (a == b // 2) & (b < level.nx)
        edges = ((a == nx_c) & (b == level.right)) | ((a == LANES - 1) & (b == LANES - 1))
        wide = halo and level.nx == LANES
        if halo and not wide:
            main = main | edges
        height = (nz_c + 2) * stride_c
        stacked = jnp.concatenate([get(ze) for ze in range(nz_c + 2)], axis=0)
        M[0, pl.ds(0, height), :] = dot(stacked, jnp.where(main, 1.0, 0.0).astype(F32))
        if wide:
            M[1, pl.ds(0, height), :] = dot(stacked, jnp.where(edges, 1.0, 0.0).astype(F32))
        V = R[f"V{l}"]
        for layer in range(2 if wide else 1):
            for ze in range(nz_c + 2):
                value = M[layer, pl.ds(ze * stride_c + RO - 1, ny_c + 2), :]
                slabs = [zf for zf in (2 * ze - 1, 2 * ze) if 0 <= zf <= level.nz + 1]
                for phase in range(2):
                    PV[layer, ze, pl.ds(RO - 2 + phase, ny_c + 2, stride=2), :] = value
        for ze in range(nz_c + 2):
            for zf in (2 * ze - 1, 2 * ze):
                if 0 <= zf <= level.nz + 1:
                    size = level.stride
                    V[2, zf] = V[1, zf] + PV[0, ze, pl.ds(0, size), :]
                    if halo:
                        H = R[f"H{l}"]
                        H[2, zf] = H[1, zf] + PV[1 if wide else 0, ze, pl.ds(0, size), :]

    def coarse_slab(level, slot):
        V = R[f"V{level.index}"]

        def get(ze):
            value = V[slot, ze]
            if level.split:
                lane = lanes_of(value.shape)
                edge = (lane == level.right) | (lane == LANES - 1)
                value = jnp.where(edge, R[f"H{level.index}"][slot, ze], value)
            return value

        return get

    spread(L3, L4.nz, L4.ny, L4.nx, L4.stride, coarse_slab(L4, last4), 0, False)
    sweep(L3, 2, into(L3, 0), False)
    sweep(L3, 0, into(L3, 1), False)

    def start_region(level, slabs):
        a, b = rows_of((LANES, LANES)), lanes_of((LANES, LANES))
        copied = dot(jnp.concatenate(slabs, axis=0), jnp.where((a == b // 2) & (b < level.nx), 1.0, 0.0).astype(F32))
        V = R[f"V{level.index}"]
        for i in range(len(slabs)):
            for phase in range(2):
                R["spread"][0, i, pl.ds(phase, 8, stride=2), :] = copied[8 * i : 8 * i + 8]
        for z in range(level.nz):
            where_rows = pl.ds(RO, level.rows)
            added = jnp.where(inside(level, z) > 0.5, R["spread"][0, z // 2, pl.ds(0, level.rows), :], 0.0)
            V[2, z + 1, where_rows, :] = V[2, z + 1, where_rows, :] + added

    finish_around("p", around_p, 1, iterate_region(2))
    finish_wide("p", wide_p, 1, lambda i, z: R["V1"][2, z + 1, pl.ds(RO, 16), :], iterate_region(1))
    slabs = []
    count3 = L3.nz + 2
    for i in range(6):
        value = R["V3"][1, lax.rem(2 * gz + (count3 - 1 + i), count3)]
        value = roll(value, lax.rem(2 * L3.stride - RO + 2 - 2 * gy, L3.stride), axis=0)
        value = roll(value, lax.rem(LANES + 16 - 16 * gx, LANES))
        slabs.append(value[0:8])
    start_region(L2, slabs)
    sweep(L2, 2, into(L2, 3), False, 1, 11)
    sweep(L2, 3, into(L2, 0), False, 2, 10)
    start_region(L1, [roll(R["V2"][0, 3 + i, pl.ds(RO + 2, 8), :], -30) for i in range(8)])
    sweep(L1, 2, into(L1, 3), False, 2, 14)
    sweep(L1, 3, into(L1, 0), False, 3, 13)

    def region_slab(ze):
        return roll(R["V1"][0, 4 + ze, pl.ds(4, 24), :], -4)

    spread(L0, 8, 8, 64, 24, region_slab, 0, True)
    sweep(L0, 2, into(L0, 3))
    exchange(L0, 3, 2)

    def emit_out(z, value, delta):
        R["out"][z] = value + delta

    sweep(L0, 3, emit_out)
    drain()


def solution(mesh):
    sizes = (mesh.shape["gx"], mesh.shape["gy"], mesh.shape["gz"])
    GX, GY, GZ = sizes

    def body(conduct, cross, tissue, src_z, src_y, src_x):
        nz, ny, nx = tissue.shape
        sources = src_z.shape[0]
        levels = [Level(0, nz, ny, nx, True)]
        levels.append(Level(1, 16, 16, 72, False, (4, 4, 4)))
        levels.append(Level(2, 12, 12, 96, False, (4, 4, 32)))
        levels.append(Level(3, 2 * GZ, 2 * GY, 16 * GX, False))
        levels.append(Level(4, GZ, GY, 8 * GX, False))
        scratch = {}

        def vmem(name, *shape, dtype=F32):
            scratch[name] = pltpu.VMEM(shape, dtype)

        for level in levels:
            l, z, rows, stride, zrows = level.index, level.nz, level.rows, level.stride, level.zrows
            slots = 4 if l < 3 else 3
            vmem(f"K{l}", 6, z + 2, stride, LANES)
            vmem(f"C{l}", 18, z, rows, LANES)
            vmem(f"D{l}", 2, z, rows, LANES)
            vmem(f"G{l}", z, rows, LANES)
            vmem(f"V{l}", slots, z + 2, stride, LANES)
            vmem(f"XP{l}", z + 2, stride, LANES)
            vmem(f"XM{l}", z + 2, stride, LANES)
            vmem(f"XR{l}", z, stride, LANES)
            if level.split:
                vmem(f"H{l}", slots, z + 2, stride, LANES)
                vmem(f"KH{l}", 3, z, rows, LANES)
                vmem(f"YB{l}", 2, zrows, LANES)
                vmem(f"PB{l}", rows, LANES)
                vmem(f"ZB{l}", 2, rows, LANES)
                vmem(f"RZ{l}", 4, 2, rows, LANES)
                vmem(f"RY{l}", 4, 6, zrows, LANES)
                vmem(f"RP{l}", 4, 10, rows, LANES)
                vmem(f"KZ{l}", 2, 3, rows, LANES)
                vmem(f"KY{l}", 2, 3, zrows, LANES)
                vmem(f"KP{l}", 3, rows, LANES)
                vmem(f"RKZ{l}", 2, 3, rows, LANES)
                vmem(f"RKY{l}", 2, 3, zrows, LANES)
                vmem(f"RKP{l}", 2, 3, rows, LANES)
        for tag, height in (("k", 24), ("f", 8), ("p", 8)):
            vmem(f"TA{tag}", height, LANES)
            vmem(f"RA{tag}", len(AROUND), height, LANES)
        scratch["asend"] = pltpu.SemaphoreType.DMA((3, len(AROUND)))
        scratch["arecv"] = pltpu.SemaphoreType.DMA((3, len(AROUND)))
        for tag, comps in (("k", 6), ("f", 1), ("p", 1)):
            half = (comps + 1) // 2
            vmem(f"WA{tag}", 4, comps, 8, LANES)
            vmem(f"WB{tag}", 2, 2, comps, 8, LANES)
            vmem(f"WS{tag}", comps, 8, LANES)
            vmem(f"WT{tag}", 2, half, 8, LANES)
            vmem(f"WRA{tag}", 2, 2, comps, 8, LANES)
            vmem(f"WRB{tag}", 2, 2, comps, 8, LANES)
            vmem(f"WRC{tag}", 4, comps, 8, LANES)
            vmem(f"WRS{tag}", 6, comps, 8, LANES)
            vmem(f"WRT{tag}", 12, half, 8, LANES)
        scratch["wsend"] = pltpu.SemaphoreType.DMA((3, len(AROUND)))
        scratch["wrecv"] = pltpu.SemaphoreType.DMA((3, len(AROUND)))
        vmem("strips", 3, 16, LANES)
        vmem("KB1", 6, 8, 8, LANES)
        vmem("KB2", 6, 4, 8, LANES)
        vmem("PX", levels[0].stride, LANES)
        vmem("stage", 6 * 8 * 8, LANES)
        vmem("tile", 16, LANES)
        vmem("key", 2, sources, dtype=jnp.int32)
        vmem("counts", nz * ny, LANES)
        vmem("load", max(levels[3].nz * levels[3].rows, 64), LANES)
        vmem("merge", 2, 10 * 32, LANES)
        vmem("spread", 2, 10, 48, LANES)
        for tag, comps, height in (("k", 6, 16), ("f", 1, 8)):
            vmem(f"GX{tag}", height, LANES)
            vmem(f"RX{tag}", GX - 1, height, LANES)
            vmem(f"RY{tag}", GY, height, LANES)
            vmem(f"RZ{tag}", GZ, comps, levels[3].rows, LANES)
            most = max(sizes) - 1
            scratch[f"gs{tag}"] = pltpu.SemaphoreType.DMA((3, most))
            scratch[f"gr{tag}"] = pltpu.SemaphoreType.DMA((3, most))
        scratch["send"] = pltpu.SemaphoreType.DMA((len(MESSAGES),))
        scratch["recv"] = pltpu.SemaphoreType.DMA((2, len(MESSAGES)))
        scratch["ksend"] = pltpu.SemaphoreType.DMA((2, len(FACES)))
        scratch["krecv"] = pltpu.SemaphoreType.DMA((2, len(FACES)))
        names = ["conduct", "cross", "tissue", "src_z", "src_y", "src_x", "out"] + list(scratch)
        row = lambda value: value.reshape(1, sources)
        return pl.pallas_call(
            functools.partial(kernel, names, levels, sizes, sources),
            out_shape=jax.ShapeDtypeStruct((nz, ny, nx), F32),
            in_specs=[pl.BlockSpec(memory_space=pltpu.VMEM)] * 6,
            out_specs=pl.BlockSpec(memory_space=pltpu.VMEM),
            scratch_shapes=list(scratch.values()),
            compiler_params=pltpu.CompilerParams(
                collective_id=0, has_side_effects=True, vmem_limit_bytes=60 * 1024 * 1024
            ),
        )(conduct, cross, tissue, row(src_z), row(src_y), row(src_x))

    placed = (P(None, "gz", "gy", "gx"), P(None, "gz", "gy", "gx"), P("gz", "gy", "gx"), P(), P(), P())
    return jax.shard_map(body, mesh=mesh, in_specs=placed, out_specs=P("gz", "gy", "gx"), check_vma=False)
```

```python
import functools

import jax
import jax.numpy as jnp
from jax import lax
from jax.experimental import pallas as pl
from jax.experimental.pallas import tpu as pltpu
from jax.sharding import PartitionSpec as P

tau_step = 4000.0
relax = 0.55
stim_height = 64000.0
COARSE = 12
RO = 8
LANES = 128
MESH = pl.DeviceIdType.MESH
F32 = jnp.float32
PAIRS = ((0, 1, 3), (0, 2, 4), (1, 2, 5))


class Level:
    def __init__(self, index, nz, ny, nx, split, margin=None):
        self.index, self.nz, self.ny, self.nx, self.split, self.margin = index, nz, ny, nx, split, margin
        self.rows = max(8, -(-ny // 8) * 8)
        self.zrows = max(8, -(-nz // 8) * 8)
        self.stride = RO + self.rows + 8
        self.tau = tau_step / 4.0**index
        self.right = nx % LANES


def lanes_of(shape):
    return lax.broadcasted_iota(jnp.int32, shape, len(shape) - 1)


def rows_of(shape):
    return lax.broadcasted_iota(jnp.int32, shape, len(shape) - 2)


def roll(value, shift, axis=None):
    axis = value.ndim - 1 if axis is None else axis
    if isinstance(shift, int):
        shift = shift % value.shape[axis]
        if shift == 0:
            return value
    return pltpu.roll(value, shift, axis)


def dot(a, b):
    return lax.dot_general(
        a, b, (((1,), (0,)), ((), ())), precision=lax.Precision.HIGHEST, preferred_element_type=F32
    )


MESSAGES = [("z", 1, (0, 0, -1)), ("z", 0, (0, 0, 1))]
for _face, _oy in ((0, -1), (1, 1)):
    for _part, _oz in ((0, 0), (1, -1), (2, 1)):
        MESSAGES.append(("y", 3 * _face + _part, (0, _oy, _oz)))
for _side, _ox in ((0, -1), (1, 1)):
    for _part, (_oy, _oz) in enumerate(((0, 0), (-1, 0), (1, 0), (0, -1), (0, 1))):
        MESSAGES.append(("p", 5 * _side + _part, (_ox, _oy, _oz)))
AROUND = [(dx, dy, dz) for dz in (-1, 0, 1) for dy in (-1, 0, 1) for dx in (-1, 0, 1) if (dx, dy, dz) != (0, 0, 0)]
AROUND.sort(key=lambda offset: -sum(map(abs, offset)))
MESSAGES.sort(key=lambda message: -sum(map(abs, message[2])))
FACES = [("z", 1, (0, 0, -1)), ("z", 0, (0, 0, 1)), ("y", 0, (0, -1, 0)), ("y", 1, (0, 1, 0)), ("p", 0, (-1, 0, 0)), ("p", 1, (1, 0, 0))]


def kernel(names, levels, sizes, sources, *refs):
    R = dict(zip(names, refs))
    GX, GY, GZ = sizes
    gx, gy, gz = lax.axis_index("gx"), lax.axis_index("gy"), lax.axis_index("gz")

    def device(ox, oy, oz):
        return (lax.rem(gx + (ox + GX), GX), lax.rem(gy + (oy + GY), GY), lax.rem(gz + (oz + GZ), GZ))

    peers = list(AROUND)
    peers += [(k, 0, 0) for k in range(1, GX)] + [(0, k, 0) for k in range(1, GY)] + [(0, 0, k) for k in range(1, GZ)]
    seen, unique = set(), []
    for ox, oy, oz in peers:
        key = (ox % GX, oy % GY, oz % GZ)
        if key not in seen:
            seen.add(key)
            unique.append(key)
    barrier = pltpu.get_barrier_semaphore()
    for ox, oy, oz in unique:
        pl.semaphore_signal(barrier, inc=1, device_id=device(ox, oy, oz), device_id_type=MESH)

    def flag(condition):
        return jnp.where(condition, 0.0, 1.0).astype(F32)

    in_xp, in_xm = flag(gx == GX - 1), flag(gx == 0)
    in_yp, in_ym = flag(gy == GY - 1), flag(gy == 0)
    in_zp, in_zm = flag(gz == GZ - 1), flag(gz == 0)

    def clean(level, value):
        return value if level.ny == level.rows else jnp.where(rows_of(value.shape) < level.ny, value, 0.0)

    def bounds(level):
        if level.split:
            return in_zp, in_zm, in_yp, in_ym, in_xp, in_xm
        return (jnp.zeros((), F32),) * 6

    def inside(level, z):
        mz, my, mx = level.margin
        shape = (level.rows, LANES)
        lane, row = lanes_of(shape), rows_of(shape)
        mask_z = jnp.where(z < mz, in_zm, jnp.where(z >= level.nz - mz, in_zp, 1.0))
        mask_y = jnp.where(row < my, in_ym, jnp.where(row >= level.ny - my, in_yp, 1.0))
        mask_x = jnp.where(lane < mx, in_xm, jnp.where(lane >= level.nx - mx, in_xp, 1.0))
        return jnp.where((row < level.ny) & (lane < level.nx), mask_z * mask_y * mask_x, 0.0)

    def valid(dx, dy, dz):
        factor = None
        for d, plus, minus in ((dx, in_xp, in_xm), (dy, in_yp, in_ym), (dz, in_zp, in_zm)):
            if d:
                one = plus if d > 0 else minus
                factor = one if factor is None else factor * one
        return factor

    def times(value, factor):
        return value if factor is None else value * factor

    def pack_x(level, get):
        shape = (level.rows, LANES)
        lane = lanes_of(shape)
        out = jnp.zeros(shape, F32)
        for z in range(level.nz):
            value = get(z)
            first = (level.right + 2 * (z + 1)) % LANES
            last = (2 * (z + 1) + LANES - 1) % LANES
            a = roll(value, first)
            b = roll(value, last - (level.nx - 1))
            out = jnp.where(lane == first, a, jnp.where(lane == last, b, out))
        return out

    def coarsen_rows(level, lower, get, count):
        stage = R["stage"]
        half = level.ny // 2
        for i in range(count):
            for z in range(level.nz // 2):
                total = None
                for dz in range(2):
                    for dy in range(2):
                        piece = get(i, 2 * z + dz, dy, half)
                        total = piece if total is None else total + piece
                stage[pl.ds((i * (level.nz // 2) + z) * lower.rows, half), :] = total

    def coarsen_lanes(level, rows, first=0):
        a, b = rows_of((LANES, LANES)), lanes_of((LANES, LANES))
        matrix = jnp.where((b == (a - first) // 2) & (a >= first) & (b < level.nx // 2), 0.125, 0.0).astype(F32)
        return dot(R["stage"][pl.ds(0, rows), :], matrix)

    def coefficients(level):
        l = level.index
        K, C, D = R[f"K{l}"], R[f"C{l}"], R[f"D{l}"]
        n, rows = level.nz, level.rows
        shape = (rows, LANES)
        lane, row = lanes_of(shape), rows_of(shape)
        zp, zm, yp, ym, xp, xm = bounds(level)
        keep_yp = jnp.where(row == level.ny - 1, yp, 1.0)
        keep_ym = jnp.where(row == 0, ym, 1.0)
        keep_xp = jnp.where(lane == level.nx - 1, xp, 1.0)
        keep_xm = jnp.where(lane == 0, xm, 1.0)

        def step(z, carry):
            ze = z + 1

            def at(comp, dz=0, dy=0):
                return K[comp, ze + dz, pl.ds(RO + dy, rows), :]

            def along(comp, which, sign):
                value = at(comp)
                if level.split:
                    halo = R[f"KH{l}"][which, z]
                    value = jnp.where(lane == (level.right if sign > 0 else LANES - 1), halo, value)
                return roll(value, LANES - 1 if sign > 0 else 1)

            keep_zp = jnp.where(z == n - 1, zp, 1.0)
            keep_zm = jnp.where(z == 0, zm, 1.0)
            keep = ((keep_zp, keep_zm), (keep_yp, keep_ym), (keep_xp, keep_xm))
            weights = (
                (0.5 * (at(0) + at(0, 1)), 0.5 * (at(0) + at(0, -1))),
                (0.5 * (at(1) + at(1, 0, 1)), 0.5 * (at(1) + at(1, 0, -1))),
                (0.5 * (at(2) + along(2, 0, 1)), 0.5 * (at(2) + along(2, 0, -1))),
            )
            total = weights[0][0] + weights[0][1] + weights[1][0] + weights[1][1] + weights[2][0] + weights[2][1]
            diagonal = 1.0 + level.tau * total
            inverse = relax / diagonal
            scale = level.tau * inverse
            if level.margin:
                scale = scale * inside(level, z)
            D[0, z] = inverse
            D[1, z] = diagonal * (1.0 / relax)
            for a in range(3):
                for s in range(2):
                    C[2 * a + s, z] = scale * weights[a][s] * keep[a][s]
            quarter = 0.25 * scale

            def shifted(comp, axis, sign):
                if axis == 0:
                    return at(comp, sign)
                if axis == 1:
                    return at(comp, 0, sign)
                return along(comp, 1 if comp == 4 else 2, sign)

            for number, (a, b, comp) in enumerate(PAIRS):
                ka = [shifted(comp, a, 1), shifted(comp, a, -1)]
                kb = [shifted(comp, b, 1), shifted(comp, b, -1)]
                for sa in range(2):
                    for sb in range(2):
                        value = quarter * (ka[sa] + kb[sb]) * keep[a][sa] * keep[b][sb]
                        C[6 + 4 * number + 2 * sa + sb, z] = value if sa == sb else -value
            return carry

        lax.fori_loop(0, n, step, 0, unroll=min(n, 4))

    def sweep(level, source, emit, halo=True, first=0, last=None):
        l = level.index
        V, C, G, XP, XM = R[f"V{l}"], R[f"C{l}"], R[f"G{l}"], R[f"XP{l}"], R[f"XM{l}"]
        rows = level.rows

        def shift(ze, carry):
            value = V[source, ze]
            up = down = value
            if halo:
                lane = lanes_of(value.shape)
                edge = R[f"H{l}"][source, ze]
                up = jnp.where(lane == level.right, edge, value)
                down = jnp.where(lane == LANES - 1, edge, value)
            XP[ze] = roll(up, LANES - 1)
            XM[ze] = roll(down, 1)
            return carry

        last = level.nz if last is None else last
        lax.fori_loop(first, last + 2, shift, 0, unroll=last + 2 - first)

        def step(z, carry):
            ze = z + 1

            def at(dz, dy, dx):
                where_rows = pl.ds(RO + dy, rows)
                if dx == 0:
                    return V[source, ze + dz, where_rows, :]
                return (XP if dx > 0 else XM)[ze + dz, where_rows, :]

            center = at(0, 0, 0)
            parts = [G[z] - relax * center, None, None]
            offsets = [(1, 0, 0), (-1, 0, 0), (0, 1, 0), (0, -1, 0), (0, 0, 1), (0, 0, -1)]
            for a, b, _ in PAIRS:
                for sa in (1, -1):
                    for sb in (1, -1):
                        offset = [0, 0, 0]
                        offset[a], offset[b] = sa, sb
                        offsets.append(tuple(offset))
            for number, offset in enumerate(offsets):
                term = C[number, z] * at(*offset)
                slot = number % 3
                parts[slot] = term if parts[slot] is None else parts[slot] + term
            emit(z, center, (parts[0] + parts[1]) + parts[2])
            return carry

        lax.fori_loop(first, last, step, 0, unroll=min(last - first, 8))

    def into(level, slot):
        V = R[f"V{level.index}"]

        def emit(z, value, delta):
            V[slot, z + 1, pl.ds(RO, level.rows), :] = value + delta

        return emit

    pending = []
    count = [0]

    def drain():
        for copy in pending:
            copy.wait_send()
        pending.clear()

    def exchange(level, slot, step, during=None):
        l = level.index
        V, H, YB, PB, X = R[f"V{l}"], R[f"H{l}"], R[f"YB{l}"], R[f"PB{l}"], R["PX"]
        ZB = R[f"ZB{l}"]
        RZ, RY, RP = R[f"RZ{l}"], R[f"RY{l}"], R[f"RP{l}"]
        nz, ny, rows, zrows = level.nz, level.ny, level.rows, level.zrows
        drain()
        for z in range(nz):
            YB[0, pl.ds(z, 1), :] = V[slot, z + 1, pl.ds(RO, 1), :]
            YB[1, pl.ds(z, 1), :] = V[slot, z + 1, pl.ds(RO + ny - 1, 1), :]
        ZB[0] = V[slot, 1, pl.ds(RO, rows), :]
        ZB[1] = V[slot, nz, pl.ds(RO, rows), :]
        PB[...] = pack_x(level, lambda z: V[slot, z + 1, pl.ds(RO, rows), :])
        parity = count[0] % 2
        count[0] += 1
        copies = []
        ylow, zlow = rows - 8, zrows - 8
        for number, (kind, where, (ox, oy, oz)) in enumerate(MESSAGES):
            if kind == "z":
                src, dst = ZB.at[0 if where else 1], RZ.at[step, where]
            elif kind == "y":
                face = where // 3
                if where % 3 == 0:
                    src, dst = YB.at[face], RY.at[step, where]
                else:
                    low = 0 if where % 3 == 1 else zlow
                    src, dst = YB.at[face, pl.ds(low, 8)], RY.at[step, where, pl.ds(0, 8)]
            else:
                part = where % 5
                if part in (1, 2):
                    low = 0 if part == 1 else ylow
                    src, dst = PB.at[pl.ds(low, 8)], RP.at[step, where, pl.ds(0, 8)]
                else:
                    src, dst = PB, RP.at[step, where]
            copy = pltpu.make_async_remote_copy(
                src_ref=src, dst_ref=dst, send_sem=R["send"].at[number], recv_sem=R["recv"].at[parity, number],
                device_id=device(ox, oy, oz), device_id_type=MESH,
            )
            copy.start()
            copies.append(copy)
        pending.extend(copies)
        if during is not None:
            during()
        for copy in copies:
            copy.wait_recv()
        V[slot, nz + 1, pl.ds(RO, rows), :] = RZ[step, 1]
        V[slot, 0, pl.ds(RO, rows), :] = RZ[step, 0]
        for face in range(2):
            place = RO + ny if face == 0 else RO - 1
            for z in range(nz):
                V[slot, z + 1, pl.ds(place, 1), :] = RY[step, 3 * face, pl.ds(z, 1), :]
            V[slot, nz + 1, pl.ds(place, 1), :] = RY[step, 3 * face + 1, pl.ds(0, 1), :]
            V[slot, 0, pl.ds(place, 1), :] = RY[step, 3 * face + 2, pl.ds(nz - 1 - zlow, 1), :]

        def merged(part, size):
            even = lanes_of((size, LANES)) % 2 == 0
            return jnp.where(even, RP[step, part, pl.ds(0, size), :], RP[step, 5 + part, pl.ds(0, size), :])

        lane = lanes_of((rows, LANES))
        middle = merged(0, rows)
        above = roll(merged(3, rows), 2 * nz)
        below = roll(merged(4, rows), -2 * nz)

        def slab_lanes(ze):
            return (lane == (level.right + 2 * ze) % LANES) | (lane == (2 * ze + LANES - 1) % LANES)

        middle = jnp.where(slab_lanes(nz + 1), above, jnp.where(slab_lanes(0), below, middle))
        size = level.stride
        X[pl.ds(RO, rows), :] = middle
        X[pl.ds(RO + ny, 1), :] = merged(1, 8)[0:1]
        X[pl.ds(RO - 1, 1), :] = merged(2, 8)[ny - 1 - ylow : ny - ylow]
        whole = X[pl.ds(0, size), :]
        for ze in range(nz + 2):
            H[slot, ze] = roll(whole, -2 * ze)

    def start_faces(level):
        l = level.index
        K, KY, KP, KZ = R[f"K{l}"], R[f"KY{l}"], R[f"KP{l}"], R[f"KZ{l}"]
        nz, ny, rows = level.nz, level.ny, level.rows
        for i, comp in enumerate((0, 3, 4)):
            KZ[0, i] = K[comp, 1, pl.ds(RO, rows), :]
            KZ[1, i] = K[comp, nz, pl.ds(RO, rows), :]
        for i, comp in enumerate((1, 3, 5)):
            for z in range(nz):
                KY[0, i, pl.ds(z, 1), :] = K[comp, z + 1, pl.ds(RO, 1), :]
                KY[1, i, pl.ds(z, 1), :] = K[comp, z + 1, pl.ds(RO + ny - 1, 1), :]
        for i, comp in enumerate((2, 4, 5)):
            KP[i] = pack_x(level, lambda z: K[comp, z + 1, pl.ds(RO, rows), :])
        copies = []
        for number, (kind, where, (ox, oy, oz)) in enumerate(FACES):
            if kind == "z":
                src, dst = KZ.at[0 if where else 1], R[f"RKZ{l}"].at[where]
            elif kind == "y":
                src, dst = KY.at[where], R[f"RKY{l}"].at[where]
            else:
                src, dst = KP, R[f"RKP{l}"].at[where]
            copy = pltpu.make_async_remote_copy(
                src_ref=src, dst_ref=dst, send_sem=R["ksend"].at[l, number], recv_sem=R["krecv"].at[l, number],
                device_id=device(ox, oy, oz), device_id_type=MESH,
            )
            copy.start()
            copies.append(copy)
        return copies

    def finish_faces(level, copies):
        l = level.index
        K, KH = R[f"K{l}"], R[f"KH{l}"]
        nz, ny, rows = level.nz, level.ny, level.rows
        for copy in copies:
            copy.wait()
        for i, comp in enumerate((0, 3, 4)):
            K[comp, nz + 1, pl.ds(RO, rows), :] = R[f"RKZ{l}"][1, i] * in_zp
            K[comp, 0, pl.ds(RO, rows), :] = R[f"RKZ{l}"][0, i] * in_zm
        for i, comp in enumerate((1, 3, 5)):
            for z in range(nz):
                K[comp, z + 1, pl.ds(RO + ny, 1), :] = R[f"RKY{l}"][0, i, pl.ds(z, 1), :] * in_yp
                K[comp, z + 1, pl.ds(RO - 1, 1), :] = R[f"RKY{l}"][1, i, pl.ds(z, 1), :] * in_ym
        even = lanes_of((rows, LANES)) % 2 == 0
        for i in range(3):
            both = jnp.where(even, R[f"RKP{l}"][0, i] * in_xp, R[f"RKP{l}"][1, i] * in_xm)
            for z in range(nz):
                KH[i, z] = roll(both, -2 * (z + 1))

    def start_around(tag):
        tag_index = "kfp".index(tag)
        copies = []
        for number, (dx, dy, dz) in enumerate(AROUND):
            copy = pltpu.make_async_remote_copy(
                src_ref=R[f"TA{tag}"], dst_ref=R[f"RA{tag}"].at[number], send_sem=R["asend"].at[tag_index, number],
                recv_sem=R["arecv"].at[tag_index, number], device_id=device(-dx, -dy, -dz), device_id_type=MESH,
            )
            copy.start()
            copies.append(copy)
        return copies

    def finish_around(tag, copies, comps, store):
        for copy in copies:
            copy.wait()
        tile = R[f"TA{tag}"]
        lane = lanes_of(tile.shape)
        for dz in (-1, 0, 1):
            for dy in (-1, 0, 1):
                row_tiles = []
                for dx in (-1, 0, 1):
                    if (dx, dy, dz) == (0, 0, 0):
                        row_tiles.append(tile[...])
                        continue
                    value = R[f"RA{tag}"][AROUND.index((dx, dy, dz))]
                    row_tiles.append(times(value, valid(dx, dy, dz)))
                for z in range(4):
                    low, mid, high = (roll(row_tiles[i], 32 * i - 32 * z) for i in range(3))
                    value = jnp.where(lane < 32, low, jnp.where(lane < 64, mid, jnp.where(lane < 96, high, 0.0)))
                    for comp in range(comps):
                        store(comp, 4 * (dz + 1) + z, 4 * (dy + 1), value[4 * comp : 4 * comp + 4])

    def start_wide(tag, comps, get):
        tag_index = "kfp".index(tag)
        A, B, S, S2 = (R[f"{name}{tag}"] for name in ("WA", "WB", "WS", "WT"))
        shape = (8, LANES)
        lane = lanes_of(shape)
        for c in range(comps):
            slabs = [get(c, z) for z in range(8)]
            strip = jnp.zeros(shape, F32)
            for z in range(8):
                low, high = 68 + 8 * z, 8 * z
                strip = jnp.where((lane >= low) & (lane < low + 4), roll(slabs[z], low), strip)
                strip = jnp.where((lane >= high) & (lane < high + 4), roll(slabs[z], high - 60), strip)
            S[c] = strip
            for h in range(2):
                S2[h, c // 2, pl.ds(4 * (c % 2), 4), :] = strip[4 * h : 4 * h + 4]
            for p in range(4):
                pair = slabs[2 * p] + roll(slabs[2 * p + 1], 64)
                A[p, c] = pair
                for h in range(2):
                    B[h, p // 2, c, pl.ds(4 * (p % 2), 4), :] = pair[4 * h : 4 * h + 4]
        copies = []
        for number, (dx, dy, dz) in enumerate(AROUND):
            t, h = int(dz < 0), int(dy < 0)
            iz, iy, ix = int(dz > 0), int(dy > 0), int(dx > 0)
            if dx == 0 and dy == 0:
                src, dst = A.at[pl.ds(2 * t, 2)], R[f"WRA{tag}"].at[iz]
            elif dx == 0 and dz == 0:
                src, dst = B.at[h], R[f"WRB{tag}"].at[iy]
            elif dx == 0:
                src, dst = B.at[h, t], R[f"WRC{tag}"].at[2 * iy + iz]
            elif dy == 0:
                src, dst = S, R[f"WRS{tag}"].at[3 * ix + dz + 1]
            else:
                src, dst = S2.at[h], R[f"WRT{tag}"].at[3 * (2 * ix + iy) + dz + 1]
            copy = pltpu.make_async_remote_copy(
                src_ref=src, dst_ref=dst, send_sem=R["wsend"].at[tag_index, number],
                recv_sem=R["wrecv"].at[tag_index, number], device_id=device(-dx, -dy, -dz), device_id_type=MESH,
            )
            copy.start()
            copies.append(copy)
        return copies

    def finish_wide(tag, copies, comps, load, store):
        for copy in copies:
            copy.wait()
        A = R[f"WA{tag}"]
        MS = R["strips"]
        lane8, lane16 = lanes_of((8, LANES)), lanes_of((16, LANES))
        edge = (lane16 < 4) | ((lane16 >= 68) & (lane16 < 72))
        for c in range(comps):
            for dz in (-1, 0, 1):
                iz = int(dz > 0)
                zs = range(4, 8) if dz < 0 else range(0, 8) if dz == 0 else range(0, 4)
                base = {-1: -4, 0: 4, 1: 12}[dz]
                for z in zs:
                    tile = A[z // 2, c] if dz == 0 else R[f"WRA{tag}"][iz, z // 2 - (2 if dz < 0 else 0), c]
                    store(c, z + base, 4, roll(times(tile, valid(0, 0, dz)), 4 - 64 * (z % 2)))
                for dy in (-1, 1):
                    iy = int(dy > 0)
                    for z in zs:
                        tile = R[f"WRB{tag}"][iy, z // 4, c] if dz == 0 else R[f"WRC{tag}"][2 * iy + iz, c]
                        part = 4 * ((z % 4) // 2)
                        piece = roll(times(tile, valid(0, dy, dz)), 4 - 64 * (z % 2))
                        store(c, z + base, 0 if dy < 0 else 12, piece[part : part + 4])
                for dy in (-1, 0, 1):
                    iy = int(dy > 0)
                    sides = []
                    for ix, dx in enumerate((-1, 1)):
                        if dy == 0:
                            tile = R[f"WRS{tag}"][3 * ix + dz + 1, c]
                        else:
                            tile = R[f"WRT{tag}"][3 * (2 * ix + iy) + dz + 1, c // 2]
                        sides.append(times(tile, valid(dx, dy, dz)))
                    both = jnp.where(lane8 < 64, sides[0], sides[1])
                    if dy == 0:
                        MS[dz + 1, pl.ds(4, 8), :] = both
                    else:
                        MS[dz + 1, pl.ds(0 if dy < 0 else 12, 4), :] = both[4 * (c % 2) : 4 * (c % 2) + 4]
                strip = MS[dz + 1]
                for z in zs:
                    store(c, z + base, 0, jnp.where(edge, roll(strip, -8 * z), load(c, z + base)))

    class Gather:
        def __init__(self, tag, comps):
            self.tag, self.comps = tag, comps
            self.copies = []

        def send(self, phase, src, dst_of, targets):
            self.copies = []
            for number, offset in enumerate(targets):
                copy = pltpu.make_async_remote_copy(
                    src_ref=src, dst_ref=dst_of(number), send_sem=R[f"gs{self.tag}"].at[phase, number],
                    recv_sem=R[f"gr{self.tag}"].at[phase, number], device_id=device(*offset), device_id_type=MESH,
                )
                copy.start()
                self.copies.append(copy)

        def wait(self):
            for copy in self.copies:
                copy.wait()

        def phase_x(self, tiles):
            own, received = R[f"GX{self.tag}"], R[f"RX{self.tag}"]
            own[...] = tiles
            self.send(0, own, lambda number: received.at[number], [(k, 0, 0) for k in range(1, GX)])

        def phase_y(self):
            self.wait()
            slots = R[f"RY{self.tag}"]
            total = R[f"GX{self.tag}"][...]
            for k in range(GX - 1):
                total = total + R[f"RX{self.tag}"][k]
            slots[gy] = total
            self.send(1, slots.at[gy], lambda number: slots.at[gy], [(0, k, 0) for k in range(1, GY)])

        def phase_z(self):
            self.wait()
            slots, out = R[f"RY{self.tag}"], R[f"RZ{self.tag}"]
            for i in range(self.comps):
                for y in range(GY):
                    out[gz, i, pl.ds(2 * y, 2), :] = slots[y, pl.ds(2 * i, 2), :]
            self.send(2, out.at[gz], lambda number: out.at[gz], [(0, 0, k) for k in range(1, GZ)])

        def finish(self, store):
            self.wait()
            out = R[f"RZ{self.tag}"]
            for i in range(self.comps):
                for z in range(GZ):
                    value = out[z, i]
                    left = lanes_of(value.shape) < 64
                    store(i, 2 * z, jnp.where(left, value, 0.0))
                    store(i, 2 * z + 1, jnp.where(left, roll(value, 64), 0.0))

    def own_tile(values, comps, total_rows):
        T = R["tile"]
        T[...] = jnp.zeros(T.shape, F32)
        for i in range(comps):
            low = values[(2 * i) * 8 : (2 * i) * 8 + 8]
            high = values[(2 * i + 1) * 8 : (2 * i + 1) * 8 + 8]
            T[pl.ds(2 * i, 2), :] = (low + roll(high, 64))[0:2]
        return roll(T[pl.ds(0, total_rows), :], 16 * gx)

    L0, L1, L2, L3, L4 = levels
    block1, block2, block3 = Level(1, 8, 8, 64, True), Level(2, 4, 4, 32, True), Level(3, 2, 2, 16, False)

    def fill(z, carry):
        weight = R["tissue"][z].astype(F32)
        for comp in range(3):
            R["K0"][comp, z + 1, pl.ds(RO, L0.rows), :] = R["conduct"][comp, z] * weight
            R["K0"][3 + comp, z + 1, pl.ds(RO, L0.rows), :] = R["cross"][comp, z] * weight
        return carry

    lax.fori_loop(0, L0.nz, fill, 0, unroll=4)
    pl.semaphore_wait(barrier, len(unique))
    faces0 = start_faces(L0)

    R["stage"][...] = jnp.zeros(R["stage"].shape, F32)

    def tensor_rows(l, offset):
        return lambda i, z, dy, n: R[f"K{l}"][i, z + 1, pl.ds(offset + dy, n, stride=2), :]

    coarsen_rows(L0, block1, tensor_rows(0, RO), 6)
    values = coarsen_lanes(L0, 6 * 8 * 8)

    def slab_of(values):
        return lambda c, z: values[(c * 8 + z) * 8 : (c * 8 + z) * 8 + 8]

    wide_k = start_wide("k", 6, slab_of(values))
    for i in range(6):
        for z in range(8):
            R["KB1"][i, z] = values[(i * 8 + z) * 8 : (i * 8 + z) * 8 + 8]
    coarsen_rows(block1, block2, lambda i, z, dy, n: R["KB1"][i, z, pl.ds(dy, n, stride=2), :], 6)
    values = coarsen_lanes(block1, 6 * 4 * 8)

    def block2_tile(ref, comps, values):
        for i in range(comps):
            total = None
            for z in range(4):
                start = (i * 4 + z) * 8
                piece = roll(values[start : start + 8], 32 * z)
                total = piece if total is None else total + piece
            ref[pl.ds(4 * i, 4), :] = total[0:4]

    R["TAf"][...] = jnp.zeros(R["TAf"].shape, F32)
    R["TAp"][...] = jnp.zeros(R["TAp"].shape, F32)
    block2_tile(R["TAk"], 6, values)
    around_k = start_around("k")
    for i in range(6):
        for z in range(4):
            start = (i * 4 + z) * 8
            R["KB2"][i, z] = values[start : start + 8]
    coarsen_rows(block2, block3, lambda i, z, dy, n: R["KB2"][i, z, pl.ds(dy, n, stride=2), :], 6)
    gather_k = Gather("k", 6)
    gather_k.phase_x(own_tile(coarsen_lanes(block2, 6 * 2 * 8), 6, 16))

    for level in (L1, L2, L3, L4):
        for name in ("K", "V"):
            ref = R[f"{name}{level.index}"]
            for i in range(ref.shape[0]):
                ref[i] = jnp.zeros(ref.shape[1:], F32)
    R["load"][...] = jnp.zeros(R["load"].shape, F32)

    zl = R["src_z"][...] - gz * L0.nz
    yl = R["src_y"][...] - gy * L0.ny
    xl = R["src_x"][...] - gx * L0.nx
    here = (zl >= 0) & (zl < L0.nz) & (yl >= 0) & (yl < L0.ny)
    R["key"][0:1, :] = jnp.where(here, zl * L0.ny + yl, -1)
    R["key"][1:2, :] = xl
    R["counts"][...] = jnp.zeros(R["counts"].shape, F32)
    chunk = 256

    def scatter(i, carry):
        start = pl.multiple_of(i * chunk, chunk)
        key = R["key"][0:1, pl.ds(start, chunk)]
        key_x = R["key"][1:2, pl.ds(start, chunk)]
        left = jnp.where(rows_of((L0.nz * L0.ny, chunk)) == key, 1.0, 0.0).astype(jnp.bfloat16)
        right = jnp.where(rows_of((LANES, chunk)) == key_x, 1.0, 0.0).astype(jnp.bfloat16)
        R["counts"][...] += lax.dot_general(left, right, (((1,), (1,)), ((), ())), preferred_element_type=F32)
        return carry

    lax.fori_loop(0, sources // chunk, scatter, 0, unroll=2)

    finish_faces(L0, faces0)
    coefficients(L0)

    def load0(z):
        return stim_height * R["counts"][pl.ds(pl.multiple_of(z * L0.ny, 8), L0.rows), :]

    def first_sweep(level, load):
        l = level.index

        def step(z, carry):
            value = load(z) * R[f"D{l}"][0, z]
            R[f"G{l}"][z] = value
            R[f"V{l}"][0, z + 1, pl.ds(RO, level.rows), :] = value
            return carry

        lax.fori_loop(0, level.nz, step, 0, unroll=min(level.nz, 8))

    def residual(level, slot, halo=True, first=0, last=None):
        l = level.index
        store = R[f"XR{l}"]

        def emit(z, value, delta):
            store[z, pl.ds(RO, level.rows), :] = delta * R[f"D{l}"][1, z]

        sweep(level, slot, emit, halo, first, last)

    def restricted(level, lower, z0=0, y0=0, x0=0):
        def get(i, z, dy, n):
            return R[f"XR{level.index}"][z + z0, pl.ds(RO + y0 + dy, n, stride=2), :]

        coarsen_rows(level, lower, get, 1)
        return coarsen_lanes(level, (level.nz // 2) * lower.rows, x0)

    def tensor_region(l):
        def store(i, z, row, value):
            R[f"K{l}"][i, z + 1, pl.ds(RO + row, value.shape[0]), :] = value

        return store

    def iterate_region(l):
        def store(i, z, row, value):
            R[f"V{l}"][2, z + 1, pl.ds(RO + row, value.shape[0]), :] = value

        return store

    def load_region(level):
        def store(i, z, row, value):
            R["load"][pl.ds(z * level.rows + row, value.shape[0]), :] = value

        return store

    def during_01():
        gather_k.phase_y()

    def during_02():
        gather_k.phase_z()
        finish_wide("k", wide_k, 6, lambda i, z: R["K1"][i, z + 1, pl.ds(RO, 16), :], tensor_region(1))
        coefficients(L1)

    def during_10():
        finish_around("k", around_k, 6, tensor_region(2))
        coefficients(L2)

    def coarse_setup():
        def store(i, z, value):
            R["K3"][i, z + 1, pl.ds(RO, L3.rows), :] = clean(L3, value)

        gather_k.finish(store)
        coefficients(L3)
        coarsen_rows(L3, L4, tensor_rows(3, RO), 6)
        height = L4.nz * L4.rows
        values = coarsen_lanes(L3, 6 * height)
        for i in range(6):
            for z in range(L4.nz):
                start = i * height + z * L4.rows
                R["K4"][i, z + 1, pl.ds(RO, L4.rows), :] = clean(L4, values[start : start + L4.rows])
        coefficients(L4)

    def load_of(level):
        return lambda z: clean(level, R["load"][pl.ds(pl.multiple_of(z * level.rows, 8), level.rows), :])

    first_sweep(L0, load0)
    exchange(L0, 0, 0, during_01)
    sweep(L0, 0, into(L0, 1))
    exchange(L0, 1, 1, during_02)
    residual(L0, 1)
    values = restricted(L0, block1)

    wide_f = start_wide("f", 1, slab_of(values))
    during_10()
    finish_wide("f", wide_f, 1, lambda i, z: R["load"][pl.ds(16 * z, 16), :], load_region(L1))
    first_sweep(L1, load_of(L1))
    sweep(L1, 0, into(L1, 1), False, 3, 13)
    residual(L1, 1, False, 4, 12)
    values = restricted(block1, block2, 4, 4, 4)

    block2_tile(R["TAf"], 1, values)
    around_f = start_around("f")
    coarse_setup()
    R["load"][...] = jnp.zeros(R["load"].shape, F32)
    finish_around("f", around_f, 1, load_region(L2))
    first_sweep(L2, load_of(L2))
    sweep(L2, 0, into(L2, 1), False, 3, 9)
    residual(L2, 1, False, 4, 8)
    values = restricted(block2, block3, 4, 4, 32)

    gather_f = Gather("f", 1)
    gather_f.phase_x(own_tile(values, 1, 8))
    gather_f.phase_y()
    gather_f.phase_z()
    tile_lane = lanes_of((8, LANES))
    total = jnp.zeros((8, LANES), F32)
    for z in range(4):
        piece = roll(R["V2"][1, 5 + z, pl.ds(RO + 4, 8), :], 32 * z - 32)
        total = jnp.where((tile_lane >= 32 * z) & (tile_lane < 32 * z + 32), piece, total)
    R["TAp"][0:4, :] = total[0:4]
    around_p = start_around("p")
    lane8 = lanes_of((8, LANES))

    def pre_slab(c, z):
        return jnp.where(lane8 < 64, roll(R["V1"][1, 5 + z, pl.ds(RO + 4, 8), :], -4), 0.0)

    wide_p = start_wide("p", 1, pre_slab)

    def store_load(i, z, value):
        R["load"][pl.ds(z * L3.rows, L3.rows), :] = value

    gather_f.finish(store_load)

    first_sweep(L3, load_of(L3))
    sweep(L3, 0, into(L3, 1), False)
    residual(L3, 1, False)
    values = restricted(L3, L4)
    R["load"][pl.ds(0, L4.nz * L4.rows), :] = values
    first_sweep(L4, load_of(L4))
    for i in range(COARSE - 1):
        sweep(L4, i % 2, into(L4, (i + 1) % 2), False)
    last4 = (COARSE - 1) % 2

    def spread(level, nz_c, ny_c, nx_c, stride_c, get, base, halo):
        l = level.index
        M, PV = R["merge"], R["spread"]
        a, b = rows_of((LANES, LANES)), lanes_of((LANES, LANES))
        main = (a == b // 2) & (b < level.nx)
        edges = ((a == nx_c) & (b == level.right)) | ((a == LANES - 1) & (b == LANES - 1))
        wide = halo and level.nx == LANES
        if halo and not wide:
            main = main | edges
        height = (nz_c + 2) * stride_c
        stacked = jnp.concatenate([get(ze) for ze in range(nz_c + 2)], axis=0)
        M[0, pl.ds(0, height), :] = dot(stacked, jnp.where(main, 1.0, 0.0).astype(F32))
        if wide:
            M[1, pl.ds(0, height), :] = dot(stacked, jnp.where(edges, 1.0, 0.0).astype(F32))
        V = R[f"V{l}"]
        for layer in range(2 if wide else 1):
            for ze in range(nz_c + 2):
                value = M[layer, pl.ds(ze * stride_c + RO - 1, ny_c + 2), :]
                slabs = [zf for zf in (2 * ze - 1, 2 * ze) if 0 <= zf <= level.nz + 1]
                for phase in range(2):
                    PV[layer, ze, pl.ds(RO - 2 + phase, ny_c + 2, stride=2), :] = value
        for ze in range(nz_c + 2):
            for zf in (2 * ze - 1, 2 * ze):
                if 0 <= zf <= level.nz + 1:
                    size = level.stride
                    V[2, zf] = V[1, zf] + PV[0, ze, pl.ds(0, size), :]
                    if halo:
                        H = R[f"H{l}"]
                        H[2, zf] = H[1, zf] + PV[1 if wide else 0, ze, pl.ds(0, size), :]

    def coarse_slab(level, slot):
        V = R[f"V{level.index}"]

        def get(ze):
            value = V[slot, ze]
            if level.split:
                lane = lanes_of(value.shape)
                edge = (lane == level.right) | (lane == LANES - 1)
                value = jnp.where(edge, R[f"H{level.index}"][slot, ze], value)
            return value

        return get

    spread(L3, L4.nz, L4.ny, L4.nx, L4.stride, coarse_slab(L4, last4), 0, False)
    sweep(L3, 2, into(L3, 0), False)
    sweep(L3, 0, into(L3, 1), False)

    def start_region(level, slabs):
        a, b = rows_of((LANES, LANES)), lanes_of((LANES, LANES))
        copied = dot(jnp.concatenate(slabs, axis=0), jnp.where((a == b // 2) & (b < level.nx), 1.0, 0.0).astype(F32))
        V = R[f"V{level.index}"]
        for i in range(len(slabs)):
            for phase in range(2):
                R["spread"][0, i, pl.ds(phase, 8, stride=2), :] = copied[8 * i : 8 * i + 8]
        for z in range(level.nz):
            where_rows = pl.ds(RO, level.rows)
            added = jnp.where(inside(level, z) > 0.5, R["spread"][0, z // 2, pl.ds(0, level.rows), :], 0.0)
            V[2, z + 1, where_rows, :] = V[2, z + 1, where_rows, :] + added

    finish_around("p", around_p, 1, iterate_region(2))
    slabs = []
    count3 = L3.nz + 2
    for i in range(6):
        value = R["V3"][1, lax.rem(2 * gz + (count3 - 1 + i), count3)]
        value = roll(value, lax.rem(2 * L3.stride - RO + 2 - 2 * gy, L3.stride), axis=0)
        value = roll(value, lax.rem(LANES + 16 - 16 * gx, LANES))
        slabs.append(value[0:8])
    start_region(L2, slabs)
    sweep(L2, 2, into(L2, 3), False, 1, 11)
    sweep(L2, 3, into(L2, 0), False, 2, 10)
    finish_wide("p", wide_p, 1, lambda i, z: R["V1"][2, z + 1, pl.ds(RO, 16), :], iterate_region(1))
    start_region(L1, [roll(R["V2"][0, 3 + i, pl.ds(RO + 2, 8), :], -30) for i in range(8)])
    sweep(L1, 2, into(L1, 3), False, 2, 14)
    sweep(L1, 3, into(L1, 0), False, 3, 13)

    def region_slab(ze):
        return roll(R["V1"][0, 4 + ze, pl.ds(4, 24), :], -4)

    spread(L0, 8, 8, 64, 24, region_slab, 0, True)
    sweep(L0, 2, into(L0, 3))
    exchange(L0, 3, 2)

    def emit_out(z, value, delta):
        R["out"][z] = value + delta

    sweep(L0, 3, emit_out)
    drain()


def solution(mesh):
    sizes = (mesh.shape["gx"], mesh.shape["gy"], mesh.shape["gz"])
    GX, GY, GZ = sizes

    def body(conduct, cross, tissue, src_z, src_y, src_x):
        nz, ny, nx = tissue.shape
        sources = src_z.shape[0]
        levels = [Level(0, nz, ny, nx, True)]
        levels.append(Level(1, 16, 16, 72, False, (4, 4, 4)))
        levels.append(Level(2, 12, 12, 96, False, (4, 4, 32)))
        levels.append(Level(3, 2 * GZ, 2 * GY, 16 * GX, False))
        levels.append(Level(4, GZ, GY, 8 * GX, False))
        scratch = {}

        def vmem(name, *shape, dtype=F32):
            scratch[name] = pltpu.VMEM(shape, dtype)

        for level in levels:
            l, z, rows, stride, zrows = level.index, level.nz, level.rows, level.stride, level.zrows
            slots = 4 if l < 3 else 3
            vmem(f"K{l}", 6, z + 2, stride, LANES)
            vmem(f"C{l}", 18, z, rows, LANES)
            vmem(f"D{l}", 2, z, rows, LANES)
            vmem(f"G{l}", z, rows, LANES)
            vmem(f"V{l}", slots, z + 2, stride, LANES)
            vmem(f"XP{l}", z + 2, stride, LANES)
            vmem(f"XM{l}", z + 2, stride, LANES)
            vmem(f"XR{l}", z, stride, LANES)
            if level.split:
                vmem(f"H{l}", slots, z + 2, stride, LANES)
                vmem(f"KH{l}", 3, z, rows, LANES)
                vmem(f"YB{l}", 2, zrows, LANES)
                vmem(f"PB{l}", rows, LANES)
                vmem(f"ZB{l}", 2, rows, LANES)
                vmem(f"RZ{l}", 4, 2, rows, LANES)
                vmem(f"RY{l}", 4, 6, zrows, LANES)
                vmem(f"RP{l}", 4, 10, rows, LANES)
                vmem(f"KZ{l}", 2, 3, rows, LANES)
                vmem(f"KY{l}", 2, 3, zrows, LANES)
                vmem(f"KP{l}", 3, rows, LANES)
                vmem(f"RKZ{l}", 2, 3, rows, LANES)
                vmem(f"RKY{l}", 2, 3, zrows, LANES)
                vmem(f"RKP{l}", 2, 3, rows, LANES)
        for tag, height in (("k", 24), ("f", 8), ("p", 8)):
            vmem(f"TA{tag}", height, LANES)
            vmem(f"RA{tag}", len(AROUND), height, LANES)
        scratch["asend"] = pltpu.SemaphoreType.DMA((3, len(AROUND)))
        scratch["arecv"] = pltpu.SemaphoreType.DMA((3, len(AROUND)))
        for tag, comps in (("k", 6), ("f", 1), ("p", 1)):
            half = (comps + 1) // 2
            vmem(f"WA{tag}", 4, comps, 8, LANES)
            vmem(f"WB{tag}", 2, 2, comps, 8, LANES)
            vmem(f"WS{tag}", comps, 8, LANES)
            vmem(f"WT{tag}", 2, half, 8, LANES)
            vmem(f"WRA{tag}", 2, 2, comps, 8, LANES)
            vmem(f"WRB{tag}", 2, 2, comps, 8, LANES)
            vmem(f"WRC{tag}", 4, comps, 8, LANES)
            vmem(f"WRS{tag}", 6, comps, 8, LANES)
            vmem(f"WRT{tag}", 12, half, 8, LANES)
        scratch["wsend"] = pltpu.SemaphoreType.DMA((3, len(AROUND)))
        scratch["wrecv"] = pltpu.SemaphoreType.DMA((3, len(AROUND)))
        vmem("strips", 3, 16, LANES)
        vmem("KB1", 6, 8, 8, LANES)
        vmem("KB2", 6, 4, 8, LANES)
        vmem("PX", levels[0].stride, LANES)
        vmem("stage", 6 * 8 * 8, LANES)
        vmem("tile", 16, LANES)
        vmem("key", 2, sources, dtype=jnp.int32)
        vmem("counts", nz * ny, LANES)
        vmem("load", max(levels[3].nz * levels[3].rows, 64), LANES)
        vmem("merge", 2, 10 * 32, LANES)
        vmem("spread", 2, 10, 48, LANES)
        for tag, comps, height in (("k", 6, 16), ("f", 1, 8)):
            vmem(f"GX{tag}", height, LANES)
            vmem(f"RX{tag}", GX - 1, height, LANES)
            vmem(f"RY{tag}", GY, height, LANES)
            vmem(f"RZ{tag}", GZ, comps, levels[3].rows, LANES)
            most = max(sizes) - 1
            scratch[f"gs{tag}"] = pltpu.SemaphoreType.DMA((3, most))
            scratch[f"gr{tag}"] = pltpu.SemaphoreType.DMA((3, most))
        scratch["send"] = pltpu.SemaphoreType.DMA((len(MESSAGES),))
        scratch["recv"] = pltpu.SemaphoreType.DMA((2, len(MESSAGES)))
        scratch["ksend"] = pltpu.SemaphoreType.DMA((2, len(FACES)))
        scratch["krecv"] = pltpu.SemaphoreType.DMA((2, len(FACES)))
        names = ["conduct", "cross", "tissue", "src_z", "src_y", "src_x", "out"] + list(scratch)
        row = lambda value: value.reshape(1, sources)
        return pl.pallas_call(
            functools.partial(kernel, names, levels, sizes, sources),
            out_shape=jax.ShapeDtypeStruct((nz, ny, nx), F32),
            in_specs=[pl.BlockSpec(memory_space=pltpu.VMEM)] * 6,
            out_specs=pl.BlockSpec(memory_space=pltpu.VMEM),
            scratch_shapes=list(scratch.values()),
            compiler_params=pltpu.CompilerParams(
                collective_id=0, has_side_effects=True, vmem_limit_bytes=60 * 1024 * 1024
            ),
        )(conduct, cross, tissue, row(src_z), row(src_y), row(src_x))

    placed = (P(None, "gz", "gy", "gx"), P(None, "gz", "gy", "gx"), P("gz", "gy", "gx"), P(), P(), P())
    return jax.shard_map(body, mesh=mesh, in_specs=placed, out_specs=P("gz", "gy", "gx"), check_vma=False)
```
